32 devices in a mesh: ty: 4 (over x, core), tx: 8 (over z, y).
Axes of the slice: x: 2, y: 2, z: 4, core: 2. Of those that a mesh axis runs over, the one named last changes fastest.
Arguments:
- tiles: bfloat16 [4, 8, 4, 512, 512], P('ty', 'tx'), may hold values from -6 to 6
- shifts: int32 [4, 8, 2], P('ty', 'tx'), may hold values from -28 to 28
- piece_target: int32 [4, 8, 256], P('ty', 'tx'), may hold values from 0 to 2047, as said below
- coarse_target: int32 [4, 8, 64], P('ty', 'tx'), may hold values from 0 to 511, as said below
Outputs:
- joined: bfloat16 [2048, 4096], P(('ty', 'tx'))
- coarse: bfloat16 [512, 256], P(('ty', 'tx'))
- corr_right: float32 [48, 1024], P('ty', 'tx')
- corr_below: float32 [48, 1024], P('ty', 'tx')
The draws below stay inside these ranges and needn't reach their ends.
Inputs may be any that keep to these rules, and one draw needn't show every extreme that they name: `piece_target`: each tile sends at most 16 sub-blocks to the sub-blocks of one owner device; in every draw some owner devices receive exactly 16 from every tile. `coarse_target`: owners lie in the same tile row; every device sends exactly 8 pieces to each device of its row, and every target of every device is named exactly once.
All inputs are finite; a program needn't handle non-finite values.
Results may differ from the reference program's by a relative error of at most 0.008.
Values may be sent and summed in bfloat16 or wider, within the bound.
A program may use at most 128 MiB of HBM per device.

```python
import math
import jax
import jax.numpy as jnp
from jax import lax

TS = 512
TILE_SLICES = 4
SUBBLOCK_SIDE = 32
OV = 48
H = 8
DEVICE_SUBBLOCKS = 64
NP = 256
CAP = 16
N_TY = 4
N_TX = 8


def draw_piece_target(key, part):
    count_all = N_TY * N_TX
    order = jax.random.permutation(jax.random.fold_in(key, 11), count_all)
    hottest = order[:count_all // 8]
    others = order[count_all // 8:]

    def per_device(device):
        dev_key = jax.random.fold_in(jax.random.fold_in(key, 12), device)
        mixed = jax.random.permutation(jax.random.fold_in(dev_key, 1), others)
        owners = jnp.concatenate([jnp.repeat(hottest, CAP), jnp.repeat(mixed[:count_all // 4], CAP // 4), jnp.repeat(mixed[count_all // 4:], CAP // 2)])
        owners = jax.random.permutation(jax.random.fold_in(dev_key, 2), owners)
        slot_ids = jax.random.randint(jax.random.fold_in(dev_key, 3), (NP,), 0, DEVICE_SUBBLOCKS)
        return owners * DEVICE_SUBBLOCKS + slot_ids
    drawn = jax.vmap(per_device)(jnp.arange(count_all))
    return drawn.reshape(N_TY, N_TX, NP).astype(jnp.int32)


def draw_coarse_target(key, part):
    per_peer = DEVICE_SUBBLOCKS // N_TX

    def per_row(row):
        row_key = jax.random.fold_in(jax.random.fold_in(key, 21), row)
        offsets = jax.random.permutation(jax.random.fold_in(row_key, 0), N_TX)
        orders = jax.vmap(lambda owner: jax.random.permutation(jax.random.fold_in(row_key, owner + 1), DEVICE_SUBBLOCKS))(jnp.arange(N_TX))
        fine_slot = jnp.arange(DEVICE_SUBBLOCKS)[None, :]
        source = jnp.arange(N_TX)[:, None]
        owner_col = (fine_slot + offsets[:, None]) % N_TX
        within = source * per_peer + fine_slot // N_TX
        chosen = orders[owner_col, within]
        return owner_col * DEVICE_SUBBLOCKS + chosen
    drawn = jax.vmap(per_row)(jnp.arange(N_TY))
    return drawn.reshape(N_TY, N_TX, DEVICE_SUBBLOCKS).astype(jnp.int32)


def plant(result, own_key, least, high):
    longest = result.shape.index(max(result.shape))
    spots = []
    for shift in (0, 1):
        where = [jax.random.randint(jax.random.fold_in(own_key, axis), (), 0, length) for axis, length in enumerate(result.shape)]
        where[longest] = (where[longest] + shift) % result.shape[longest]
        spots.append(tuple(where))
    return result.at[spots[0]].set(least).at[spots[1]].set(high)


def block_scale(rng, shape, shards, smallest, high):
    factor_of = 1.0
    for position, blocks in shards:
        heights = jax.random.uniform(jax.random.fold_in(jax.random.fold_in(rng, 6), position), (blocks,), jnp.float32, smallest / len(shards), high / len(shards))
        factor_of = factor_of * jnp.repeat(jnp.exp(heights), shape[position] // blocks).reshape((-1,) + (1,) * (len(shape) - 1 - position))
    return factor_of


def noise(key, shape, scale, bound, split=(), held_as=jnp.bfloat16):
    level = block_scale(key, shape, split, -0.22, 0.18) if split else 1.0
    entries = jax.random.normal(key, shape, jnp.float32) * scale * level
    return jnp.minimum(jnp.maximum(entries, -bound), bound).astype(held_as)


def setup_inputs(seed: int = 0) -> dict:
    splits = jax.random.split(jax.random.key(seed), 5)
    tiles = noise(splits[0], (N_TY, N_TX, TILE_SLICES, TS, TS), 1.0, 6.0, ((0, 4), (1, 8)))
    shifts = plant(jax.random.randint(splits[1], (N_TY, N_TX, 2), 4 - 4 * H, 4 * H - 3), jax.random.fold_in(splits[1], 1), 4 - 4 * H, (4 * H - 3) - 1).astype(jnp.int32)
    piece_target = draw_piece_target(jax.random.fold_in(splits[4], 71), 0)
    coarse_target = draw_coarse_target(jax.random.fold_in(splits[4], 71), 0)
    return dict(tiles=tiles, shifts=shifts, piece_target=piece_target, coarse_target=coarse_target)


def bin_columns(strips):
    lead = strips.shape[:-3]
    voxel_values = strips.astype(jnp.float32).reshape(lead + (TILE_SLICES, TS // 4, 4, OV // 4, 4))
    summed = lax.optimization_barrier(jnp.sum(voxel_values, axis=(-5, -3, -1)))
    return jnp.swapaxes(summed, -1, -2) * (1.0 / math.sqrt(16.0 * TILE_SLICES))

def bin_rows(strips):
    lead = strips.shape[:-3]
    voxel_values = strips.astype(jnp.float32).reshape(lead + (TILE_SLICES, OV // 4, 4, TS // 4, 4))
    return lax.optimization_barrier(jnp.sum(voxel_values, axis=(-5, -3, -1))) * (1.0 / math.sqrt(16.0 * TILE_SLICES))

def phase_surface(own, other):
    own_spec = jnp.fft.fft2(own, norm='ortho')
    other_spec = jnp.fft.fft2(other, norm='ortho')
    cross = own_spec * jnp.conj(other_spec)
    normed = cross / jnp.sqrt(jnp.real(cross) ** 2 + jnp.imag(cross) ** 2 + 1.0)
    return jnp.real(jnp.fft.ifft2(normed, norm='ortho')).astype(jnp.float32)

def layout(surfaces):
    return surfaces.transpose(0, 2, 1, 3).reshape(N_TY * (OV // 4), N_TX * (TS // 4))

def ramp_weights():
    index = jnp.arange(TS, dtype=jnp.int32)
    nearest = jnp.minimum(jnp.minimum(index + 1, TS - index), OV).astype(jnp.float32)
    ramp = 1.0 + 3.0 * nearest / OV
    return ramp[:, None] * ramp[None, :]

def shift_axis(voxel_values, shift, axis):
    whole = jnp.floor_divide(shift, 4)
    frac = (shift - 4 * whole).astype(jnp.float32) * 0.25
    start = (whole + H).astype(jnp.int32)
    first = lax.dynamic_slice_in_dim(voxel_values, start, TS, axis).astype(jnp.float32)
    second = lax.dynamic_slice_in_dim(voxel_values, start + 1, TS, axis).astype(jnp.float32)
    return (1.0 - frac) * first + frac * second

def to_pieces(volume):
    slice_depth = volume.shape[0]
    grid_side = TS // SUBBLOCK_SIDE
    shaped = volume.reshape(slice_depth, grid_side, SUBBLOCK_SIDE, grid_side, SUBBLOCK_SIDE).transpose(1, 3, 0, 2, 4)
    return shaped.reshape(grid_side * grid_side, slice_depth * SUBBLOCK_SIDE * SUBBLOCK_SIDE)

def reduce_resolution(voxel_values):
    count, slice_depth, height, width = voxel_values.shape
    shaped = voxel_values.astype(jnp.float32).reshape(count, slice_depth // 2, 2, height // 2, 2, width // 2, 2)
    return lax.optimization_barrier(jnp.sum(shaped, axis=(2, 4, 6))) * 0.125

def assemble(quadrant_blocks):
    count, slice_depth, height, width = quadrant_blocks.shape
    shaped = quadrant_blocks.reshape(count // 4, 2, 2, slice_depth, height, width).transpose(0, 3, 1, 4, 2, 5)
    return shaped.reshape(count // 4, slice_depth * 4 * height * width)

def reference(tiles, shifts, piece_target, coarse_target):
    right_bins = bin_columns(tiles[..., TS - OV:])
    left_bins = bin_columns(tiles[..., :OV])
    bottom_bins = bin_rows(tiles[..., TS - OV:, :])
    top_bins = bin_rows(tiles[..., :OV, :])
    next_left = jnp.concatenate([left_bins[:, 1:], jnp.zeros_like(left_bins[:, :1])], axis=1)
    next_top = jnp.concatenate([top_bins[1:], jnp.zeros_like(top_bins[:1])], axis=0)
    corr_right = layout(phase_surface(right_bins, next_left))
    corr_below = layout(phase_surface(bottom_bins, next_top))
    device_list = N_TY * N_TX
    placed_grid = tiles.transpose(2, 0, 3, 1, 4).reshape(TILE_SLICES, N_TY * TS, N_TX * TS)
    padded = jnp.pad(placed_grid, ((0, 0), (H, H), (H, H)))
    weights = ramp_weights()
    weight_pieces = to_pieces(weights.astype(jnp.bfloat16)[None]).astype(jnp.float32)
    targets = piece_target.reshape(device_list, -1)

    def accumulate(carry, index):
        numer, denom = carry
        row = (index // N_TX).astype(jnp.int32)
        column = (index % N_TX).astype(jnp.int32)
        extended = lax.dynamic_slice(padded, (jnp.int32(0), row * TS, column * TS), (TILE_SLICES, TS + 2 * H, TS + 2 * H))
        along_y = shift_axis(extended, shifts[row, column, 0], 1).astype(jnp.bfloat16)
        resampled = shift_axis(along_y, shifts[row, column, 1], 2)
        weighted = (weights[None] * resampled).astype(jnp.bfloat16)
        pieces = to_pieces(weighted).astype(jnp.float32)
        chosen = targets[index]
        numer = numer.at[chosen].add(pieces)
        denom = denom.at[chosen].add(weight_pieces)
        return ((numer, denom), None)
    numer0 = jnp.zeros((device_list * DEVICE_SUBBLOCKS, TILE_SLICES * SUBBLOCK_SIDE * SUBBLOCK_SIDE), jnp.float32)
    denom0 = jnp.zeros((device_list * DEVICE_SUBBLOCKS, SUBBLOCK_SIDE * SUBBLOCK_SIDE), jnp.float32)
    (numer, denom), _ = lax.scan(accumulate, (numer0, denom0), jnp.arange(device_list, dtype=jnp.int32))
    joined = (numer.reshape(device_list * DEVICE_SUBBLOCKS, TILE_SLICES, SUBBLOCK_SIDE * SUBBLOCK_SIDE) / jnp.maximum(denom, 1.0)[:, None, :]).astype(jnp.bfloat16)
    first_level = reduce_resolution(joined.reshape(device_list * DEVICE_SUBBLOCKS, TILE_SLICES, SUBBLOCK_SIDE, SUBBLOCK_SIDE)).astype(jnp.bfloat16)
    quadrant_blocks = reduce_resolution(first_level)
    flat_target = coarse_target.reshape(-1)
    source_dev = jnp.arange(device_list * DEVICE_SUBBLOCKS, dtype=jnp.int32) // DEVICE_SUBBLOCKS
    destination = (source_dev // N_TX * N_TX + flat_target // DEVICE_SUBBLOCKS) * DEVICE_SUBBLOCKS + flat_target % DEVICE_SUBBLOCKS
    positioned_tiles = jnp.zeros_like(quadrant_blocks).at[destination].set(quadrant_blocks)
    coarse = assemble(positioned_tiles).astype(jnp.bfloat16)
    return (joined.reshape(device_list * DEVICE_SUBBLOCKS, TILE_SLICES * SUBBLOCK_SIDE * SUBBLOCK_SIDE), coarse, corr_right, corr_below)
```

```python
import functools
import math

import jax
import jax.numpy as jnp
import numpy as np
from jax import lax
from jax.experimental import pallas as pl
from jax.experimental.pallas import tpu as pltpu
from jax.sharding import PartitionSpec as P

SIDE = 32
OV = 48
H = 8
SLOTS = 64
LANES = 128
GROUPS = LANES // SIDE
EDGE = 16
NZ = 4
PIECES = 256
PAIRS = SIDE // 2
WIDE = 2 * LANES
CHUNKS = 4
PER = PAIRS // CHUNKS
F32 = jnp.float32
BF16 = jnp.bfloat16
MESH = pl.DeviceIdType.MESH
DIRECTIONS = ((1, 0), (-1, 0), (0, 1), (0, -1), (1, 1), (1, -1), (-1, 1), (-1, -1))


def highest(left, right):
    return jnp.dot(left, right, precision=lax.Precision.HIGHEST, preferred_element_type=F32)


def iota(shape, dim):
    return lax.broadcasted_iota(jnp.int32, shape, dim)


def mm(a, b):
    return jnp.dot(a, b, preferred_element_type=F32)


def mm_t(a, b):
    return lax.dot_general(a, b, (((1,), (1,)), ((), ())), preferred_element_type=F32)


def mark(condition):
    return condition.astype(F32).astype(BF16)


def front_kernel(
    count_y, count_x, tile_ref, ids_ref,
    tb_ref, side_ref, ct_ref, cb_ref, right_ref, next_left_ref, bottom_ref, next_top_ref, all_ids_ref,
    strips_ref, left_ref, top_ref, halo_send, halo_recv, bin_send, bin_recv, id_send, id_recv,
):
    depth, length, _ = tile_ref.shape
    devices = count_y * count_x
    ty, tx = lax.axis_index("ty"), lax.axis_index("tx")
    me = ty * count_x + tx
    barrier = pltpu.get_barrier_semaphore()

    def at(peer):
        return (peer // count_x, peer % count_x)

    def greet(d, carry):
        pl.semaphore_signal(barrier, inc=1, device_id=at((me + d) % devices), device_id_type=MESH)
        return carry

    lax.fori_loop(1, devices, greet, 0)

    def there(dy, dx):
        y, x = ty + dy, tx + dx
        return (y >= 0) & (y < count_y) & (x >= 0) & (x < count_x)

    low, high = pl.ds(0, EDGE), pl.ds(EDGE, EDGE)

    def landing(dy, dx):
        if dx == 0:
            return tb_ref.at[:, low if dy == 1 else high, :]
        half = low if dx == 1 else high
        if dy == 0:
            return side_ref.at[:, half, :]
        return (ct_ref if dy == 1 else cb_ref).at[:, half, :]

    def halo(i):
        dy, dx = DIRECTIONS[i]
        if dx == 0:
            source = tile_ref.at[:, pl.ds(length - EDGE if dy == 1 else 0, EDGE), :]
        else:
            half = high if dx == 1 else low
            if dy == 0:
                source = strips_ref.at[:, half, :]
            else:
                source = strips_ref.at[:, half, pl.ds(length - LANES if dy == 1 else 0, LANES)]
        return pltpu.make_async_remote_copy(
            src_ref=source,
            dst_ref=landing(dy, dx),
            send_sem=halo_send.at[i],
            recv_sem=halo_recv.at[i],
            device_id=(ty + dy, tx + dx),
            device_id_type=MESH,
        )

    for dy, dx in DIRECTIONS:

        @pl.when(jnp.logical_not(there(-dy, -dx)))
        def _():
            ref = landing(dy, dx)
            ref[...] = jnp.zeros(ref.shape, ref.dtype)

    @pl.when(jnp.logical_not(there(0, 1)))
    def _():
        next_left_ref[...] = jnp.zeros_like(next_left_ref)

    @pl.when(jnp.logical_not(there(1, 0)))
    def _():
        next_top_ref[...] = jnp.zeros_like(next_top_ref)

    row, lane = iota((2 * EDGE, LANES), 0), iota((2 * EDGE, LANES), 1)
    back = lane - (LANES - OV)
    first = mark(((row < EDGE) & (lane == row)) | ((row >= EDGE) & (lane < OV) & (lane // 4 == row - EDGE)))
    last = mark(
        ((row < EDGE) & (lane - (LANES - EDGE) == row)) | ((row >= EDGE) & (back >= 0) & (back // 4 == row - EDGE))
    )
    left = right = jnp.zeros((EDGE, length), F32)
    for z in range(depth):
        value = mm_t(first, tile_ref[z, :, :LANES])
        strips_ref[z, :EDGE, :] = value[:EDGE].astype(BF16)
        left += value[EDGE:]
        value = mm_t(last, tile_ref[z, :, length - LANES :])
        strips_ref[z, EDGE:, :] = value[:EDGE].astype(BF16)
        right += value[EDGE:]

    pl.semaphore_wait(barrier, devices - 1)
    for i, (dy, dx) in enumerate(DIRECTIONS):

        @pl.when(there(dy, dx))
        def _():
            halo(i).start()

    def ids(source, target, peer):
        return pltpu.make_async_remote_copy(
            src_ref=ids_ref,
            dst_ref=all_ids_ref.at[target],
            send_sem=id_send.at[source],
            recv_sem=id_recv.at[target],
            device_id=at(peer),
            device_id_type=MESH,
        )

    def start(d, carry):
        peer = (me + d) % devices
        ids(peer, me, peer).start()
        return carry

    lax.fori_loop(1, devices, start, 0)
    all_ids_ref[me] = ids_ref[...]

    top = bottom = jnp.zeros((EDGE, length), F32)
    for z in range(depth):
        top += mm(first[EDGE:], tile_ref[z, :LANES, :])
        bottom += mm(last[EDGE:], tile_ref[z, length - LANES :, :])
    pool = (iota((length, length // 4), 0) // 4 == iota((length, length // 4), 1)).astype(F32)
    scale = 1.0 / math.sqrt(16.0 * depth)
    left_ref[...] = highest(left, pool) * scale
    top_ref[...] = highest(top, pool) * scale

    def bins(i):
        return pltpu.make_async_remote_copy(
            src_ref=(left_ref, top_ref)[i],
            dst_ref=(next_left_ref, next_top_ref)[i],
            send_sem=bin_send.at[i],
            recv_sem=bin_recv.at[i],
            device_id=((ty, tx - 1), (ty - 1, tx))[i],
            device_id_type=MESH,
        )

    toward = ((0, -1), (-1, 0))
    for i in range(2):

        @pl.when(there(*toward[i]))
        def _():
            bins(i).start()

    right_ref[...] = highest(right, pool) * scale
    bottom_ref[...] = highest(bottom, pool) * scale

    for i, (dy, dx) in enumerate(DIRECTIONS):

        @pl.when(there(-dy, -dx))
        def _():
            halo(i).wait_recv()

        @pl.when(there(dy, dx))
        def _():
            halo(i).wait_send()

    for i in range(2):
        dy, dx = toward[i]

        @pl.when(there(-dy, -dx))
        def _():
            bins(i).wait_recv()

        @pl.when(there(dy, dx))
        def _():
            bins(i).wait_send()

    def finish(d, carry):
        peer = (me + d) % devices
        copy = ids(peer, peer, peer)
        copy.wait_send()
        copy.wait_recv()
        return carry

    lax.fori_loop(1, devices, finish, 0)


def front(tile, ids, count_y, count_x):
    depth, length, _ = tile.shape
    devices = count_y * count_x
    vmem = pl.BlockSpec(memory_space=pltpu.VMEM)
    strip = jax.ShapeDtypeStruct((depth, 2 * EDGE, length), BF16)
    corner = jax.ShapeDtypeStruct((depth, 2 * EDGE, LANES), BF16)
    bins = jax.ShapeDtypeStruct((EDGE, length // 4), F32)
    return pl.pallas_call(
        functools.partial(front_kernel, count_y, count_x),
        out_shape=[strip, strip, corner, corner, bins, bins, bins, bins,
                   jax.ShapeDtypeStruct((devices, 8, LANES), jnp.int32)],
        in_specs=[vmem] * 2,
        out_specs=[vmem] * 9,
        scratch_shapes=[
            pltpu.VMEM((depth, 2 * EDGE, length), BF16),
            pltpu.VMEM((EDGE, length // 4), F32),
            pltpu.VMEM((EDGE, length // 4), F32),
            pltpu.SemaphoreType.DMA((8,)),
            pltpu.SemaphoreType.DMA((8,)),
            pltpu.SemaphoreType.DMA((2,)),
            pltpu.SemaphoreType.DMA((2,)),
            pltpu.SemaphoreType.DMA((devices,)),
            pltpu.SemaphoreType.DMA((devices,)),
        ],
        name="front",
        compiler_params=pltpu.CompilerParams(
            collective_id=0, has_side_effects=True, vmem_limit_bytes=16 * 2**20
        ),
        cost_estimate=pl.CostEstimate(flops=10**8, bytes_accessed=2**21, transcendentals=0),
    )(tile, ids)


def swap_groups(parts):
    group = iota(parts[0].shape, 1) // SIDE

    def pick(choices):
        value = choices[3]
        for g in range(3):
            value = jnp.where(group == g, choices[g], value)
        return value

    turned = []
    for d in range(GROUPS):
        mixed = pick([parts[(g + d) % GROUPS] for g in range(GROUPS)])
        turned.append(pltpu.roll(mixed, d * SIDE, 1) if d else mixed)
    return [pick([turned[(j - g) % GROUPS] for j in range(GROUPS)]) for g in range(GROUPS)]


def taps(offset, out, column):
    whole, frac = offset
    at = out + whole + H
    return (
        jnp.where(column == at, 1.0 - frac, 0.0) + jnp.where(column == at + 1, frac, 0.0)
    ).astype(BF16)


def split_shift(shift):
    whole = lax.shift_right_arithmetic(shift, 2)
    return whole, (shift - 4 * whole).astype(F32) * 0.25


def ramp_at(index, length):
    nearest = jnp.minimum(jnp.minimum(index + 1, length - index), OV).astype(F32)
    return 1.0 + nearest * (3.0 / OV)


def pieces_kernel(shift_ref, tile_ref, tb_ref, side_ref, ct_ref, cb_ref, out_ref, work_ref):
    depth, length, _ = tile_ref.shape
    grid = length // SIDE

    def turned(shape, dim):
        at = iota(shape, dim)
        return (at % grid) * SIDE + at // grid

    def edge_column(shape, dim):
        c = iota(shape, dim)
        return jnp.where(c < EDGE, c + (H - EDGE), c + (length + H - EDGE))

    sy, sx = split_shift(shift_ref[0]), split_shift(shift_ref[1])
    full, thin, wide, corner = (length, length), (length, 2 * EDGE), (2 * EDGE, length), (length, LANES)
    ry = taps(sy, turned(full, 0), iota(full, 1) + H)
    ry_edge = taps(sy, turned(thin, 0), edge_column(thin, 1))
    ry_above = taps(sy, turned(corner, 0), iota(corner, 1) + (H - LANES))
    ry_below = taps(sy, turned(corner, 0), iota(corner, 1) + (length + H))
    rx = taps(sx, iota(full, 1), iota(full, 0) + H)
    rx_edge = taps(sx, iota(wide, 1), edge_column(wide, 0))
    weights = ramp_at(turned((length, 1), 0), length) * ramp_at(iota((1, length), 1), length)
    for z in range(depth):
        along = (mm(ry, tile_ref[z]) + mm(ry_edge, tb_ref[z])).astype(BF16)
        along_side = (
            mm_t(ry, side_ref[z]) + mm_t(ry_above, ct_ref[z]) + mm_t(ry_below, cb_ref[z])
        ).astype(BF16)
        work_ref[z] = weights * (mm(along, rx) + mm(along_side, rx_edge))

    def pair(i, carry):
        start = pl.multiple_of(i * 2 * grid, 2 * grid)
        for q in range(length // LANES):
            parts = [work_ref[z, pl.ds(start, 2 * grid), q * LANES : (q + 1) * LANES] for z in range(depth)]
            for g, piece in enumerate(swap_groups(parts)):
                rows = pl.ds((q * GROUPS + g) * grid, grid)
                out_ref[i, rows, :LANES] = piece[:grid].astype(BF16)
                out_ref[i, rows, LANES:] = piece[grid:].astype(BF16)
        return carry

    lax.fori_loop(0, PAIRS, pair, 0)


def make_pieces(shifts, tile, tb, side, ct, cb):
    vmem = pl.BlockSpec(memory_space=pltpu.VMEM)
    smem = pl.BlockSpec(memory_space=pltpu.SMEM)
    return pl.pallas_call(
        pieces_kernel,
        out_shape=jax.ShapeDtypeStruct((PAIRS, PIECES, WIDE), BF16),
        in_specs=[smem] + [vmem] * 5,
        out_specs=vmem,
        scratch_shapes=[pltpu.VMEM(tile.shape, F32)],
        name="pieces",
        compiler_params=pltpu.CompilerParams(vmem_limit_bytes=32 * 2**20),
        cost_estimate=pl.CostEstimate(flops=2 * 10**9, bytes_accessed=2**23, transcendentals=0),
    )(shifts, tile, tb, side, ct, cb)


def phase(cos_a, sin_a, cos_b, sin_b, own, other):
    def spectrum(values):
        left_cos = highest(cos_a, values)
        left_sin = highest(sin_a, values)
        re = highest(left_cos, cos_b) - highest(left_sin, sin_b)
        im = -(highest(left_cos, sin_b) + highest(left_sin, cos_b))
        return (re, im)

    own_re, own_im = spectrum(own)
    other_re, other_im = spectrum(other)
    cross_re = own_re * other_re + own_im * other_im
    cross_im = own_im * other_re - own_re * other_im
    scale = 1.0 / jnp.sqrt(cross_re * cross_re + cross_im * cross_im + 1.0)
    normed_re = cross_re * scale
    normed_im = cross_im * scale
    out = highest(highest(cos_a, normed_re) - highest(sin_a, normed_im), cos_b)
    return out - highest(highest(sin_a, normed_re) + highest(cos_a, normed_im), sin_b)


def exchange_kernel(
    count_y, count_x, length, cap, piece_ref, ids_ref, ca_ref, sa_ref, cb_ref, sb_ref, right_ref, left_ref, bottom_ref, top_ref,
    joined_ref, coarse_ref, corr_right_ref, corr_below_ref,
    pack_ref, send_ref, recv_ref, targets_ref, rank_ref, turn_ref, reduce_ref, inv_ref, dense_ref, zsend_ref, zrecv_ref,
    quads_ref, all_quads_ref, plane_send, plane_recv, line_send, line_recv, row_send, row_recv,
):
    ny = count_x // NZ
    plane = count_y * ny
    devices = count_y * count_x
    sums = NZ * SLOTS
    grid = length // SIDE
    ty, tx = lax.axis_index("ty"), lax.axis_index("tx")
    me = ty * count_x + tx
    y, z = tx % ny, tx // ny
    mine = ty * ny + y
    near = z + 1 - 2 * (z % 2)
    cross, diag = NZ - 1 - z, NZ - 1 - near
    mid = ((z + 1) // 2) % 2
    barrier = pltpu.get_barrier_semaphore()

    def in_plane(p):
        return (p // ny, z * ny + p % ny)

    def in_line(other):
        return (ty, other * ny + y)

    def greet_plane(d, carry):
        pl.semaphore_signal(barrier, inc=1, device_id=in_plane((mine + d) % plane), device_id_type=MESH)
        return carry

    def greet_row(d, carry):
        pl.semaphore_signal(barrier, inc=1, device_id=(ty, (z * ny + d) % count_x), device_id_type=MESH)
        return carry

    lax.fori_loop(1, plane, greet_plane, 0)
    lax.fori_loop(ny, count_x, greet_row, 0)

    def targets_of(device):
        block = ids_ref[device]
        return jnp.concatenate([block[0:1, :], block[1:2, :]], axis=1)

    def column_of(targets):
        owner = targets // SLOTS
        return (owner // count_x) * ny + owner % ny

    def sum_row_of(targets):
        return ((targets // SLOTS) % count_x) // ny * SLOTS + targets % SLOTS

    square = (PIECES, PIECES)
    earlier = mark(iota(square, 0) < iota(square, 1))
    column = column_of(targets_of(me))
    onehot = (iota((targets_ref.shape[0], PIECES), 0) == column).astype(F32)
    rank = jnp.sum(onehot * mm(onehot.astype(BF16), earlier), axis=0, keepdims=True)
    position = (column * cap).astype(F32) + rank
    pack_ref[...] = mark(iota((plane * cap, PIECES), 0).astype(F32) == position)

    pl.semaphore_wait(barrier, plane - 1 + count_x - ny)

    def rows_of(p):
        return pl.ds(pl.multiple_of(p * cap, cap), cap)

    def plane_copy(c, source, target, peer):
        part = pl.ds(c * PER, PER)
        return pltpu.make_async_remote_copy(
            src_ref=send_ref.at[part, rows_of(source), :],
            dst_ref=recv_ref.at[part, rows_of(target), :],
            send_sem=plane_send.at[c, source],
            recv_sem=plane_recv.at[c, target],
            device_id=in_plane(peer),
            device_id_type=MESH,
        )

    def pack(c, carry):
        for j in range(PER):
            i = c * PER + j
            send_ref[i] = mm(pack_ref[...], piece_ref[i]).astype(BF16)

        def start(d, inner):
            peer = (mine + d) % plane
            plane_copy(c, peer, mine, peer).start()
            return inner

        lax.fori_loop(1, plane, start, 0)
        for j in range(PER):
            i = c * PER + j
            recv_ref[i, rows_of(mine), :] = send_ref[i, rows_of(mine), :]
        return carry

    lax.fori_loop(0, CHUNKS, pack, 0)

    targets_ref[...] = jnp.full(targets_ref.shape, -1, jnp.int32)

    def fetch(p, carry):
        targets_ref[pl.ds(p, 1), :] = targets_of((p // ny) * count_x + z * ny + p % ny)
        return carry

    lax.fori_loop(0, plane, fetch, 0)
    rank_ref[...] = mm(mark(column_of(targets_ref[...]) == mine), earlier)

    def turn(p, carry):
        targets = targets_ref[pl.ds(p, 1), :]
        into = jnp.where(column_of(targets) == mine, sum_row_of(targets), -1)
        into = mark(iota((sums, PIECES), 0) == into)
        listed = mark(iota((cap, PIECES), 0).astype(F32) == rank_ref[pl.ds(p, 1), :])
        turn_ref[rows_of(p), :] = mm_t(listed, into).astype(BF16)
        return carry

    lax.fori_loop(0, plane, turn, 0)
    reduce_ref[...] = mm_t(mark(iota((sums, sums), 0) == iota((sums, sums), 1)), turn_ref[...]).astype(BF16)

    slot = iota((SLOTS, PIECES), 0) + me * SLOTS

    def count(device, counts):
        return counts + (targets_of(device) == slot).astype(F32)

    counts = lax.fori_loop(0, devices, count, jnp.zeros((SLOTS, PIECES), F32)).astype(BF16)
    place = iota((PIECES, WIDE), 0)
    lane = iota((PIECES, WIDE), 1)
    across = ramp_at(place // grid * SIDE + lane % SIDE, length)
    down = place % grid * SIDE + lane // LANES

    def weigh(i, carry):
        patch = (ramp_at(down + 2 * i, length) * across).astype(BF16)
        inv_ref[i] = 1.0 / jnp.maximum(mm(counts, patch), 1.0)
        return carry

    lax.fori_loop(0, PAIRS, weigh, 0)

    tables = (ca_ref[...], sa_ref[...], cb_ref[...], sb_ref[...])
    bins = corr_right_ref.shape[0]
    corr_right_ref[...] = phase(*tables, right_ref[...], left_ref[...])[:bins]
    corr_below_ref[...] = phase(*tables, bottom_ref[...], top_ref[...])[:bins]

    def line_copy(c, kind):
        part = pl.ds(c * PER, PER)
        unit, slot, peer = (
            (near, 0, near),
            (diag, 1, diag),
            (cross, 3 - mid, mid * cross + (1 - mid) * near),
        )[kind]
        return pltpu.make_async_remote_copy(
            src_ref=zsend_ref.at[part, pl.ds(pl.multiple_of(unit * SLOTS, SLOTS), SLOTS), :],
            dst_ref=zrecv_ref.at[slot, part],
            send_sem=line_send.at[c, kind],
            recv_sem=line_recv.at[c, slot],
            device_id=in_line(peer),
            device_id_type=MESH,
        )

    def line_arrived(c, slot):
        part = pl.ds(c * PER, PER)
        pltpu.make_async_remote_copy(
            src_ref=zsend_ref.at[part, pl.ds(0, SLOTS), :],
            dst_ref=zrecv_ref.at[slot, part],
            send_sem=line_send.at[c, 0],
            recv_sem=line_recv.at[c, slot],
            device_id=in_line(near),
            device_id_type=MESH,
        ).wait_recv()

    def unit_rows(unit):
        return pl.ds(pl.multiple_of(unit * SLOTS, SLOTS), SLOTS)

    def reduce(c):
        def arrived(d, carry):
            peer = (mine + d) % plane
            plane_copy(c, peer, peer, peer).wait_recv()
            return carry

        lax.fori_loop(1, plane, arrived, 0)
        for i in range(c * PER, (c + 1) * PER):
            value = mm(reduce_ref[...], recv_ref[i])
            dense_ref[i] = value
            zsend_ref[i] = value.astype(BF16)
        line_copy(c, 2).start()
        line_copy(c, 0).start()

        @pl.when(mid == 0)
        def _():
            line_copy(c, 1).start()

    def merge(c):
        @pl.when(mid == 1)
        def _():
            line_arrived(c, 3)
            for i in range(c * PER, (c + 1) * PER):
                value = dense_ref[i, unit_rows(diag), :] + zrecv_ref[3, i].astype(F32)
                zsend_ref[i, unit_rows(diag), :] = value.astype(BF16)
            line_copy(c, 1).start()

    inner = iota((WIDE, LANES), 0)
    outer = iota((WIDE, LANES), 1)
    pooled = inner % LANES // (2 * SIDE) * (SIDE // 2) + inner % SIDE // 2

    def final(c, quads):
        line_arrived(c, 0)
        line_arrived(c, 1)

        @pl.when(mid == 1)
        def _():
            line_arrived(c, 2)
            for i in range(c * PER, (c + 1) * PER):
                dense_ref[i, unit_rows(z), :] = dense_ref[i, unit_rows(z), :] + zrecv_ref[2, i].astype(F32)

        level = jnp.zeros((SLOTS, LANES), F32)
        rows = []
        for j in range(PER):
            i = c * PER + j
            value = dense_ref[i, unit_rows(z), :] + zrecv_ref[0, i].astype(F32) + zrecv_ref[1, i].astype(F32)
            value = (value * inv_ref[i]).astype(BF16)
            level += mm(value, mark(outer == pooled + j * SIDE))
            value = value.astype(F32)
            rows += [value[:, :LANES], value[:, LANES:]]
        for g in range(2 * PER // GROUPS):
            for s, part in enumerate(swap_groups(rows[g * GROUPS : (g + 1) * GROUPS])):
                start = s * SIDE * SIDE + (c * (2 * PER // GROUPS) + g) * LANES
                joined_ref[:, start : start + LANES] = part.astype(BF16)
        a, b = iota((LANES, LANES), 0), iota((LANES, LANES), 1)
        into = (2 * c + a // (2 * SIDE)) * (SIDE // 4) + a % (SIDE // 2) // 2
        return quads + mm((level * 0.125).astype(BF16), mark(b == into))

    quads = jnp.zeros((SLOTS, LANES), F32)
    for c in range(CHUNKS + 2):
        if c < CHUNKS:
            reduce(c)
        if 1 <= c <= CHUNKS:
            merge(c - 1)
        if c >= 2:
            quads = final(c - 2, quads)

    quads_ref[...] = (quads * 0.125).astype(BF16)

    def row_copy(source, target, peer):
        return pltpu.make_async_remote_copy(
            src_ref=quads_ref,
            dst_ref=all_quads_ref.at[target],
            send_sem=row_send.at[source],
            recv_sem=row_recv.at[target],
            device_id=(ty, peer),
            device_id_type=MESH,
        )

    def start_row(d, carry):
        peer = (tx + d) % count_x
        row_copy(peer, tx, peer).start()
        return carry

    lax.fori_loop(1, count_x, start_row, 0)
    all_quads_ref[tx] = quads_ref[...]

    def sent(c, carry):
        def one(d, inner):
            peer = (mine + d) % plane
            plane_copy(c, peer, peer, peer).wait_send()
            return inner

        for kind in range(3):
            line_copy(c, kind).wait_send()
        return lax.fori_loop(1, plane, one, carry)

    lax.fori_loop(0, CHUNKS, sent, 0)

    def finish_row(d, carry):
        peer = (tx + d) % count_x
        copy = row_copy(peer, peer, peer)
        copy.wait_send()
        copy.wait_recv()
        return carry

    lax.fori_loop(1, count_x, finish_row, 0)

    u = iota((SLOTS, SLOTS), 0)
    wanted = tx * SLOTS + 4 * (u % (SLOTS // 4)) + u // (SLOTS // 4)

    def regroup(source, placed):
        named = ids_ref[ty * count_x + source][2:3, :SLOTS]
        return placed + mm(mark(named == wanted), all_quads_ref[source])

    placed = lax.fori_loop(0, count_x, regroup, jnp.zeros((SLOTS, LANES), F32)).astype(BF16)
    side = SIDE // 4
    a, b = iota((LANES, WIDE), 0), iota((LANES, WIDE), 1)
    out = jnp.zeros((SLOTS // 4, WIDE), F32)
    for q in range(4):
        into = (q // 2) * 2 * side * side + a // side * 2 * side + (q % 2) * side + a % side
        out += mm(placed[q * (SLOTS // 4) : (q + 1) * (SLOTS // 4)], mark((a < side * side) & (b == into)))
    coarse_ref[...] = out.astype(BF16)


def dft_tables(length, padded):
    index = np.arange(length)
    angle = (index[:, None] * index[None, :] % length) * (2.0 * math.pi / length)
    pad = ((0, padded - length),) * 2
    return tuple(
        jnp.asarray(np.pad(table / math.sqrt(length), pad).astype(np.float32)) for table in (np.cos(angle), np.sin(angle))
    )


def exchange(pieces, ids, bins, length, cap, count_y, count_x, collective_id):
    plane = count_y * (count_x // NZ)
    sums = NZ * SLOTS
    vmem = pl.BlockSpec(memory_space=pltpu.VMEM)
    tables = dft_tables(OV // 4, EDGE) + dft_tables(length // 4, length // 4)
    corr = jax.ShapeDtypeStruct((OV // 4, length // 4), F32)
    return pl.pallas_call(
        functools.partial(exchange_kernel, count_y, count_x, length, cap),
        out_shape=[
            jax.ShapeDtypeStruct((SLOTS, SIDE * LANES), BF16),
            jax.ShapeDtypeStruct((SLOTS // 4, WIDE), BF16),
            corr,
            corr,
        ],
        in_specs=[vmem] * 10,
        out_specs=[vmem] * 4,
        scratch_shapes=[
            pltpu.VMEM((plane * cap, PIECES), BF16),
            pltpu.VMEM((PAIRS, plane * cap, WIDE), BF16),
            pltpu.VMEM((PAIRS, plane * cap, WIDE), BF16),
            pltpu.VMEM((max(16, plane), PIECES), jnp.int32),
            pltpu.VMEM((max(16, plane), PIECES), F32),
            pltpu.VMEM((plane * cap, sums), BF16),
            pltpu.VMEM((sums, plane * cap), BF16),
            pltpu.VMEM((PAIRS, SLOTS, WIDE), F32),
            pltpu.VMEM((PAIRS, sums, WIDE), F32),
            pltpu.VMEM((PAIRS, sums, WIDE), BF16),
            pltpu.VMEM((4, PAIRS, SLOTS, WIDE), BF16),
            pltpu.VMEM((SLOTS, LANES), BF16),
            pltpu.VMEM((count_x, SLOTS, LANES), BF16),
            pltpu.SemaphoreType.DMA((CHUNKS, plane)),
            pltpu.SemaphoreType.DMA((CHUNKS, plane)),
            pltpu.SemaphoreType.DMA((CHUNKS, 3)),
            pltpu.SemaphoreType.DMA((CHUNKS, 4)),
            pltpu.SemaphoreType.DMA((count_x,)),
            pltpu.SemaphoreType.DMA((count_x,)),
        ],
        name="exchange",
        compiler_params=pltpu.CompilerParams(
            collective_id=collective_id, has_side_effects=True, vmem_limit_bytes=44 * 2**20
        ),
        cost_estimate=pl.CostEstimate(flops=3 * 10**9, bytes_accessed=2**23, transcendentals=0),
    )(pieces, ids, *tables, *bins)


def per_device(tiles, shifts, piece_target, coarse_target):
    tile = tiles[0, 0]
    count_y = lax.axis_size("ty")
    count_x = lax.axis_size("tx")
    _, length, _ = tile.shape
    grid = length // SIDE
    cap = NZ * 2 * PIECES // (count_y * count_x)
    targets = piece_target[0, 0].reshape(grid, grid).T.reshape(2, LANES)
    coarse_ids = jnp.pad(coarse_target[0], ((0, 0), (0, LANES - SLOTS)), constant_values=-1)
    ids = jnp.pad(jnp.concatenate([targets, coarse_ids]), ((0, 5), (0, 0)), constant_values=-1)
    tb, side, ct, cb, right, next_left, bottom, next_top, all_ids = front(tile, ids, count_y, count_x)
    pieces = make_pieces(shifts[0, 0], tile, tb, side, ct, cb)
    bins = (right, next_left, bottom, next_top)
    return tuple(exchange(pieces, all_ids, bins, length, cap, count_y, count_x, 1))


def solution(mesh):
    placed = (
        P("ty", "tx", None, None, None),
        P("ty", "tx", None),
        P("ty", "tx", None),
        P("ty", "tx", None),
    )
    return jax.shard_map(
        per_device,
        mesh=mesh,
        in_specs=placed,
        out_specs=(P(("ty", "tx"), None), P(("ty", "tx"), None), P("ty", "tx"), P("ty", "tx")),
        check_vma=False,
    )
```

```python
import functools
import math

import jax
import jax.numpy as jnp
import numpy as np
from jax import lax
from jax.experimental import pallas as pl
from jax.experimental.pallas import tpu as pltpu
from jax.sharding import PartitionSpec as P

SIDE = 32
OV = 48
H = 8
SLOTS = 64
LANES = 128
GROUPS = LANES // SIDE
EDGE = 2 * H
NZ = 4
PIECES = 256
PAIRS = SIDE // 2
WIDE = 2 * LANES
CHUNKS = 8
AHEAD = 3
PER = PAIRS // CHUNKS
F32 = jnp.float32
BF16 = jnp.bfloat16
MESH = pl.DeviceIdType.MESH
DIRECTIONS = ((1, 0), (-1, 0), (0, 1), (0, -1), (1, 1), (1, -1), (-1, 1), (-1, -1))


def highest(left, right):
    return jnp.dot(left, right, precision=lax.Precision.HIGHEST, preferred_element_type=F32)


def iota(shape, dim):
    return lax.broadcasted_iota(jnp.int32, shape, dim)


def mm(a, b):
    return jnp.dot(a, b, preferred_element_type=F32)


def mm_t(a, b):
    return lax.dot_general(a, b, (((1,), (1,)), ((), ())), preferred_element_type=F32)


def mark(condition):
    return condition.astype(F32).astype(BF16)


def swap_groups(parts):
    group = iota(parts[0].shape, 1) // SIDE

    def pick(choices):
        value = choices[3]
        for g in range(3):
            value = jnp.where(group == g, choices[g], value)
        return value

    turned = []
    for d in range(GROUPS):
        mixed = pick([parts[(g + d) % GROUPS] for g in range(GROUPS)])
        turned.append(pltpu.roll(mixed, d * SIDE, 1) if d else mixed)
    return [pick([turned[(j - g) % GROUPS] for j in range(GROUPS)]) for g in range(GROUPS)]


def taps(offset, out, column):
    whole, frac = offset
    at = out + whole + H
    return (
        jnp.where(column == at, 1.0 - frac, 0.0) + jnp.where(column == at + 1, frac, 0.0)
    ).astype(BF16)


def split_shift(shift):
    whole = lax.shift_right_arithmetic(shift, 2)
    return whole, (shift - 4 * whole).astype(F32) * 0.25


def ramp_at(index, length):
    nearest = jnp.minimum(jnp.minimum(index + 1, length - index), OV).astype(F32)
    return 1.0 + nearest * (3.0 / OV)


def turned_row(at, grid):
    return (at % grid) * SIDE + at // grid


def edge_index(c, length):
    return c % H + jnp.where(c < EDGE, 0, length + H)


def column_of(targets, count_x):
    owner = targets // SLOTS
    return (owner // count_x) * (count_x // NZ) + owner % (count_x // NZ)


def front_kernel(
    count_y, count_x, shift_ref, tile_hbm, piece_ids_hbm, coarse_ids_hbm,
    along_ref, aside_ref, right_ref, next_left_ref, bottom_ref, next_top_ref, all_ids_ref, most_ref,
    tile_ref, piece_ids_ref, coarse_ids_ref, ids_ref, ids_rows_ref, tb_ref, side_ref, ct_ref, cb_ref, strips_ref, ends_ref, left_ref, top_ref, partial_ref,
    tile_sem, halo_send, halo_recv, bin_send, bin_recv, id_send, id_recv,
):
    depth, length, _ = tile_ref.shape
    grid = length // SIDE
    devices = count_y * count_x
    ty, tx = lax.axis_index("ty"), lax.axis_index("tx")
    me = ty * count_x + tx
    barrier = pltpu.get_barrier_semaphore()
    load = pltpu.make_async_copy(tile_hbm, tile_ref, tile_sem.at[0])
    load.start()
    loads = (
        pltpu.make_async_copy(piece_ids_hbm, piece_ids_ref, tile_sem.at[1]),
        pltpu.make_async_copy(coarse_ids_hbm, coarse_ids_ref, tile_sem.at[2]),
    )
    for copy in loads:
        copy.start()

    def at(peer):
        return (peer // count_x, peer % count_x)

    def greet(d, carry):
        pl.semaphore_signal(barrier, inc=1, device_id=at((me + d) % devices), device_id_type=MESH)
        return carry

    lax.fori_loop(1, devices, greet, 0)

    def there(dy, dx):
        y, x = ty + dy, tx + dx
        return (y >= 0) & (y < count_y) & (x >= 0) & (x < count_x)

    low, high = pl.ds(0, EDGE), pl.ds(EDGE, EDGE)

    def landing(dy, dx):
        if dx == 0:
            return tb_ref.at[:, low if dy == 1 else high, :]
        half = low if dx == 1 else high
        if dy == 0:
            return side_ref.at[:, half, :]
        return (ct_ref if dy == 1 else cb_ref).at[:, half, :]

    def halo(i):
        dy, dx = DIRECTIONS[i]
        if dx == 0:
            source = ends_ref.at[:, high if dy == 1 else low, :]
        else:
            half = high if dx == 1 else low
            if dy == 0:
                source = strips_ref.at[:, half, :]
            else:
                source = strips_ref.at[:, half, pl.ds(length - LANES if dy == 1 else 0, LANES)]
        return pltpu.make_async_remote_copy(
            src_ref=source,
            dst_ref=landing(dy, dx),
            send_sem=halo_send.at[i],
            recv_sem=halo_recv.at[i],
            device_id=(ty + dy, tx + dx),
            device_id_type=MESH,
        )

    for dy, dx in DIRECTIONS:

        @pl.when(jnp.logical_not(there(-dy, -dx)))
        def _():
            ref = landing(dy, dx)
            ref[...] = jnp.zeros(ref.shape, ref.dtype)

    @pl.when(jnp.logical_not(there(0, 1)))
    def _():
        next_left_ref[...] = jnp.zeros_like(next_left_ref)

    @pl.when(jnp.logical_not(there(1, 0)))
    def _():
        next_top_ref[...] = jnp.zeros_like(next_top_ref)

    for copy in loads:
        copy.wait()
    ids_ref[...] = jnp.full(ids_ref.shape, -1, jnp.int32)
    ids_ref[0:1, :] = piece_ids_ref[...]
    ids_ref[1:2, :SLOTS] = coarse_ids_ref[...]

    row, lane = iota((2 * EDGE, LANES), 0), iota((2 * EDGE, LANES), 1)
    back = lane - (LANES - OV)
    first_bins = (row >= EDGE) & (lane < OV) & (lane // 4 == row - EDGE)
    last_bins = (row >= EDGE) & (back >= 0) & (back // 4 == row - EDGE)

    def picks(z):
        own = (row < EDGE) & (row // H == z % 2)
        first = mark((own & (lane == row % H)) | first_bins)
        return first, mark((own & (lane - (LANES - H) == row % H)) | last_bins)

    load.wait()
    left = right = jnp.zeros((EDGE, length), F32)
    for k in range(depth // 2):
        lows = highs = jnp.zeros((2 * EDGE, length), F32)
        for z in (2 * k, 2 * k + 1):
            first, last = picks(z)
            lows += mm_t(first, tile_ref[z, :, :LANES])
            highs += mm_t(last, tile_ref[z, :, length - LANES :])
        left += lows[EDGE:]
        right += highs[EDGE:]
        strips_ref[k, :EDGE, :] = lows[:EDGE].astype(BF16)
        strips_ref[k, EDGE:, :] = highs[:EDGE].astype(BF16)
        pair = (2 * k, 2 * k + 1)
        ends = [tile_ref[z, :EDGE, :].astype(F32)[:H] for z in pair]
        ends += [tile_ref[z, length - EDGE :, :].astype(F32)[H:] for z in pair]
        ends_ref[k] = jnp.concatenate(ends).astype(BF16)
    first, last = picks(0)

    pl.semaphore_wait(barrier, devices - 1)
    for i, (dy, dx) in enumerate(DIRECTIONS):

        @pl.when(there(dy, dx))
        def _():
            halo(i).start()

    def ids(source, target, peer):
        return pltpu.make_async_remote_copy(
            src_ref=ids_ref,
            dst_ref=all_ids_ref.at[target],
            send_sem=id_send.at[source],
            recv_sem=id_recv.at[target],
            device_id=at(peer),
            device_id_type=MESH,
        )

    def start(d, carry):
        peer = (me + d) % devices
        ids(peer, me, peer).start()
        return carry

    lax.fori_loop(1, devices, start, 0)
    all_ids_ref[me] = ids_ref[...]

    top = bottom = jnp.zeros((EDGE, length), F32)
    for z in range(depth):
        top += mm(first[EDGE:], tile_ref[z, :LANES, :])
        bottom += mm(last[EDGE:], tile_ref[z, length - LANES :, :])
    pool = (iota((length, length // 4), 0) // 4 == iota((length, length // 4), 1)).astype(F32)
    scale = 1.0 / math.sqrt(16.0 * depth)
    bins_of = highest(jnp.concatenate([left, top, right, bottom]), pool) * scale
    left_ref[...] = bins_of[:EDGE]
    top_ref[...] = bins_of[EDGE : 2 * EDGE]
    right_ref[...] = bins_of[2 * EDGE : 3 * EDGE]
    bottom_ref[...] = bins_of[3 * EDGE :]

    def bins(i):
        return pltpu.make_async_remote_copy(
            src_ref=(left_ref, top_ref)[i],
            dst_ref=(next_left_ref, next_top_ref)[i],
            send_sem=bin_send.at[i],
            recv_sem=bin_recv.at[i],
            device_id=((ty, tx - 1), (ty - 1, tx))[i],
            device_id_type=MESH,
        )

    toward = ((0, -1), (-1, 0))
    for i in range(2):

        @pl.when(there(*toward[i]))
        def _():
            bins(i).start()

    sy = split_shift(shift_ref[0])
    full, thin, corner = (length, length), (length, 2 * EDGE), (length, LANES)
    ry = taps(sy, turned_row(iota(full, 0), grid), iota(full, 1) + H)
    for z in range(depth):
        partial_ref[z] = mm(ry, tile_ref[z])
    rows, c = turned_row(iota(thin, 0), grid), iota(thin, 1)
    ry_edges = [taps(sy, rows, jnp.where(c // H % 2 == par, edge_index(c, length), -1)) for par in range(2)]
    ry_above = taps(sy, turned_row(iota(corner, 0), grid), iota(corner, 1) + (H - LANES))
    ry_below = taps(sy, turned_row(iota(corner, 0), grid), iota(corner, 1) + (length + H))

    def finish(d, carry):
        peer = (me + d) % devices
        copy = ids(peer, peer, peer)
        copy.wait_send()
        copy.wait_recv()
        return carry

    lax.fori_loop(1, devices, finish, 0)

    def gather(d, carry):
        ids_rows_ref[pl.ds(d, 1), :] = all_ids_ref[d][0:1, :]
        return carry

    lax.fori_loop(0, devices, gather, 0)
    columns = column_of(ids_rows_ref[...], count_x)
    ones = jnp.ones((PIECES, LANES), BF16)
    most = jnp.zeros((devices, LANES), F32)
    for p in range(count_y * (count_x // NZ)):
        most = jnp.maximum(most, mm(mark(columns == p), ones))
    most_ref[0, 0] = jnp.max(most).astype(jnp.int32)

    for i, (dy, dx) in enumerate(DIRECTIONS):

        @pl.when(there(-dy, -dx))
        def _():
            halo(i).wait_recv()

    part = length // CHUNKS
    lane = iota((length, 2 * EDGE), 1)
    for k in range(depth // 2):
        aside = mm_t(ry, side_ref[k]) + mm_t(ry_above, ct_ref[k]) + mm_t(ry_below, cb_ref[k])
        for par in range(2):
            z = 2 * k + par
            along = (partial_ref[z] + mm(ry_edges[par], tb_ref[k])).astype(BF16)
            beside = jnp.where(lane // H % 2 == par, aside, 0.0).astype(BF16)
            for c in range(CHUNKS):
                along_ref[c, z * part : (z + 1) * part, :] = along[c * part : (c + 1) * part]
                aside_ref[c, z * part : (z + 1) * part, :] = beside[c * part : (c + 1) * part]

    for i, (dy, dx) in enumerate(DIRECTIONS):

        @pl.when(there(dy, dx))
        def _():
            halo(i).wait_send()

    for i in range(2):
        dy, dx = toward[i]

        @pl.when(there(-dy, -dx))
        def _():
            bins(i).wait_recv()

        @pl.when(there(dy, dx))
        def _():
            bins(i).wait_send()


def front(shifts, tile, piece_ids, coarse_ids, count_y, count_x):
    depth, length, _ = tile.shape
    devices = count_y * count_x
    vmem = pl.BlockSpec(memory_space=pltpu.VMEM)
    smem = pl.BlockSpec(memory_space=pltpu.SMEM)
    bins = jax.ShapeDtypeStruct((EDGE, length // 4), F32)
    rows = depth * length // CHUNKS
    return pl.pallas_call(
        functools.partial(front_kernel, count_y, count_x),
        out_shape=[
            jax.ShapeDtypeStruct((CHUNKS, rows, length), BF16),
            jax.ShapeDtypeStruct((CHUNKS, rows, 2 * EDGE), BF16),
            bins, bins, bins, bins,
            jax.ShapeDtypeStruct((devices, 2, PIECES), jnp.int32),
            jax.ShapeDtypeStruct((1, 1), jnp.int32),
        ],
        in_specs=[smem] + [pl.BlockSpec(memory_space=pltpu.HBM)] * 3,
        out_specs=[vmem] * 7 + [smem],
        scratch_shapes=[
            pltpu.VMEM(tile.shape, BF16),
            pltpu.VMEM((1, PIECES), jnp.int32),
            pltpu.VMEM((1, SLOTS), jnp.int32),
            pltpu.VMEM((2, PIECES), jnp.int32),
            pltpu.VMEM((devices, PIECES), jnp.int32),
            pltpu.VMEM((depth // 2, 2 * EDGE, length), BF16),
            pltpu.VMEM((depth // 2, 2 * EDGE, length), BF16),
            pltpu.VMEM((depth // 2, 2 * EDGE, LANES), BF16),
            pltpu.VMEM((depth // 2, 2 * EDGE, LANES), BF16),
            pltpu.VMEM((depth // 2, 2 * EDGE, length), BF16),
            pltpu.VMEM((depth // 2, 2 * EDGE, length), BF16),
            pltpu.VMEM((EDGE, length // 4), F32),
            pltpu.VMEM((EDGE, length // 4), F32),
            pltpu.VMEM(tile.shape, F32),
            pltpu.SemaphoreType.DMA((3,)),
            pltpu.SemaphoreType.DMA((8,)),
            pltpu.SemaphoreType.DMA((8,)),
            pltpu.SemaphoreType.DMA((2,)),
            pltpu.SemaphoreType.DMA((2,)),
            pltpu.SemaphoreType.DMA((devices,)),
            pltpu.SemaphoreType.DMA((devices,)),
        ],
        name="front",
        compiler_params=pltpu.CompilerParams(
            collective_id=0, has_side_effects=True, vmem_limit_bytes=57 * 2**20
        ),
        cost_estimate=pl.CostEstimate(flops=10**9, bytes_accessed=2**21, transcendentals=0),
    )(shifts, tile, piece_ids, coarse_ids)


def phase(cos_a, sin_a, cos_b, sin_b, own, other):
    def spectrum(values):
        left_cos = highest(cos_a, values)
        left_sin = highest(sin_a, values)
        re = highest(left_cos, cos_b) - highest(left_sin, sin_b)
        im = -(highest(left_cos, sin_b) + highest(left_sin, cos_b))
        return (re, im)

    own_re, own_im = spectrum(own)
    other_re, other_im = spectrum(other)
    cross_re = own_re * other_re + own_im * other_im
    cross_im = own_im * other_re - own_re * other_im
    scale = 1.0 / jnp.sqrt(cross_re * cross_re + cross_im * cross_im + 1.0)
    normed_re = cross_re * scale
    normed_im = cross_im * scale
    out = highest(highest(cos_a, normed_re) - highest(sin_a, normed_im), cos_b)
    return out - highest(highest(sin_a, normed_re) + highest(cos_a, normed_im), sin_b)


def exchange_kernel(
    count_y, count_x, length, cap, shift_ref, along_ref, aside_ref, ids_ref, ca_ref, sa_ref, cb_ref, sb_ref, right_ref, left_ref, bottom_ref, top_ref,
    joined_ref, coarse_ref, corr_right_ref, corr_below_ref,
    rx_ref, rx_edge_ref, pack_ref, piece_ref, send_ref, recv_ref, targets_ref, rank_ref, turn_ref, reduce_ref, inv_ref, dense_ref, zsend_ref, zrecv_ref,
    sum_ref, regroup_ref, quads_ref, all_quads_ref, plane_send, plane_recv, line_send, line_recv, row_send, row_recv,
):
    ny = count_x // NZ
    plane = count_y * ny
    devices = count_y * count_x
    sums = NZ * SLOTS
    grid = length // SIDE
    ty, tx = lax.axis_index("ty"), lax.axis_index("tx")
    me = ty * count_x + tx
    y, z = tx % ny, tx // ny
    mine = ty * ny + y
    near = z + 1 - 2 * (z % 2)
    cross, diag = NZ - 1 - z, NZ - 1 - near
    mid = ((z + 1) // 2) % 2
    barrier = pltpu.get_barrier_semaphore()

    def in_plane(p):
        return (p // ny, z * ny + p % ny)

    def in_line(other):
        return (ty, other * ny + y)

    def greet_plane(d, carry):
        pl.semaphore_signal(barrier, inc=1, device_id=in_plane((mine + d) % plane), device_id_type=MESH)
        return carry

    def greet_row(d, carry):
        pl.semaphore_signal(barrier, inc=1, device_id=(ty, (z * ny + d) % count_x), device_id_type=MESH)
        return carry

    lax.fori_loop(1, plane, greet_plane, 0)
    lax.fori_loop(ny, count_x, greet_row, 0)

    def targets_of(device):
        return ids_ref[device][0:1, :]

    def sum_row_of(targets):
        return ((targets // SLOTS) % count_x) // ny * SLOTS + targets % SLOTS

    square = (PIECES, PIECES)
    earlier = mark(iota(square, 0) < iota(square, 1))
    column = column_of(targets_of(me), count_x)
    onehot = (iota((targets_ref.shape[0], PIECES), 0) == column).astype(F32)
    rank = jnp.sum(onehot * mm(onehot.astype(BF16), earlier), axis=0, keepdims=True)
    position = (column * cap).astype(F32) + rank
    listed = mark(iota((plane * cap, PIECES), 0).astype(F32) == position)
    stacked = iota(square, 1)
    stacked = mark(iota(square, 0) == (stacked % grid) * grid + stacked // grid)
    pack_ref[...] = mm(listed, stacked).astype(BF16)

    sx = split_shift(shift_ref[1])
    full, wide = (length, length), (2 * EDGE, length)
    rx_ref[...] = taps(sx, iota(full, 1), iota(full, 0) + H)
    rx_edge_ref[...] = taps(sx, iota(wide, 1), edge_index(iota(wide, 0), length))
    rows = along_ref.shape[1]
    depth = rows // (length // CHUNKS)
    ramp_x = ramp_at(iota((1, length), 1), length)

    pl.semaphore_wait(barrier, plane - 1 + count_x - ny)

    def rows_of(p):
        return pl.ds(pl.multiple_of(p * cap, cap), cap)

    def plane_copy(c, source, target, peer):
        part = pl.ds(c * PER, PER)
        return pltpu.make_async_remote_copy(
            src_ref=send_ref.at[part, rows_of(source), :],
            dst_ref=recv_ref.at[part, rows_of(target), :],
            send_sem=plane_send.at[c, source],
            recv_sem=plane_recv.at[c, target],
            device_id=in_plane(peer),
            device_id_type=MESH,
        )

    def pack(c):
        work = mm(along_ref[c], rx_ref[...]) + mm(aside_ref[c], rx_edge_ref[...])
        part = rows // depth
        at = iota((rows, 1), 0) % part + c * part
        work = work * (ramp_at(turned_row(at, grid), length) * ramp_x)
        for q in range(length // LANES):
            parts = [work[d * part : (d + 1) * part, q * LANES : (q + 1) * LANES] for d in range(depth)]
            for g, piece in enumerate(swap_groups(parts)):
                into = slice((q * GROUPS + g) * grid, (q * GROUPS + g + 1) * grid)
                for r in range(2 * PER):
                    value = piece[r * grid : (r + 1) * grid].astype(BF16)
                    piece_ref[r // 2, into, (r % 2) * LANES : (r % 2 + 1) * LANES] = value
        for j in range(PER):
            send_ref[c * PER + j] = mm(pack_ref[...], piece_ref[j]).astype(BF16)

        def start(d, inner):
            peer = (mine + d) % plane
            plane_copy(c, peer, mine, peer).start()
            return inner

        lax.fori_loop(1, plane, start, 0)
        for j in range(PER):
            i = c * PER + j
            recv_ref[i, rows_of(mine), :] = send_ref[i, rows_of(mine), :]

    def ahead(c, carry):
        pack(c)
        return carry

    lax.fori_loop(0, AHEAD, ahead, 0)

    targets_ref[...] = jnp.full(targets_ref.shape, -1, jnp.int32)

    def fetch(p, carry):
        targets_ref[pl.ds(p, 1), :] = targets_of((p // ny) * count_x + z * ny + p % ny)
        return carry

    lax.fori_loop(0, plane, fetch, 0)
    rank_ref[...] = mm(mark(column_of(targets_ref[...], count_x) == mine), earlier)

    def turn(p, carry):
        targets = targets_ref[pl.ds(p, 1), :]
        into = jnp.where(column_of(targets, count_x) == mine, sum_row_of(targets), -1)
        into = mark(iota((sums, PIECES), 0) == into)
        listed = mark(iota((cap, PIECES), 0).astype(F32) == rank_ref[pl.ds(p, 1), :])
        turn_ref[rows_of(p), :] = mm_t(listed, into).astype(BF16)
        return carry

    lax.fori_loop(0, plane, turn, 0)
    reduce_ref[...] = mm_t(mark(iota((sums, sums), 0) == iota((sums, sums), 1)), turn_ref[...]).astype(BF16)

    def line_copy(c, kind):
        part = pl.ds(c * PER, PER)
        unit, slot, peer = (
            (near, 0, near),
            (diag, 1, diag),
            (cross, 3 - mid, mid * cross + (1 - mid) * near),
        )[kind]
        return pltpu.make_async_remote_copy(
            src_ref=zsend_ref.at[part, pl.ds(pl.multiple_of(unit * SLOTS, SLOTS), SLOTS), :],
            dst_ref=zrecv_ref.at[slot, part],
            send_sem=line_send.at[c, kind],
            recv_sem=line_recv.at[c, slot],
            device_id=in_line(peer),
            device_id_type=MESH,
        )

    def line_arrived(c, slot):
        part = pl.ds(c * PER, PER)
        pltpu.make_async_remote_copy(
            src_ref=zsend_ref.at[part, pl.ds(0, SLOTS), :],
            dst_ref=zrecv_ref.at[slot, part],
            send_sem=line_send.at[c, 0],
            recv_sem=line_recv.at[c, slot],
            device_id=in_line(near),
            device_id_type=MESH,
        ).wait_recv()

    def unit_rows(unit):
        return pl.ds(pl.multiple_of(unit * SLOTS, SLOTS), SLOTS)

    def reduce(c):
        def arrived(d, carry):
            peer = (mine + d) % plane
            plane_copy(c, peer, peer, peer).wait_recv()
            return carry

        lax.fori_loop(1, plane, arrived, 0)
        for j in range(PER):
            i = c * PER + j
            value = mm(reduce_ref[...], recv_ref[i])
            dense_ref[i] = value
            zsend_ref[i] = value.astype(BF16)
        line_copy(c, 2).start()
        line_copy(c, 0).start()

        @pl.when(mid == 0)
        def _():
            line_copy(c, 1).start()

    def merge(c):
        @pl.when(mid == 1)
        def _():
            line_arrived(c, 3)
            for j in range(PER):
                i = c * PER + j
                value = dense_ref[i, unit_rows(diag), :] + zrecv_ref[3, i].astype(F32)
                zsend_ref[i, unit_rows(diag), :] = value.astype(BF16)
            line_copy(c, 1).start()

    def denominators():
        slot = iota((SLOTS, PIECES), 0) + me * SLOTS

        def count(device, counts):
            return counts + (targets_of(device) == slot).astype(F32)

        counts = lax.fori_loop(0, devices, count, jnp.zeros((SLOTS, PIECES), F32)).astype(BF16)
        place = iota((PIECES, WIDE), 0)
        lane = iota((PIECES, WIDE), 1)
        across = ramp_at(place % grid * SIDE + lane % SIDE, length)
        down = place // grid * SIDE + lane // LANES

        def weigh(i, carry):
            patch = (ramp_at(down + 2 * i, length) * across).astype(BF16)
            inv_ref[i] = 1.0 / jnp.maximum(mm(counts, patch), 1.0)
            return carry

        lax.fori_loop(0, PAIRS, weigh, 0)

    def surfaces():
        tables = (ca_ref[...], sa_ref[...], cb_ref[...], sb_ref[...])
        bins = corr_right_ref.shape[0]
        corr_right_ref[...] = phase(*tables, right_ref[...], left_ref[...])[:bins]
        corr_below_ref[...] = phase(*tables, bottom_ref[...], top_ref[...])[:bins]

    inner = iota((WIDE, LANES), 0)
    outer = iota((WIDE, LANES), 1)
    pooled = inner % LANES // (2 * SIDE) * (SIDE // 2) + inner % SIDE // 2

    def final(c):
        line_arrived(c, 0)
        line_arrived(c, 1)

        @pl.when(mid == 1)
        def _():
            line_arrived(c, 2)
            for j in range(PER):
                i = c * PER + j
                dense_ref[i, unit_rows(z), :] = dense_ref[i, unit_rows(z), :] + zrecv_ref[2, i].astype(F32)

        level = jnp.zeros((SLOTS, LANES), F32)
        rows = []
        for j in range(PER):
            i = c * PER + j
            value = dense_ref[i, unit_rows(z), :] + zrecv_ref[0, i].astype(F32) + zrecv_ref[1, i].astype(F32)
            value = (value * inv_ref[i]).astype(BF16)
            level += mm(value, mark(outer == pooled + j * SIDE))
            value = value.astype(F32)
            rows += [value[:, :LANES], value[:, LANES:]]
        for s, part in enumerate(swap_groups(rows)):
            joined_ref[:, pl.ds(pl.multiple_of(s * SIDE * SIDE + c * LANES, LANES), LANES)] = part.astype(BF16)
        a, b = iota((LANES, LANES), 0), iota((LANES, LANES), 1)
        into = c * (SIDE // 4) + a % (SIDE // 2) // 2
        sum_ref[...] += mm((level * 0.125).astype(BF16), mark((a < PER * SIDE) & (b == into)))

    def regroup():
        u = iota((SLOTS, LANES), 0)
        wanted = tx * SLOTS + 4 * (u % (SLOTS // 4)) + u // (SLOTS // 4)
        for q in range(count_x // 2):
            pair = [ids_ref[ty * count_x + 2 * q + j][1:2, :LANES] for j in range(2)]
            named = jnp.where(iota((1, LANES), 1) < SLOTS, pair[0], pltpu.roll(pair[1], SLOTS, 1))
            regroup_ref[:, q * LANES : (q + 1) * LANES] = mark(named == wanted)

    sum_ref[...] = jnp.zeros_like(sum_ref)

    def step(c, carry):
        @pl.when(c + AHEAD < CHUNKS)
        def _():
            pack(c + AHEAD)

        @pl.when(c < CHUNKS)
        def _():
            reduce(c)

        pl.when(c == 1)(denominators)
        pl.when(c == CHUNKS - AHEAD)(surfaces)
        pl.when(c == CHUNKS - AHEAD + 1)(regroup)

        @pl.when((c >= 1) & (c <= CHUNKS))
        def _():
            merge(c - 1)

        @pl.when(c >= 2)
        def _():
            final(c - 2)

        return carry

    lax.fori_loop(0, CHUNKS + 2, step, 0)
    quads_ref[...] = (sum_ref[...] * 0.125).astype(BF16)

    def row_copy(source, target, peer):
        return pltpu.make_async_remote_copy(
            src_ref=quads_ref,
            dst_ref=all_quads_ref.at[target],
            send_sem=row_send.at[source],
            recv_sem=row_recv.at[target],
            device_id=(ty, peer),
            device_id_type=MESH,
        )

    def start_row(d, carry):
        peer = (tx + d) % count_x
        row_copy(peer, tx, peer).start()
        return carry

    lax.fori_loop(1, count_x, start_row, 0)
    all_quads_ref[tx] = quads_ref[...]

    def sent(c, carry):
        def one(d, inner):
            peer = (mine + d) % plane
            plane_copy(c, peer, peer, peer).wait_send()
            return inner

        for kind in range(3):
            line_copy(c, kind).wait_send()
        return lax.fori_loop(1, plane, one, carry)

    lax.fori_loop(0, CHUNKS, sent, 0)

    def finish_row(d, carry):
        peer = (tx + d) % count_x
        copy = row_copy(peer, peer, peer)
        copy.wait_send()
        copy.wait_recv()
        return carry

    lax.fori_loop(1, count_x, finish_row, 0)

    placed = mm(regroup_ref[...], all_quads_ref[...].reshape(count_x * SLOTS, LANES)).astype(BF16)
    side = SIDE // 4
    a, b = iota((LANES, WIDE), 0), iota((LANES, WIDE), 1)
    out = jnp.zeros((SLOTS // 4, WIDE), F32)
    for q in range(4):
        into = (q // 2) * 2 * side * side + a // side * 2 * side + (q % 2) * side + a % side
        out += mm(placed[q * (SLOTS // 4) : (q + 1) * (SLOTS // 4)], mark((a < side * side) & (b == into)))
    coarse_ref[...] = out.astype(BF16)


def dft_tables(length, padded):
    index = np.arange(length)
    angle = (index[:, None] * index[None, :] % length) * (2.0 * math.pi / length)
    pad = ((0, padded - length),) * 2
    return tuple(
        jnp.asarray(np.pad(table / math.sqrt(length), pad).astype(np.float32)) for table in (np.cos(angle), np.sin(angle))
    )


def exchange(shifts, along, aside, ids, *bins, cap, count_y, count_x, collective_id):
    length = along.shape[2]
    plane = count_y * (count_x // NZ)
    sums = NZ * SLOTS
    vmem = pl.BlockSpec(memory_space=pltpu.VMEM)
    tables = dft_tables(OV // 4, EDGE) + dft_tables(length // 4, length // 4)
    corr = jax.ShapeDtypeStruct((OV // 4, length // 4), F32)
    return pl.pallas_call(
        functools.partial(exchange_kernel, count_y, count_x, length, cap),
        out_shape=[
            jax.ShapeDtypeStruct((SLOTS, SIDE * LANES), BF16),
            jax.ShapeDtypeStruct((SLOTS // 4, WIDE), BF16),
            corr,
            corr,
        ],
        in_specs=[pl.BlockSpec(memory_space=pltpu.SMEM)] + [vmem] * 11,
        out_specs=[vmem] * 4,
        scratch_shapes=[
            pltpu.VMEM((length, length), BF16),
            pltpu.VMEM((2 * EDGE, length), BF16),
            pltpu.VMEM((plane * cap, PIECES), BF16),
            pltpu.VMEM((PER, PIECES, WIDE), BF16),
            pltpu.VMEM((PAIRS, plane * cap, WIDE), BF16),
            pltpu.VMEM((PAIRS, plane * cap, WIDE), BF16),
            pltpu.VMEM((max(16, plane), PIECES), jnp.int32),
            pltpu.VMEM((max(16, plane), PIECES), F32),
            pltpu.VMEM((plane * cap, sums), BF16),
            pltpu.VMEM((sums, plane * cap), BF16),
            pltpu.VMEM((PAIRS, SLOTS, WIDE), F32),
            pltpu.VMEM((PAIRS, sums, WIDE), F32),
            pltpu.VMEM((PAIRS, sums, WIDE), BF16),
            pltpu.VMEM((4, PAIRS, SLOTS, WIDE), BF16),
            pltpu.VMEM((SLOTS, LANES), F32),
            pltpu.VMEM((SLOTS, count_x * SLOTS), BF16),
            pltpu.VMEM((SLOTS, LANES), BF16),
            pltpu.VMEM((count_x, SLOTS, LANES), BF16),
            pltpu.SemaphoreType.DMA((CHUNKS, plane)),
            pltpu.SemaphoreType.DMA((CHUNKS, plane)),
            pltpu.SemaphoreType.DMA((CHUNKS, 3)),
            pltpu.SemaphoreType.DMA((CHUNKS, 4)),
            pltpu.SemaphoreType.DMA((count_x,)),
            pltpu.SemaphoreType.DMA((count_x,)),
        ],
        name="exchange",
        compiler_params=pltpu.CompilerParams(
            collective_id=collective_id, has_side_effects=True, vmem_limit_bytes=44 * 2**20
        ),
        cost_estimate=pl.CostEstimate(flops=3 * 10**9, bytes_accessed=2**23, transcendentals=0),
    )(shifts, along, aside, ids, *tables, *bins)


def finish_kernel(*refs):
    count = len(refs) // 2
    sems = refs[-1]
    copies = [pltpu.make_async_copy(refs[i], refs[count + i], sems.at[i]) for i in range(count)]
    for copy in copies:
        copy.start()
    for copy in copies:
        copy.wait()


def finish(*results):
    hbm = pl.BlockSpec(memory_space=pltpu.HBM)
    return pl.pallas_call(
        finish_kernel,
        out_shape=[jax.ShapeDtypeStruct(r.shape, r.dtype) for r in results],
        in_specs=[pl.BlockSpec(memory_space=pltpu.VMEM)] * len(results),
        out_specs=[hbm] * len(results),
        scratch_shapes=[pltpu.SemaphoreType.DMA((len(results),))],
        name="finish",
    )(*results)


def per_device(tiles, shifts, piece_target, coarse_target):
    tile = tiles[0, 0]
    count_y = lax.axis_size("ty")
    count_x = lax.axis_size("tx")
    cap = NZ * 2 * PIECES // (count_y * count_x)
    along, aside, *bins, ids, most = front(shifts[0, 0], tile, piece_target[0], coarse_target[0], count_y, count_x)
    run = functools.partial(exchange, shifts[0, 0], along, aside, ids, *bins, count_y=count_y, count_x=count_x)
    fewer = cap * 3 // 4
    if fewer % 16:
        return tuple(finish(*run(cap=cap, collective_id=1)))
    results = lax.cond(
        most[0, 0] <= fewer,
        lambda: tuple(run(cap=fewer, collective_id=1)),
        lambda: tuple(run(cap=cap, collective_id=2)),
    )
    return tuple(finish(*results))


def solution(mesh):
    placed = (
        P("ty", "tx", None, None, None),
        P("ty", "tx", None),
        P("ty", "tx", None),
        P("ty", "tx", None),
    )
    return jax.shard_map(
        per_device,
        mesh=mesh,
        in_specs=placed,
        out_specs=(P(("ty", "tx"), None), P(("ty", "tx"), None), P("ty", "tx"), P("ty", "tx")),
        check_vma=False,
    )
```

```python
import functools
import math

import jax
import jax.numpy as jnp
import numpy as np
from jax import lax
from jax.experimental import pallas as pl
from jax.experimental.pallas import tpu as pltpu
from jax.sharding import PartitionSpec as P

SIDE = 32
OV = 48
H = 8
SLOTS = 64
LANES = 128
GROUPS = LANES // SIDE
EDGE = 2 * H
NZ = 4
PIECES = 256
PAIRS = SIDE // 2
WIDE = 2 * LANES
CHUNKS = 8
AHEAD = 3
PER = PAIRS // CHUNKS
F32 = jnp.float32
BF16 = jnp.bfloat16
MESH = pl.DeviceIdType.MESH
DIRECTIONS = ((1, 0), (-1, 0), (0, 1), (0, -1), (1, 1), (1, -1), (-1, 1), (-1, -1))


def highest(left, right):
    return jnp.dot(left, right, precision=lax.Precision.HIGHEST, preferred_element_type=F32)


def iota(shape, dim):
    return lax.broadcasted_iota(jnp.int32, shape, dim)


def mm(a, b):
    return jnp.dot(a, b, preferred_element_type=F32)


def mm_t(a, b):
    return lax.dot_general(a, b, (((1,), (1,)), ((), ())), preferred_element_type=F32)


def mark(condition):
    return condition.astype(F32).astype(BF16)


def swap_groups(parts):
    group = iota(parts[0].shape, 1) // SIDE

    def pick(choices):
        value = choices[3]
        for g in range(3):
            value = jnp.where(group == g, choices[g], value)
        return value

    turned = []
    for d in range(GROUPS):
        mixed = pick([parts[(g + d) % GROUPS] for g in range(GROUPS)])
        turned.append(pltpu.roll(mixed, d * SIDE, 1) if d else mixed)
    return [pick([turned[(j - g) % GROUPS] for j in range(GROUPS)]) for g in range(GROUPS)]


def taps(offset, out, column):
    whole, frac = offset
    at = out + whole + H
    return (
        jnp.where(column == at, 1.0 - frac, 0.0) + jnp.where(column == at + 1, frac, 0.0)
    ).astype(BF16)


def split_shift(shift):
    whole = lax.shift_right_arithmetic(shift, 2)
    return whole, (shift - 4 * whole).astype(F32) * 0.25


def ramp_at(index, length):
    nearest = jnp.minimum(jnp.minimum(index + 1, length - index), OV).astype(F32)
    return 1.0 + nearest * (3.0 / OV)


def turned_row(at, grid):
    return (at % grid) * SIDE + at // grid


def edge_index(c, length):
    return c % H + jnp.where(c < EDGE, 0, length + H)


def column_of(targets, count_x):
    owner = targets // SLOTS
    return (owner // count_x) * (count_x // NZ) + owner % (count_x // NZ)


def front_kernel(
    count_y, count_x, shift_ref, tile_hbm, piece_ids_hbm, coarse_ids_hbm,
    along_ref, tb_ref, side_ref, ct_ref, cb_ref, sums_ref, all_ids_ref, most_ref,
    tile_ref, piece_ids_ref, coarse_ids_ref, ids_ref, ids_rows_ref, strips_ref, ends_ref,
    tile_sem, halo_send, halo_recv, id_send, id_recv,
):
    depth, length, _ = tile_ref.shape
    grid = length // SIDE
    devices = count_y * count_x
    ty, tx = lax.axis_index("ty"), lax.axis_index("tx")
    me = ty * count_x + tx
    barrier = pltpu.get_barrier_semaphore()
    load = pltpu.make_async_copy(tile_hbm, tile_ref, tile_sem.at[0])
    load.start()
    loads = (
        pltpu.make_async_copy(piece_ids_hbm, piece_ids_ref, tile_sem.at[1]),
        pltpu.make_async_copy(coarse_ids_hbm, coarse_ids_ref, tile_sem.at[2]),
    )
    for copy in loads:
        copy.start()

    def at(peer):
        return (peer // count_x, peer % count_x)

    def greet(d, carry):
        pl.semaphore_signal(barrier, inc=1, device_id=at((me + d) % devices), device_id_type=MESH)
        return carry

    lax.fori_loop(1, devices, greet, 0)

    def there(dy, dx):
        y, x = ty + dy, tx + dx
        return (y >= 0) & (y < count_y) & (x >= 0) & (x < count_x)

    low, high = pl.ds(0, EDGE), pl.ds(EDGE, EDGE)

    def landing(dy, dx):
        if dx == 0:
            return tb_ref.at[:, low if dy == 1 else high, :]
        half = low if dx == 1 else high
        if dy == 0:
            return side_ref.at[:, half, :]
        return (ct_ref if dy == 1 else cb_ref).at[:, half, :]

    def halo(i):
        dy, dx = DIRECTIONS[i]
        if dx == 0:
            source = ends_ref.at[:, high if dy == 1 else low, :]
        else:
            half = high if dx == 1 else low
            if dy == 0:
                source = strips_ref.at[:, half, :]
            else:
                source = strips_ref.at[:, half, pl.ds(length - LANES if dy == 1 else 0, LANES)]
        return pltpu.make_async_remote_copy(
            src_ref=source,
            dst_ref=landing(dy, dx),
            send_sem=halo_send.at[i],
            recv_sem=halo_recv.at[i],
            device_id=(ty + dy, tx + dx),
            device_id_type=MESH,
        )

    for dy, dx in DIRECTIONS:

        @pl.when(jnp.logical_not(there(-dy, -dx)))
        def _():
            ref = landing(dy, dx)
            ref[...] = jnp.zeros(ref.shape, ref.dtype)

    for copy in loads:
        copy.wait()
    ids_ref[...] = jnp.full(ids_ref.shape, -1, jnp.int32)
    ids_ref[0:1, :] = piece_ids_ref[...]
    ids_ref[1:2, :SLOTS] = coarse_ids_ref[...]

    row, lane = iota((2 * EDGE, LANES), 0), iota((2 * EDGE, LANES), 1)
    back = lane - (LANES - OV)
    first_bins = (row >= EDGE) & (lane < OV) & (lane // 4 == row - EDGE)
    last_bins = (row >= EDGE) & (back >= 0) & (back // 4 == row - EDGE)

    def picks(z):
        own = (row < EDGE) & (row // H == z % 2)
        first = mark((own & (lane == row % H)) | first_bins)
        return first, mark((own & (lane - (LANES - H) == row % H)) | last_bins)

    load.wait()
    left = right = jnp.zeros((EDGE, length), F32)
    for k in range(depth // 2):
        lows = highs = jnp.zeros((2 * EDGE, length), F32)
        for z in (2 * k, 2 * k + 1):
            first, last = picks(z)
            lows += mm_t(first, tile_ref[z, :, :LANES])
            highs += mm_t(last, tile_ref[z, :, length - LANES :])
        left += lows[EDGE:]
        right += highs[EDGE:]
        strips_ref[k, :EDGE, :] = lows[:EDGE].astype(BF16)
        strips_ref[k, EDGE:, :] = highs[:EDGE].astype(BF16)
        pair = (2 * k, 2 * k + 1)
        ends = [tile_ref[z, :EDGE, :].astype(F32)[:H] for z in pair]
        ends += [tile_ref[z, length - EDGE :, :].astype(F32)[H:] for z in pair]
        ends_ref[k] = jnp.concatenate(ends).astype(BF16)
    first, last = picks(0)

    pl.semaphore_wait(barrier, devices - 1)
    for i, (dy, dx) in enumerate(DIRECTIONS):

        @pl.when(there(dy, dx))
        def _():
            halo(i).start()

    def ids(peer):
        return pltpu.make_async_remote_copy(
            src_ref=ids_ref,
            dst_ref=all_ids_ref.at[me],
            send_sem=id_send.at[peer],
            recv_sem=id_recv.at[0],
            device_id=at(peer),
            device_id_type=MESH,
        )

    def start(d, carry):
        ids((me + d) % devices).start()
        return carry

    lax.fori_loop(1, devices, start, 0)
    all_ids_ref[me] = ids_ref[...]

    sy = split_shift(shift_ref[0])
    full = (length, length)
    ry = taps(sy, turned_row(iota(full, 0), grid), iota(full, 1) + H)
    part = length // CHUNKS
    for z in range(depth):
        along = mm(ry, tile_ref[z])
        for c in range(CHUNKS):
            along_ref[c, z * part : (z + 1) * part, :] = along[c * part : (c + 1) * part]

    top = bottom = jnp.zeros((EDGE, length), F32)
    for z in range(depth):
        top += mm(first[EDGE:], tile_ref[z, :LANES, :])
        bottom += mm(last[EDGE:], tile_ref[z, length - LANES :, :])
    sums_ref[...] = jnp.concatenate([left, top, right, bottom])

    others = pl.ds(0, devices - 1)
    pltpu.make_async_remote_copy(
        src_ref=all_ids_ref.at[others],
        dst_ref=all_ids_ref.at[others],
        send_sem=id_send.at[me],
        recv_sem=id_recv.at[0],
        device_id=at(me),
        device_id_type=MESH,
    ).wait_recv()

    def gather(d, carry):
        ids_rows_ref[pl.ds(d, 1), :] = all_ids_ref[d][0:1, :]
        return carry

    lax.fori_loop(0, devices, gather, 0)
    columns = column_of(ids_rows_ref[...], count_x)
    ones = jnp.ones((PIECES, LANES), BF16)
    most = jnp.zeros((devices, LANES), F32)
    for p in range(count_y * (count_x // NZ)):
        most = jnp.maximum(most, mm(mark(columns == p), ones))
    most_ref[0, 0] = jnp.max(most).astype(jnp.int32)

    for i, (dy, dx) in enumerate(DIRECTIONS):

        @pl.when(there(-dy, -dx))
        def _():
            halo(i).wait_recv()

    for i, (dy, dx) in enumerate(DIRECTIONS):

        @pl.when(there(dy, dx))
        def _():
            halo(i).wait_send()

    def finish(d, carry):
        ids((me + d) % devices).wait_send()
        return carry

    lax.fori_loop(1, devices, finish, 0)


def front(shifts, tile, piece_ids, coarse_ids, count_y, count_x):
    depth, length, _ = tile.shape
    devices = count_y * count_x
    vmem = pl.BlockSpec(memory_space=pltpu.VMEM)
    smem = pl.BlockSpec(memory_space=pltpu.SMEM)
    strip = jax.ShapeDtypeStruct((depth // 2, 2 * EDGE, length), BF16)
    corner = jax.ShapeDtypeStruct((depth // 2, 2 * EDGE, LANES), BF16)
    return pl.pallas_call(
        functools.partial(front_kernel, count_y, count_x),
        out_shape=[
            jax.ShapeDtypeStruct((CHUNKS, depth * length // CHUNKS, length), F32),
            strip, strip, corner, corner,
            jax.ShapeDtypeStruct((4 * EDGE, length), F32),
            jax.ShapeDtypeStruct((devices, 2, PIECES), jnp.int32),
            jax.ShapeDtypeStruct((1, 1), jnp.int32),
        ],
        in_specs=[smem] + [pl.BlockSpec(memory_space=pltpu.HBM)] * 3,
        out_specs=[vmem] * 7 + [smem],
        scratch_shapes=[
            pltpu.VMEM(tile.shape, BF16),
            pltpu.VMEM((1, PIECES), jnp.int32),
            pltpu.VMEM((1, SLOTS), jnp.int32),
            pltpu.VMEM((2, PIECES), jnp.int32),
            pltpu.VMEM((devices, PIECES), jnp.int32),
            pltpu.VMEM((depth // 2, 2 * EDGE, length), BF16),
            pltpu.VMEM((depth // 2, 2 * EDGE, length), BF16),
            pltpu.SemaphoreType.DMA((3,)),
            pltpu.SemaphoreType.DMA((8,)),
            pltpu.SemaphoreType.DMA((8,)),
            pltpu.SemaphoreType.DMA((devices,)),
            pltpu.SemaphoreType.DMA((1,)),
        ],
        name="front",
        compiler_params=pltpu.CompilerParams(
            collective_id=0, has_side_effects=True, vmem_limit_bytes=55 * 2**20
        ),
        cost_estimate=pl.CostEstimate(flops=10**9, bytes_accessed=2**21, transcendentals=0),
    )(shifts, tile, piece_ids, coarse_ids)


def phase(cos_a, sin_a, cos_b, sin_b, own, other):
    def spectrum(values):
        left_cos = highest(cos_a, values)
        left_sin = highest(sin_a, values)
        re = highest(left_cos, cos_b) - highest(left_sin, sin_b)
        im = -(highest(left_cos, sin_b) + highest(left_sin, cos_b))
        return (re, im)

    own_re, own_im = spectrum(own)
    other_re, other_im = spectrum(other)
    cross_re = own_re * other_re + own_im * other_im
    cross_im = own_im * other_re - own_re * other_im
    scale = 1.0 / jnp.sqrt(cross_re * cross_re + cross_im * cross_im + 1.0)
    normed_re = cross_re * scale
    normed_im = cross_im * scale
    out = highest(highest(cos_a, normed_re) - highest(sin_a, normed_im), cos_b)
    return out - highest(highest(sin_a, normed_re) + highest(cos_a, normed_im), sin_b)


def exchange_kernel(
    count_y, count_x, length, cap, shift_ref, along_ref, tb_ref, side_ref, above_ref, below_ref, sums_ref, ids_ref,
    ca_ref, sa_ref, cb_ref, sb_ref,
    joined_ref, coarse_ref, corr_right_ref, corr_below_ref,
    rx_ref, rx_edge_ref, pack_ref, piece_ref, send_ref, recv_ref, targets_ref, rank_ref, turn_ref, reduce_ref, inv_ref, dense_ref, zsend_ref, zrecv_ref,
    sum_ref, regroup_ref, quads_ref, all_quads_ref,
    bins_ref, next_ref, bin_send, bin_recv, plane_send, plane_recv, line_send, line_recv, row_send, row_recv,
):
    ny = count_x // NZ
    plane = count_y * ny
    devices = count_y * count_x
    sums = NZ * SLOTS
    grid = length // SIDE
    ty, tx = lax.axis_index("ty"), lax.axis_index("tx")
    me = ty * count_x + tx
    y, z = tx % ny, tx // ny
    mine = ty * ny + y
    near = z + 1 - 2 * (z % 2)
    cross, diag = NZ - 1 - z, NZ - 1 - near
    mid = ((z + 1) // 2) % 2
    barrier = pltpu.get_barrier_semaphore()

    def in_plane(p):
        return (p // ny, z * ny + p % ny)

    def in_line(other):
        return (ty, other * ny + y)

    def greet_plane(d, carry):
        pl.semaphore_signal(barrier, inc=1, device_id=in_plane((mine + d) % plane), device_id_type=MESH)
        return carry

    def greet_row(d, carry):
        pl.semaphore_signal(barrier, inc=1, device_id=(ty, (z * ny + d) % count_x), device_id_type=MESH)
        return carry

    lax.fori_loop(1, plane, greet_plane, 0)
    lax.fori_loop(ny, count_x, greet_row, 0)

    def targets_of(device):
        return ids_ref[device][0:1, :]

    def sum_row_of(targets):
        return ((targets // SLOTS) % count_x) // ny * SLOTS + targets % SLOTS

    square = (PIECES, PIECES)
    earlier = mark(iota(square, 0) < iota(square, 1))
    column = column_of(targets_of(me), count_x)
    onehot = (iota((targets_ref.shape[0], PIECES), 0) == column).astype(F32)
    rank = jnp.sum(onehot * mm(onehot.astype(BF16), earlier), axis=0, keepdims=True)
    position = (column * cap).astype(F32) + rank
    listed = mark(iota((plane * cap, PIECES), 0).astype(F32) == position)
    stacked = iota(square, 1)
    stacked = mark(iota(square, 0) == (stacked % grid) * grid + stacked // grid)
    pack_ref[...] = mm(listed, stacked).astype(BF16)

    sx = split_shift(shift_ref[1])
    rows = along_ref.shape[1]
    part = length // CHUNKS
    depth = rows // part
    edges = depth // 2 * 2 * EDGE
    full, wide = (length, length), (edges, length)
    rx_ref[...] = taps(sx, iota(full, 1), iota(full, 0) + H)
    rx_edge_ref[...] = taps(sx, iota(wide, 1), edge_index(iota(wide, 0) % (2 * EDGE), length))
    sy = split_shift(shift_ref[0])
    side = side_ref[...].reshape(edges, length)
    tb = tb_ref[...].reshape(edges, length)
    above = above_ref[...].reshape(edges, LANES)
    below = below_ref[...].reshape(edges, LANES)

    def slice_of(c):
        return c // (2 * EDGE) * 2 + c // H % 2

    ramp_x = ramp_at(iota((1, length), 1), length)

    pl.semaphore_wait(barrier, plane - 1 + count_x - ny)

    def rows_of(p):
        return pl.ds(pl.multiple_of(p * cap, cap), cap)

    def plane_copy(i, peer):
        return pltpu.make_async_remote_copy(
            src_ref=send_ref.at[i, rows_of(peer), :],
            dst_ref=recv_ref.at[i, rows_of(mine), :],
            send_sem=plane_send.at[0],
            recv_sem=plane_recv.at[i],
            device_id=in_plane(peer),
            device_id_type=MESH,
        )

    def pack(c):
        def of(shape, column):
            return taps(sy, turned_row(iota(shape, 0) % part + c * part, grid), column)

        lane = iota((rows, edges), 1)
        mine_only = slice_of(lane) == iota((rows, edges), 0) // part
        ends = of((rows, edges), jnp.where(mine_only, edge_index(lane % (2 * EDGE), length), -1))
        along = (along_ref[c] + mm(ends, tb)).astype(BF16)
        aside = (
            mm_t(of((part, length), iota((part, length), 1) + H), side)
            + mm_t(of((part, LANES), iota((part, LANES), 1) + (H - LANES)), above)
            + mm_t(of((part, LANES), iota((part, LANES), 1) + (length + H)), below)
        )
        aside = jnp.where(mine_only, jnp.concatenate([aside] * depth), 0.0).astype(BF16)
        work = mm(along, rx_ref[...]) + mm(aside, rx_edge_ref[...])
        at = iota((rows, 1), 0) % part + c * part
        work = work * (ramp_at(turned_row(at, grid), length) * ramp_x)
        for q in range(length // LANES):
            parts = [work[d * part : (d + 1) * part, q * LANES : (q + 1) * LANES] for d in range(depth)]
            for g, piece in enumerate(swap_groups(parts)):
                into = slice((q * GROUPS + g) * grid, (q * GROUPS + g + 1) * grid)
                for r in range(2 * PER):
                    value = piece[r * grid : (r + 1) * grid].astype(BF16)
                    piece_ref[r // 2, into, (r % 2) * LANES : (r % 2 + 1) * LANES] = value
        for j in range(PER):
            i = c * PER + j
            send_ref[i] = mm(pack_ref[...], piece_ref[j]).astype(BF16)

            def start(d, inner):
                plane_copy(i, (mine + d) % plane).start()
                return inner

            lax.fori_loop(1, plane, start, 0)
            recv_ref[i, rows_of(mine), :] = send_ref[i, rows_of(mine), :]

    def ahead(c, carry):
        pack(c)
        return carry

    lax.fori_loop(0, AHEAD, ahead, 0)

    def bins_copy(i):
        return pltpu.make_async_remote_copy(
            src_ref=bins_ref.at[i],
            dst_ref=next_ref.at[i],
            send_sem=bin_send.at[i],
            recv_sem=bin_recv.at[i],
            device_id=((ty, tx - 1), (ty - 1, tx))[i],
            device_id_type=MESH,
        )

    to_there = (tx > 0, ty > 0)
    from_there = (tx < count_x - 1, ty < count_y - 1)

    def bins():
        pool = (iota((length, length // 4), 0) // 4 == iota((length, length // 4), 1)).astype(F32)
        value = highest(sums_ref[...], pool) * (1.0 / math.sqrt(16.0 * depth))
        for i in range(4):
            bins_ref[i] = value[i * EDGE : (i + 1) * EDGE]
        for i in range(2):

            @pl.when(to_there[i])
            def _():
                bins_copy(i).start()

            @pl.when(jnp.logical_not(from_there[i]))
            def _():
                next_ref[i] = jnp.zeros(next_ref.shape[1:], F32)

    targets_ref[...] = jnp.full(targets_ref.shape, -1, jnp.int32)

    def fetch(p, carry):
        targets_ref[pl.ds(p, 1), :] = targets_of((p // ny) * count_x + z * ny + p % ny)
        return carry

    lax.fori_loop(0, plane, fetch, 0)
    rank_ref[...] = mm(mark(column_of(targets_ref[...], count_x) == mine), earlier)

    def turn(p, carry):
        targets = targets_ref[pl.ds(p, 1), :]
        into = jnp.where(column_of(targets, count_x) == mine, sum_row_of(targets), -1)
        into = mark(iota((sums, PIECES), 0) == into)
        listed = mark(iota((cap, PIECES), 0).astype(F32) == rank_ref[pl.ds(p, 1), :])
        turn_ref[rows_of(p), :] = mm_t(listed, into).astype(BF16)
        return carry

    lax.fori_loop(0, plane, turn, 0)
    reduce_ref[...] = mm_t(mark(iota((sums, sums), 0) == iota((sums, sums), 1)), turn_ref[...]).astype(BF16)

    def unit_rows(unit):
        return pl.ds(pl.multiple_of(unit * SLOTS, SLOTS), SLOTS)

    def line_copy(i, unit, slot, peer):
        return pltpu.make_async_remote_copy(
            src_ref=zsend_ref.at[i, unit_rows(unit), :],
            dst_ref=zrecv_ref.at[slot, i],
            send_sem=line_send.at[0],
            recv_sem=line_recv.at[i, slot],
            device_id=in_line(peer),
            device_id_type=MESH,
        )

    def line_arrived(i, slot):
        line_copy(i, near, slot, near).wait_recv()

    def plane_done(i):
        others = pl.ds(0, (plane - 1) * cap)
        return pltpu.make_async_remote_copy(
            src_ref=send_ref.at[i, others, :],
            dst_ref=recv_ref.at[i, others, :],
            send_sem=plane_send.at[0],
            recv_sem=plane_recv.at[i],
            device_id=in_line(near),
            device_id_type=MESH,
        )

    def reduce(i):
        plane_done(i).wait_recv()
        value = mm(reduce_ref[...], recv_ref[i])
        dense_ref[i] = value
        zsend_ref[i] = value.astype(BF16)
        line_copy(i, cross, 3 - mid, mid * cross + (1 - mid) * near).start()

        @pl.when(mid == 0)
        def _():
            line_copy(i, diag, 1, diag).start()

        line_copy(i, near, 0, near).start()

    def merge(i):
        @pl.when(mid == 1)
        def _():
            line_arrived(i, 3)
            value = dense_ref[i, unit_rows(diag), :] + zrecv_ref[3, i].astype(F32)
            zsend_ref[i, unit_rows(diag), :] = value.astype(BF16)
            line_copy(i, diag, 1, diag).start()

    def denominators():
        slot = iota((SLOTS, PIECES), 0) + me * SLOTS

        def count(device, counts):
            return counts + (targets_of(device) == slot).astype(F32)

        counts = lax.fori_loop(0, devices, count, jnp.zeros((SLOTS, PIECES), F32)).astype(BF16)
        place = iota((PIECES, WIDE), 0)
        lane = iota((PIECES, WIDE), 1)
        across = ramp_at(place % grid * SIDE + lane % SIDE, length)
        down = place // grid * SIDE + lane // LANES

        def weigh(i, carry):
            patch = (ramp_at(down + 2 * i, length) * across).astype(BF16)
            inv_ref[i] = 1.0 / jnp.maximum(mm(counts, patch), 1.0)
            return carry

        lax.fori_loop(0, PAIRS, weigh, 0)

    def surfaces():
        tables = (ca_ref[...], sa_ref[...], cb_ref[...], sb_ref[...])
        for i, ref in enumerate((corr_right_ref, corr_below_ref)):

            @pl.when(from_there[i])
            def _():
                bins_copy(i).wait_recv()

            @pl.when(to_there[i])
            def _():
                bins_copy(i).wait_send()

            ref[...] = phase(*tables, bins_ref[2 + i], next_ref[i])[: ref.shape[0]]

    inner = iota((WIDE, LANES), 0)
    outer = iota((WIDE, LANES), 1)
    pooled = inner % LANES // (2 * SIDE) * (SIDE // 2) + inner % SIDE // 2

    def final(c):
        for j in range(PER):
            i = c * PER + j
            line_arrived(i, 0)
            line_arrived(i, 1)

            @pl.when(mid == 1)
            def _():
                line_arrived(i, 2)
                dense_ref[i, unit_rows(z), :] = dense_ref[i, unit_rows(z), :] + zrecv_ref[2, i].astype(F32)

        level = jnp.zeros((SLOTS, LANES), F32)
        rows = []
        for j in range(PER):
            i = c * PER + j
            value = dense_ref[i, unit_rows(z), :] + zrecv_ref[0, i].astype(F32) + zrecv_ref[1, i].astype(F32)
            value = (value * inv_ref[i]).astype(BF16)
            level += mm(value, mark(outer == pooled + j * SIDE))
            value = value.astype(F32)
            rows += [value[:, :LANES], value[:, LANES:]]
        for s, part in enumerate(swap_groups(rows)):
            joined_ref[:, pl.ds(pl.multiple_of(s * SIDE * SIDE + c * LANES, LANES), LANES)] = part.astype(BF16)
        a, b = iota((LANES, LANES), 0), iota((LANES, LANES), 1)
        into = c * (SIDE // 4) + a % (SIDE // 2) // 2
        sum_ref[...] += mm((level * 0.125).astype(BF16), mark((a < PER * SIDE) & (b == into)))

    def regroup():
        u = iota((SLOTS, LANES), 0)
        wanted = tx * SLOTS + 4 * (u % (SLOTS // 4)) + u // (SLOTS // 4)
        for q in range(count_x // 2):
            pair = [ids_ref[ty * count_x + 2 * q + j][1:2, :LANES] for j in range(2)]
            named = jnp.where(iota((1, LANES), 1) < SLOTS, pair[0], pltpu.roll(pair[1], SLOTS, 1))
            regroup_ref[:, q * LANES : (q + 1) * LANES] = mark(named == wanted)

    sum_ref[...] = jnp.zeros_like(sum_ref)

    def step(c, carry):
        @pl.when(c + AHEAD < CHUNKS)
        def _():
            pack(c + AHEAD)

        @pl.when(c < CHUNKS)
        def _():
            reduce(c * PER)

        @pl.when((c >= 1) & (c <= CHUNKS))
        def _():
            merge(c * PER - 1)

        for j in range(1, PER):

            @pl.when(c < CHUNKS)
            def _():
                reduce(c * PER + j)
                merge(c * PER + j - 1)

        pl.when(c == 0)(bins)
        pl.when(c == 1)(denominators)
        pl.when(c == CHUNKS - AHEAD)(surfaces)
        pl.when(c == CHUNKS - AHEAD + 1)(regroup)

        @pl.when(c >= 2)
        def _():
            final(c - 2)

        return carry

    lax.fori_loop(0, CHUNKS + 2, step, 0)
    quads_ref[...] = (sum_ref[...] * 0.125).astype(BF16)

    def row_copy(source, target, peer):
        return pltpu.make_async_remote_copy(
            src_ref=quads_ref,
            dst_ref=all_quads_ref.at[target],
            send_sem=row_send.at[source],
            recv_sem=row_recv.at[target],
            device_id=(ty, peer),
            device_id_type=MESH,
        )

    def start_row(d, carry):
        peer = (tx + d) % count_x
        row_copy(peer, tx, peer).start()
        return carry

    lax.fori_loop(1, count_x, start_row, 0)
    all_quads_ref[tx] = quads_ref[...]

    pltpu.make_async_remote_copy(
        src_ref=send_ref.at[:, pl.ds(0, (plane - 1) * cap), :],
        dst_ref=send_ref.at[:, pl.ds(0, (plane - 1) * cap), :],
        send_sem=plane_send.at[0],
        recv_sem=plane_recv.at[0],
        device_id=in_line(near),
        device_id_type=MESH,
    ).wait_send()
    pltpu.make_async_remote_copy(
        src_ref=zsend_ref.at[:, pl.ds(0, 3 * SLOTS), :],
        dst_ref=zsend_ref.at[:, pl.ds(0, 3 * SLOTS), :],
        send_sem=line_send.at[0],
        recv_sem=line_recv.at[0, 0],
        device_id=in_line(near),
        device_id_type=MESH,
    ).wait_send()

    def finish_row(d, carry):
        peer = (tx + d) % count_x
        copy = row_copy(peer, peer, peer)
        copy.wait_send()
        copy.wait_recv()
        return carry

    lax.fori_loop(1, count_x, finish_row, 0)

    placed = mm(regroup_ref[...], all_quads_ref[...].reshape(count_x * SLOTS, LANES)).astype(BF16)
    side = SIDE // 4
    a, b = iota((LANES, WIDE), 0), iota((LANES, WIDE), 1)
    out = jnp.zeros((SLOTS // 4, WIDE), F32)
    for q in range(4):
        into = (q // 2) * 2 * side * side + a // side * 2 * side + (q % 2) * side + a % side
        out += mm(placed[q * (SLOTS // 4) : (q + 1) * (SLOTS // 4)], mark((a < side * side) & (b == into)))
    coarse_ref[...] = out.astype(BF16)


def dft_tables(length, padded):
    index = np.arange(length)
    angle = (index[:, None] * index[None, :] % length) * (2.0 * math.pi / length)
    pad = ((0, padded - length),) * 2
    return tuple(
        jnp.asarray(np.pad(table / math.sqrt(length), pad).astype(np.float32)) for table in (np.cos(angle), np.sin(angle))
    )


def exchange(shifts, along, *rest, cap, count_y, count_x, collective_id):
    length = along.shape[2]
    edges = rest[0].shape[0] * 2 * EDGE
    plane = count_y * (count_x // NZ)
    sums = NZ * SLOTS
    vmem = pl.BlockSpec(memory_space=pltpu.VMEM)
    tables = dft_tables(OV // 4, EDGE) + dft_tables(length // 4, length // 4)
    corr = jax.ShapeDtypeStruct((OV // 4, length // 4), F32)
    return pl.pallas_call(
        functools.partial(exchange_kernel, count_y, count_x, length, cap),
        out_shape=[
            jax.ShapeDtypeStruct((SLOTS, SIDE * LANES), BF16),
            jax.ShapeDtypeStruct((SLOTS // 4, WIDE), BF16),
            corr,
            corr,
        ],
        in_specs=[pl.BlockSpec(memory_space=pltpu.SMEM)] + [vmem] * 11,
        out_specs=[vmem] * 4,
        scratch_shapes=[
            pltpu.VMEM((length, length), BF16),
            pltpu.VMEM((edges, length), BF16),
            pltpu.VMEM((plane * cap, PIECES), BF16),
            pltpu.VMEM((PER, PIECES, WIDE), BF16),
            pltpu.VMEM((PAIRS, plane * cap, WIDE), BF16),
            pltpu.VMEM((PAIRS, plane * cap, WIDE), BF16),
            pltpu.VMEM((max(16, plane), PIECES), jnp.int32),
            pltpu.VMEM((max(16, plane), PIECES), F32),
            pltpu.VMEM((plane * cap, sums), BF16),
            pltpu.VMEM((sums, plane * cap), BF16),
            pltpu.VMEM((PAIRS, SLOTS, WIDE), F32),
            pltpu.VMEM((PAIRS, sums, WIDE), F32),
            pltpu.VMEM((PAIRS, sums, WIDE), BF16),
            pltpu.VMEM((4, PAIRS, SLOTS, WIDE), BF16),
            pltpu.VMEM((SLOTS, LANES), F32),
            pltpu.VMEM((SLOTS, count_x * SLOTS), BF16),
            pltpu.VMEM((SLOTS, LANES), BF16),
            pltpu.VMEM((count_x, SLOTS, LANES), BF16),
            pltpu.VMEM((4, EDGE, length // 4), F32),
            pltpu.VMEM((2, EDGE, length // 4), F32),
            pltpu.SemaphoreType.DMA((2,)),
            pltpu.SemaphoreType.DMA((2,)),
            pltpu.SemaphoreType.DMA((1,)),
            pltpu.SemaphoreType.DMA((PAIRS,)),
            pltpu.SemaphoreType.DMA((1,)),
            pltpu.SemaphoreType.DMA((PAIRS, 4)),
            pltpu.SemaphoreType.DMA((count_x,)),
            pltpu.SemaphoreType.DMA((count_x,)),
        ],
        name="exchange",
        compiler_params=pltpu.CompilerParams(
            collective_id=collective_id, has_side_effects=True, vmem_limit_bytes=44 * 2**20
        ),
        cost_estimate=pl.CostEstimate(flops=3 * 10**9, bytes_accessed=2**23, transcendentals=0),
    )(shifts, along, *rest, *tables)


def finish_kernel(*refs):
    count = len(refs) // 2
    sems = refs[-1]
    copies = [pltpu.make_async_copy(refs[i], refs[count + i], sems.at[i]) for i in range(count)]
    for copy in copies:
        copy.start()
    for copy in copies:
        copy.wait()


def finish(*results):
    hbm = pl.BlockSpec(memory_space=pltpu.HBM)
    return pl.pallas_call(
        finish_kernel,
        out_shape=[jax.ShapeDtypeStruct(r.shape, r.dtype) for r in results],
        in_specs=[pl.BlockSpec(memory_space=pltpu.VMEM)] * len(results),
        out_specs=[hbm] * len(results),
        scratch_shapes=[pltpu.SemaphoreType.DMA((len(results),))],
        name="finish",
    )(*results)


def per_device(tiles, shifts, piece_target, coarse_target):
    tile = tiles[0, 0]
    count_y = lax.axis_size("ty")
    count_x = lax.axis_size("tx")
    cap = NZ * 2 * PIECES // (count_y * count_x)
    *operands, most = front(shifts[0, 0], tile, piece_target[0], coarse_target[0], count_y, count_x)
    run = functools.partial(exchange, shifts[0, 0], *operands, count_y=count_y, count_x=count_x)
    fewer = cap * 3 // 4
    if fewer % 16:
        return tuple(finish(*run(cap=cap, collective_id=1)))
    results = lax.cond(
        most[0, 0] <= fewer,
        lambda: tuple(run(cap=fewer, collective_id=1)),
        lambda: tuple(run(cap=cap, collective_id=2)),
    )
    return tuple(finish(*results))


def solution(mesh):
    placed = (
        P("ty", "tx", None, None, None),
        P("ty", "tx", None),
        P("ty", "tx", None),
        P("ty", "tx", None),
    )
    return jax.shard_map(
        per_device,
        mesh=mesh,
        in_specs=placed,
        out_specs=(P(("ty", "tx"), None), P(("ty", "tx"), None), P("ty", "tx"), P("ty", "tx")),
        check_vma=False,
    )
```

```python
import functools
import math

import jax
import jax.numpy as jnp
import numpy as np
from jax import lax
from jax.experimental import pallas as pl
from jax.experimental.pallas import tpu as pltpu
from jax.sharding import PartitionSpec as P

SIDE = 32
OV = 48
H = 8
SLOTS = 64
LANES = 128
GROUPS = LANES // SIDE
EDGE = 2 * H
NZ = 4
PIECES = 256
PAIRS = SIDE // 2
WIDE = 2 * LANES
CHUNKS = 8
AHEAD = 3
LEAD = AHEAD // 2 + 1
LAG = 3
PER = PAIRS // CHUNKS
F32 = jnp.float32
BF16 = jnp.bfloat16
MESH = pl.DeviceIdType.MESH
DIRECTIONS = ((1, 0), (-1, 0), (0, 1), (0, -1), (1, 1), (1, -1), (-1, 1), (-1, -1))


def highest(left, right):
    return jnp.dot(left, right, precision=lax.Precision.HIGHEST, preferred_element_type=F32)


def iota(shape, dim):
    return lax.broadcasted_iota(jnp.int32, shape, dim)


def mm(a, b):
    return jnp.dot(a, b, preferred_element_type=F32)


def mm_t(a, b):
    return lax.dot_general(a, b, (((1,), (1,)), ((), ())), preferred_element_type=F32)


def mark(condition):
    return condition.astype(F32).astype(BF16)


def swap_groups(parts):
    group = iota(parts[0].shape, 1) // SIDE

    def pick(choices):
        value = choices[3]
        for g in range(3):
            value = jnp.where(group == g, choices[g], value)
        return value

    turned = []
    for d in range(GROUPS):
        mixed = pick([parts[(g + d) % GROUPS] for g in range(GROUPS)])
        turned.append(pltpu.roll(mixed, d * SIDE, 1) if d else mixed)
    return [pick([turned[(j - g) % GROUPS] for j in range(GROUPS)]) for g in range(GROUPS)]


def taps(offset, out, column):
    whole, frac = offset
    at = out + whole + H
    return (
        jnp.where(column == at, 1.0 - frac, 0.0) + jnp.where(column == at + 1, frac, 0.0)
    ).astype(BF16)


def split_shift(shift):
    whole = lax.shift_right_arithmetic(shift, 2)
    return whole, (shift - 4 * whole).astype(F32) * 0.25


def ramp_at(index, length):
    nearest = jnp.minimum(jnp.minimum(index + 1, length - index), OV).astype(F32)
    return 1.0 + nearest * (3.0 / OV)


def turned_row(at, grid):
    return (at % grid) * SIDE + at // grid


def edge_index(c, length):
    return c % H + jnp.where(c < EDGE, 0, length + H)


def column_of(targets, count_x):
    owner = targets // SLOTS
    return (owner // count_x) * (count_x // NZ) + owner % (count_x // NZ)


def front_kernel(
    count_y, count_x, fewer, shorter, shift_ref, tile_hbm, piece_ids_hbm, coarse_ids_hbm,
    along_ref, tb_ref, side_ref, ct_ref, cb_ref, sums_ref, all_ids_ref, fits_ref,
    tile_ref, piece_ids_ref, coarse_ids_ref, ids_ref, ids_rows_ref, strips_ref, ends_ref,
    tile_sem, halo_send, halo_recv, id_send, id_recv,
):
    depth, length, _ = tile_ref.shape
    grid = length // SIDE
    devices = count_y * count_x
    ty, tx = lax.axis_index("ty"), lax.axis_index("tx")
    me = ty * count_x + tx
    barrier = pltpu.get_barrier_semaphore()
    load = pltpu.make_async_copy(tile_hbm, tile_ref, tile_sem.at[0])
    load.start()
    loads = (
        pltpu.make_async_copy(piece_ids_hbm, piece_ids_ref, tile_sem.at[1]),
        pltpu.make_async_copy(coarse_ids_hbm, coarse_ids_ref, tile_sem.at[2]),
    )
    for copy in loads:
        copy.start()

    def at(peer):
        return (peer // count_x, peer % count_x)

    def greet(d, carry):
        pl.semaphore_signal(barrier, inc=1, device_id=at((me + d) % devices), device_id_type=MESH)
        return carry

    lax.fori_loop(1, devices, greet, 0)

    def there(dy, dx):
        y, x = ty + dy, tx + dx
        return (y >= 0) & (y < count_y) & (x >= 0) & (x < count_x)

    low, high = pl.ds(0, EDGE), pl.ds(EDGE, EDGE)

    def landing(dy, dx):
        if dx == 0:
            return tb_ref.at[:, low if dy == 1 else high, :]
        half = low if dx == 1 else high
        if dy == 0:
            return side_ref.at[:, half, :]
        return (ct_ref if dy == 1 else cb_ref).at[:, half, :]

    def halo(i):
        dy, dx = DIRECTIONS[i]
        if dx == 0:
            source = ends_ref.at[:, high if dy == 1 else low, :]
        else:
            half = high if dx == 1 else low
            if dy == 0:
                source = strips_ref.at[:, half, :]
            else:
                source = strips_ref.at[:, half, pl.ds(length - LANES if dy == 1 else 0, LANES)]
        return pltpu.make_async_remote_copy(
            src_ref=source,
            dst_ref=landing(dy, dx),
            send_sem=halo_send.at[i],
            recv_sem=halo_recv.at[i],
            device_id=(ty + dy, tx + dx),
            device_id_type=MESH,
        )

    for dy, dx in DIRECTIONS:

        @pl.when(jnp.logical_not(there(-dy, -dx)))
        def _():
            ref = landing(dy, dx)
            ref[...] = jnp.zeros(ref.shape, ref.dtype)

    for copy in loads:
        copy.wait()
    ids_ref[...] = jnp.full(ids_ref.shape, -1, jnp.int32)
    ids_ref[0:1, :] = piece_ids_ref[...]
    ids_ref[1:2, :SLOTS] = coarse_ids_ref[...]

    row, lane = iota((2 * EDGE, LANES), 0), iota((2 * EDGE, LANES), 1)
    back = lane - (LANES - OV)
    first_bins = (row >= EDGE) & (lane < OV) & (lane // 4 == row - EDGE)
    last_bins = (row >= EDGE) & (back >= 0) & (back // 4 == row - EDGE)

    def picks(z):
        own = (row < EDGE) & (row // H == z % 2)
        first = mark((own & (lane == row % H)) | first_bins)
        return first, mark((own & (lane - (LANES - H) == row % H)) | last_bins)

    load.wait()
    left = right = jnp.zeros((EDGE, length), F32)
    for k in range(depth // 2):
        lows = highs = jnp.zeros((2 * EDGE, length), F32)
        for z in (2 * k, 2 * k + 1):
            first, last = picks(z)
            lows += mm_t(first, tile_ref[z, :, :LANES])
            highs += mm_t(last, tile_ref[z, :, length - LANES :])
        left += lows[EDGE:]
        right += highs[EDGE:]
        strips_ref[k, :EDGE, :] = lows[:EDGE].astype(BF16)
        strips_ref[k, EDGE:, :] = highs[:EDGE].astype(BF16)
        pair = (2 * k, 2 * k + 1)
        ends = [tile_ref[z, :EDGE, :].astype(F32)[:H] for z in pair]
        ends += [tile_ref[z, length - EDGE :, :].astype(F32)[H:] for z in pair]
        ends_ref[k] = jnp.concatenate(ends).astype(BF16)
    first, last = picks(0)

    pl.semaphore_wait(barrier, devices - 1)
    for i, (dy, dx) in enumerate(DIRECTIONS):

        @pl.when(there(dy, dx))
        def _():
            halo(i).start()

    def ids(peer):
        return pltpu.make_async_remote_copy(
            src_ref=ids_ref,
            dst_ref=all_ids_ref.at[me],
            send_sem=id_send.at[peer],
            recv_sem=id_recv.at[0],
            device_id=at(peer),
            device_id_type=MESH,
        )

    def start(d, carry):
        ids((me + d) % devices).start()
        return carry

    lax.fori_loop(1, devices, start, 0)
    all_ids_ref[me] = ids_ref[...]

    sy = split_shift(shift_ref[0])
    full = (length, length)
    ry = taps(sy, turned_row(iota(full, 0), grid), iota(full, 1) + H)
    part = length // CHUNKS
    for z in range(depth):
        along = mm(ry, tile_ref[z])
        for c in range(CHUNKS):
            along_ref[c, z * part : (z + 1) * part, :] = along[c * part : (c + 1) * part]

    top = bottom = jnp.zeros((EDGE, length), F32)
    for z in range(depth):
        top += mm(first[EDGE:], tile_ref[z, :LANES, :])
        bottom += mm(last[EDGE:], tile_ref[z, length - LANES :, :])
    sums_ref[...] = jnp.concatenate([left, top, right, bottom])

    others = pl.ds(0, devices - 1)
    pltpu.make_async_remote_copy(
        src_ref=all_ids_ref.at[others],
        dst_ref=all_ids_ref.at[others],
        send_sem=id_send.at[me],
        recv_sem=id_recv.at[0],
        device_id=at(me),
        device_id_type=MESH,
    ).wait_recv()

    def gather(d, carry):
        ids_rows_ref[pl.ds(d, 1), :] = all_ids_ref[d][0:1, :]
        return carry

    lax.fori_loop(0, devices, gather, 0)
    columns = column_of(ids_rows_ref[...], count_x)
    ones = jnp.ones((PIECES, LANES), BF16)
    most = jnp.zeros((devices, LANES), F32)
    for p in range(count_y * (count_x // NZ)):
        most = jnp.maximum(most, mm(mark(columns == p), ones))
    fits = jnp.max(most) <= float(fewer)

    ny = count_x // NZ
    owner = iota((count_y * ny, devices), 1)
    in_column = (owner // count_x) * ny + owner % ny == iota((count_y * ny, devices), 0)
    filled = jnp.zeros((1, 1), F32)
    for end in (0, NZ - 1):
        counts = jnp.zeros((devices, SLOTS), F32)
        for p in range(count_y * ny):
            d = (p // ny) * count_x + end * ny + p % ny
            targets = ids_rows_ref[d : d + 1, :]
            owners = mark(iota((devices, PIECES), 0) == targets // SLOTS)
            counts += mm_t(owners, mark(iota((SLOTS, PIECES), 0) == targets % SLOTS))
        elsewhere = mark(in_column & (owner % count_x // ny != end))
        slots = mm(elsewhere, mark(counts > 0.0))
        filled = jnp.maximum(filled, jnp.max(jnp.sum(slots, axis=1, keepdims=True)))
    fits_ref[0, 0] = jnp.where(fits & (jnp.max(filled) <= float(shorter)), 1, 0)

    for i, (dy, dx) in enumerate(DIRECTIONS):

        @pl.when(there(-dy, -dx))
        def _():
            halo(i).wait_recv()

    for i, (dy, dx) in enumerate(DIRECTIONS):

        @pl.when(there(dy, dx))
        def _():
            halo(i).wait_send()

    def finish(d, carry):
        ids((me + d) % devices).wait_send()
        return carry

    lax.fori_loop(1, devices, finish, 0)


def front(shifts, tile, piece_ids, coarse_ids, count_y, count_x, fewer, shorter):
    depth, length, _ = tile.shape
    devices = count_y * count_x
    vmem = pl.BlockSpec(memory_space=pltpu.VMEM)
    smem = pl.BlockSpec(memory_space=pltpu.SMEM)
    strip = jax.ShapeDtypeStruct((depth // 2, 2 * EDGE, length), BF16)
    corner = jax.ShapeDtypeStruct((depth // 2, 2 * EDGE, LANES), BF16)
    return pl.pallas_call(
        functools.partial(front_kernel, count_y, count_x, fewer, shorter),
        out_shape=[
            jax.ShapeDtypeStruct((CHUNKS, depth * length // CHUNKS, length), F32),
            strip, strip, corner, corner,
            jax.ShapeDtypeStruct((4 * EDGE, length), F32),
            jax.ShapeDtypeStruct((devices, 2, PIECES), jnp.int32),
            jax.ShapeDtypeStruct((1, 1), jnp.int32),
        ],
        in_specs=[smem] + [pl.BlockSpec(memory_space=pltpu.HBM)] * 3,
        out_specs=[vmem] * 7 + [smem],
        scratch_shapes=[
            pltpu.VMEM(tile.shape, BF16),
            pltpu.VMEM((1, PIECES), jnp.int32),
            pltpu.VMEM((1, SLOTS), jnp.int32),
            pltpu.VMEM((2, PIECES), jnp.int32),
            pltpu.VMEM((devices, PIECES), jnp.int32),
            pltpu.VMEM((depth // 2, 2 * EDGE, length), BF16),
            pltpu.VMEM((depth // 2, 2 * EDGE, length), BF16),
            pltpu.SemaphoreType.DMA((3,)),
            pltpu.SemaphoreType.DMA((8,)),
            pltpu.SemaphoreType.DMA((8,)),
            pltpu.SemaphoreType.DMA((devices,)),
            pltpu.SemaphoreType.DMA((1,)),
        ],
        name="front",
        compiler_params=pltpu.CompilerParams(
            collective_id=0, has_side_effects=True, vmem_limit_bytes=55 * 2**20
        ),
        cost_estimate=pl.CostEstimate(flops=10**9, bytes_accessed=2**21, transcendentals=0),
    )(shifts, tile, piece_ids, coarse_ids)


def phase(cos_a, sin_a, cos_b, sin_b, own, other):
    def spectrum(values):
        left_cos = highest(cos_a, values)
        left_sin = highest(sin_a, values)
        re = highest(left_cos, cos_b) - highest(left_sin, sin_b)
        im = -(highest(left_cos, sin_b) + highest(left_sin, cos_b))
        return (re, im)

    own_re, own_im = spectrum(own)
    other_re, other_im = spectrum(other)
    cross_re = own_re * other_re + own_im * other_im
    cross_im = own_im * other_re - own_re * other_im
    scale = 1.0 / jnp.sqrt(cross_re * cross_re + cross_im * cross_im + 1.0)
    normed_re = cross_re * scale
    normed_im = cross_im * scale
    out = highest(highest(cos_a, normed_re) - highest(sin_a, normed_im), cos_b)
    return out - highest(highest(sin_a, normed_re) + highest(cos_a, normed_im), sin_b)


def exchange_kernel(
    count_y, count_x, length, cap, listed, shift_ref, along_ref, tb_ref, side_ref, above_ref, below_ref, sums_ref, ids_ref,
    ca_ref, sa_ref, cb_ref, sb_ref,
    joined_ref, coarse_ref, corr_right_ref, corr_below_ref,
    rx_ref, rx_edge_ref, pack_ref, piece_ref, send_ref, recv_ref, targets_ref, rank_ref, turn_ref, reduce_ref, inv_ref, dense_ref, zsend_ref, zrecv_ref,
    counts_ref, ramp_ref, expand_ref, list_ref, lists_ref, got_lists_ref, total_ref,
    sum_ref, regroup_ref, quads_ref, all_quads_ref,
    bins_ref, next_ref, bin_send, bin_recv, plane_send, plane_recv, line_send, line_recv, row_send, row_recv,
):
    ny = count_x // NZ
    plane = count_y * ny
    devices = count_y * count_x
    sums = NZ * SLOTS
    grid = length // SIDE
    ty, tx = lax.axis_index("ty"), lax.axis_index("tx")
    me = ty * count_x + tx
    y, z = tx % ny, tx // ny
    mine = ty * ny + y
    near = z + 1 - 2 * (z % 2)
    cross, diag = NZ - 1 - z, NZ - 1 - near
    mid = ((z + 1) // 2) % 2
    barrier = pltpu.get_barrier_semaphore()

    def in_plane(p):
        return (p // ny, z * ny + p % ny)

    def in_line(other):
        return (ty, other * ny + y)

    def greet_plane(d, carry):
        pl.semaphore_signal(barrier, inc=1, device_id=in_plane((mine + d) % plane), device_id_type=MESH)
        return carry

    def greet_row(d, carry):
        pl.semaphore_signal(barrier, inc=1, device_id=(ty, (z * ny + d) % count_x), device_id_type=MESH)
        return carry

    lax.fori_loop(1, plane, greet_plane, 0)
    lax.fori_loop(ny, count_x, greet_row, 0)

    def targets_of(device):
        return ids_ref[device][0:1, :]

    def sum_row_of(targets):
        return ((targets // SLOTS) % count_x) // ny * SLOTS + targets % SLOTS

    square = (PIECES, PIECES)
    earlier = mark(iota(square, 0) < iota(square, 1))
    column = column_of(targets_of(me), count_x)
    onehot = (iota((targets_ref.shape[0], PIECES), 0) == column).astype(F32)
    rank = jnp.sum(onehot * mm(onehot.astype(BF16), earlier), axis=0, keepdims=True)
    position = (column * cap).astype(F32) + rank
    chosen = mark(iota((plane * cap, PIECES), 0).astype(F32) == position)
    stacked = iota(square, 1)
    stacked = mark(iota(square, 0) == (stacked % grid) * grid + stacked // grid)
    pack_ref[...] = mm(chosen, stacked).astype(BF16)

    sx = split_shift(shift_ref[1])
    rows = along_ref.shape[1]
    part = length // CHUNKS
    depth = rows // part
    edges = depth // 2 * 2 * EDGE
    full, wide = (length, length), (edges, length)
    rx_ref[...] = taps(sx, iota(full, 1), iota(full, 0) + H)
    rx_edge_ref[...] = taps(sx, iota(wide, 1), edge_index(iota(wide, 0) % (2 * EDGE), length))
    sy = split_shift(shift_ref[0])
    side = side_ref[...].reshape(edges, length)
    tb = tb_ref[...].reshape(edges, length)
    above = above_ref[...].reshape(edges, LANES)
    below = below_ref[...].reshape(edges, LANES)

    def slice_of(c):
        return c // (2 * EDGE) * 2 + c // H % 2

    ramp_x = ramp_at(iota((1, length), 1), length)

    pl.semaphore_wait(barrier, plane - 1 + count_x - ny)

    def rows_of(p):
        return pl.ds(pl.multiple_of(p * cap, cap), cap)

    def plane_copy(i, peer):
        return pltpu.make_async_remote_copy(
            src_ref=send_ref.at[i, rows_of(peer), :],
            dst_ref=recv_ref.at[i, rows_of(mine), :],
            send_sem=plane_send.at[0],
            recv_sem=plane_recv.at[i],
            device_id=in_plane(peer),
            device_id_type=MESH,
        )

    def pack(c):
        def of(shape, column):
            return taps(sy, turned_row(iota(shape, 0) % part + c * part, grid), column)

        lane = iota((rows, edges), 1)
        mine_only = slice_of(lane) == iota((rows, edges), 0) // part
        ends = of((rows, edges), jnp.where(mine_only, edge_index(lane % (2 * EDGE), length), -1))
        along = (along_ref[c] + mm(ends, tb)).astype(BF16)
        aside = (
            mm_t(of((part, length), iota((part, length), 1) + H), side)
            + mm_t(of((part, LANES), iota((part, LANES), 1) + (H - LANES)), above)
            + mm_t(of((part, LANES), iota((part, LANES), 1) + (length + H)), below)
        )
        aside = jnp.where(mine_only, jnp.concatenate([aside] * depth), 0.0).astype(BF16)
        work = mm(along, rx_ref[...]) + mm(aside, rx_edge_ref[...])
        at = iota((rows, 1), 0) % part + c * part
        work = work * (ramp_at(turned_row(at, grid), length) * ramp_x)
        for q in range(length // LANES):
            parts = [work[d * part : (d + 1) * part, q * LANES : (q + 1) * LANES] for d in range(depth)]
            for g, piece in enumerate(swap_groups(parts)):
                into = slice((q * GROUPS + g) * grid, (q * GROUPS + g + 1) * grid)
                for r in range(2 * PER):
                    value = piece[r * grid : (r + 1) * grid].astype(BF16)
                    piece_ref[r // 2, into, (r % 2) * LANES : (r % 2 + 1) * LANES] = value
        for j in range(PER):
            i = c * PER + j
            send_ref[i] = mm(pack_ref[...], piece_ref[j]).astype(BF16)
            recv_ref[i, rows_of(mine), :] = send_ref[i, rows_of(mine), :]

    def send(i):
        def start(d, inner):
            plane_copy(i, (mine + d) % plane).start()
            return inner

        lax.fori_loop(1, plane, start, 0)

    for c in range(LEAD):
        pack(c)
        for i in range(c * PER, min((c + 1) * PER, AHEAD)):
            send(i)

    def bins_copy(i):
        return pltpu.make_async_remote_copy(
            src_ref=bins_ref.at[i],
            dst_ref=next_ref.at[i],
            send_sem=bin_send.at[i],
            recv_sem=bin_recv.at[i],
            device_id=((ty, tx - 1), (ty - 1, tx))[i],
            device_id_type=MESH,
        )

    to_there = (tx > 0, ty > 0)
    from_there = (tx < count_x - 1, ty < count_y - 1)

    def bins():
        pool = (iota((length, length // 4), 0) // 4 == iota((length, length // 4), 1)).astype(F32)
        value = highest(sums_ref[...], pool) * (1.0 / math.sqrt(16.0 * depth))
        for i in range(4):
            bins_ref[i] = value[i * EDGE : (i + 1) * EDGE]
        for i in range(2):

            @pl.when(to_there[i])
            def _():
                bins_copy(i).start()

            @pl.when(jnp.logical_not(from_there[i]))
            def _():
                next_ref[i] = jnp.zeros(next_ref.shape[1:], F32)

    end = mid * near + (1 - mid) * z

    def fill(p, filled):
        targets = targets_of((p // ny) * count_x + end * ny + p % ny)
        into = jnp.where(column_of(targets, count_x) == mine, sum_row_of(targets), -1)
        return filled + (iota((sums, PIECES), 0) == into).astype(F32)

    filled = lax.fori_loop(0, plane, fill, jnp.zeros((sums, PIECES), F32))
    filled = jnp.broadcast_to(jnp.sum(filled, axis=1, keepdims=True), (sums, sums))
    filled = (filled > 0.0) & (iota((sums, sums), 0) // SLOTS != end)
    before = mm(mark(iota((sums, sums), 1) < iota((sums, sums), 0)), mark(filled))
    expand = mark(filled & (before == iota((sums, sums), 1).astype(F32)))
    eye = mark(iota((sums, sums), 0) == iota((sums, sums), 1))
    expand_ref[...] = expand
    list_ref[...] = mm_t(eye, expand).astype(BF16)

    targets_ref[...] = jnp.full(targets_ref.shape, -1, jnp.int32)

    def fetch(p, carry):
        targets_ref[pl.ds(p, 1), :] = targets_of((p // ny) * count_x + z * ny + p % ny)
        return carry

    lax.fori_loop(0, plane, fetch, 0)
    rank_ref[...] = mm(mark(column_of(targets_ref[...], count_x) == mine), earlier)

    def turn(p, carry):
        targets = targets_ref[pl.ds(p, 1), :]
        into = jnp.where(column_of(targets, count_x) == mine, sum_row_of(targets), -1)
        into = mark(iota((sums, PIECES), 0) == into)
        chosen = mark(iota((cap, PIECES), 0).astype(F32) == rank_ref[pl.ds(p, 1), :])
        turn_ref[rows_of(p), :] = mm_t(chosen, into).astype(BF16)
        return carry

    lax.fori_loop(0, plane, turn, 0)
    reduce_ref[...] = mm_t(eye, turn_ref[...]).astype(BF16)

    def unit_rows(unit):
        return pl.ds(pl.multiple_of(unit * SLOTS, SLOTS), SLOTS)

    def line_copy(i, unit, slot, peer):
        return pltpu.make_async_remote_copy(
            src_ref=zsend_ref.at[i, unit_rows(unit), :],
            dst_ref=zrecv_ref.at[slot, i],
            send_sem=line_send.at[0],
            recv_sem=line_recv.at[i, slot],
            device_id=in_line(peer),
            device_id_type=MESH,
        )

    def list_copy(i):
        return pltpu.make_async_remote_copy(
            src_ref=lists_ref.at[i],
            dst_ref=got_lists_ref.at[i],
            send_sem=line_send.at[1],
            recv_sem=line_recv.at[i, 3],
            device_id=in_line(near),
            device_id_type=MESH,
        )

    def plane_done(i):
        others = pl.ds(0, (plane - 1) * cap)
        return pltpu.make_async_remote_copy(
            src_ref=send_ref.at[i, others, :],
            dst_ref=recv_ref.at[i, others, :],
            send_sem=plane_send.at[0],
            recv_sem=plane_recv.at[i],
            device_id=in_line(near),
            device_id_type=MESH,
        )

    def reduce(i):
        plane_done(i).wait_recv()
        value = mm(reduce_ref[...], recv_ref[i])
        dense_ref[i] = value
        zsend_ref[i] = value.astype(BF16)

        @pl.when(mid == 1)
        def _():
            line_copy(i, near, 0, near).start()

        @pl.when(mid == 0)
        def _():
            lists_ref[i] = mm(list_ref[:listed, :], zsend_ref[i]).astype(BF16)
            list_copy(i).start()

    def merge(i):
        @pl.when(mid == 1)
        def _():
            list_copy(i).wait_recv()
            dense_ref[i] = dense_ref[i] + mm(expand_ref[:, :listed], got_lists_ref[i])
            for unit, slot in ((diag, 1), (cross, 2)):
                zsend_ref[i, unit_rows(unit), :] = dense_ref[i, unit_rows(unit), :].astype(BF16)
                line_copy(i, unit, slot, unit).start()

    slot = iota((SLOTS, PIECES), 0) + me * SLOTS

    def count(device, counts):
        return counts + (targets_of(device) == slot).astype(F32)

    counts = lax.fori_loop(0, devices, count, jnp.zeros((SLOTS, PIECES), F32))
    counts_ref[...] = counts.astype(BF16)
    place = iota((PIECES, 1), 0)
    lane = iota((1, WIDE), 1)
    ramp_ref[...] = ramp_at(place % grid * SIDE + lane % SIDE, length)

    def weigh(i):
        patch = (ramp_at(place // grid * SIDE + lane // LANES + 2 * i, length) * ramp_ref[...]).astype(BF16)
        inv_ref[i] = 1.0 / jnp.maximum(mm(counts_ref[...], patch), 1.0)

    def surface(i, ref):
        @pl.when(from_there[i])
        def _():
            bins_copy(i).wait_recv()

        @pl.when(to_there[i])
        def _():
            bins_copy(i).wait_send()

        tables = (ca_ref[...], sa_ref[...], cb_ref[...], sb_ref[...])
        ref[...] = phase(*tables, bins_ref[2 + i], next_ref[i])[: ref.shape[0]]

    inner = iota((WIDE, LANES), 0)
    outer = iota((WIDE, LANES), 1)
    pooled = inner % LANES // (2 * SIDE) * (SIDE // 2) + inner % SIDE // 2

    def final(c):
        for j in range(PER):
            i = c * PER + j

            @pl.when(mid == 1)
            def _():
                line_copy(i, cross, 2, cross).wait_recv()
                total_ref[j] = dense_ref[i, unit_rows(z), :] + zrecv_ref[2, i].astype(F32)

            @pl.when(mid == 0)
            def _():
                line_copy(i, near, 0, near).wait_recv()
                line_copy(i, near, 1, near).wait_recv()
                value = dense_ref[i, unit_rows(z), :] + zrecv_ref[0, i].astype(F32)
                total_ref[j] = value + zrecv_ref[1, i].astype(F32)

        level = jnp.zeros((SLOTS, LANES), F32)
        rows = []
        for j in range(PER):
            i = c * PER + j
            value = (total_ref[j] * inv_ref[i]).astype(BF16)
            level += mm(value, mark(outer == pooled + j * SIDE))
            value = value.astype(F32)
            rows += [value[:, :LANES], value[:, LANES:]]
        for s, part in enumerate(swap_groups(rows)):
            joined_ref[:, pl.ds(pl.multiple_of(s * SIDE * SIDE + c * LANES, LANES), LANES)] = part.astype(BF16)
        a, b = iota((LANES, LANES), 0), iota((LANES, LANES), 1)
        into = c * (SIDE // 4) + a % (SIDE // 2) // 2
        sum_ref[...] += mm((level * 0.125).astype(BF16), mark((a < PER * SIDE) & (b == into)))

    def regroup():
        u = iota((SLOTS, LANES), 0)
        wanted = tx * SLOTS + 4 * (u % (SLOTS // 4)) + u // (SLOTS // 4)
        for q in range(count_x // 2):
            pair = [ids_ref[ty * count_x + 2 * q + j][1:2, :LANES] for j in range(2)]
            named = jnp.where(iota((1, LANES), 1) < SLOTS, pair[0], pltpu.roll(pair[1], SLOTS, 1))
            regroup_ref[:, q * LANES : (q + 1) * LANES] = mark(named == wanted)

    sum_ref[...] = jnp.zeros_like(sum_ref)

    def step(i, carry):
        @pl.when(i < PAIRS)
        def _():
            reduce(i)

        @pl.when(i + AHEAD < PAIRS)
        def _():
            send(i + AHEAD)

        @pl.when((i % PER == 0) & (i // PER + LEAD < CHUNKS))
        def _():
            pack(i // PER + LEAD)

        @pl.when(i < PAIRS)
        def _():
            weigh(i)

        pl.when(i == 1)(bins)
        pl.when(i == 5)(lambda: surface(0, corr_right_ref))
        pl.when(i == 7)(lambda: surface(1, corr_below_ref))
        pl.when(i == 9)(regroup)

        @pl.when((i >= LAG) & (i < PAIRS + LAG))
        def _():
            merge(i - LAG)

        last = i - LAG - LAG

        @pl.when((last >= 0) & (last % PER == PER - 1))
        def _():
            final(last // PER)

        return carry

    lax.fori_loop(0, PAIRS + LAG + LAG, step, 0)
    quads_ref[...] = (sum_ref[...] * 0.125).astype(BF16)

    def row_copy(source, target, peer):
        return pltpu.make_async_remote_copy(
            src_ref=quads_ref,
            dst_ref=all_quads_ref.at[target],
            send_sem=row_send.at[source],
            recv_sem=row_recv.at[target],
            device_id=(ty, peer),
            device_id_type=MESH,
        )

    def start_row(d, carry):
        peer = (tx + d) % count_x
        row_copy(peer, tx, peer).start()
        return carry

    lax.fori_loop(1, count_x, start_row, 0)
    all_quads_ref[tx] = quads_ref[...]

    pltpu.make_async_remote_copy(
        src_ref=send_ref.at[:, pl.ds(0, (plane - 1) * cap), :],
        dst_ref=send_ref.at[:, pl.ds(0, (plane - 1) * cap), :],
        send_sem=plane_send.at[0],
        recv_sem=plane_recv.at[0],
        device_id=in_line(near),
        device_id_type=MESH,
    ).wait_send()

    def sent(ref, which):
        return pltpu.make_async_remote_copy(
            src_ref=ref,
            dst_ref=ref,
            send_sem=line_send.at[which],
            recv_sem=line_recv.at[0, 0],
            device_id=in_line(near),
            device_id_type=MESH,
        )

    @pl.when(mid == 1)
    def _():
        sent(zsend_ref.at[:, pl.ds(0, 3 * SLOTS), :], 0).wait_send()

    @pl.when(mid == 0)
    def _():
        sent(lists_ref, 1).wait_send()

    def finish_row(d, carry):
        peer = (tx + d) % count_x
        copy = row_copy(peer, peer, peer)
        copy.wait_send()
        copy.wait_recv()
        return carry

    lax.fori_loop(1, count_x, finish_row, 0)

    placed = mm(regroup_ref[...], all_quads_ref[...].reshape(count_x * SLOTS, LANES)).astype(BF16)
    side = SIDE // 4
    a, b = iota((LANES, WIDE), 0), iota((LANES, WIDE), 1)
    out = jnp.zeros((SLOTS // 4, WIDE), F32)
    for q in range(4):
        into = (q // 2) * 2 * side * side + a // side * 2 * side + (q % 2) * side + a % side
        out += mm(placed[q * (SLOTS // 4) : (q + 1) * (SLOTS // 4)], mark((a < side * side) & (b == into)))
    coarse_ref[...] = out.astype(BF16)


def dft_tables(length, padded):
    index = np.arange(length)
    angle = (index[:, None] * index[None, :] % length) * (2.0 * math.pi / length)
    pad = ((0, padded - length),) * 2
    return tuple(
        jnp.asarray(np.pad(table / math.sqrt(length), pad).astype(np.float32)) for table in (np.cos(angle), np.sin(angle))
    )


def exchange(shifts, along, *rest, cap, listed, count_y, count_x, collective_id):
    length = along.shape[2]
    edges = rest[0].shape[0] * 2 * EDGE
    plane = count_y * (count_x // NZ)
    sums = NZ * SLOTS
    vmem = pl.BlockSpec(memory_space=pltpu.VMEM)
    tables = dft_tables(OV // 4, EDGE) + dft_tables(length // 4, length // 4)
    corr = jax.ShapeDtypeStruct((OV // 4, length // 4), F32)
    return pl.pallas_call(
        functools.partial(exchange_kernel, count_y, count_x, length, cap, listed),
        out_shape=[
            jax.ShapeDtypeStruct((SLOTS, SIDE * LANES), BF16),
            jax.ShapeDtypeStruct((SLOTS // 4, WIDE), BF16),
            corr,
            corr,
        ],
        in_specs=[pl.BlockSpec(memory_space=pltpu.SMEM)] + [vmem] * 11,
        out_specs=[vmem] * 4,
        scratch_shapes=[
            pltpu.VMEM((length, length), BF16),
            pltpu.VMEM((edges, length), BF16),
            pltpu.VMEM((plane * cap, PIECES), BF16),
            pltpu.VMEM((PER, PIECES, WIDE), BF16),
            pltpu.VMEM((PAIRS, plane * cap, WIDE), BF16),
            pltpu.VMEM((PAIRS, plane * cap, WIDE), BF16),
            pltpu.VMEM((max(16, plane), PIECES), jnp.int32),
            pltpu.VMEM((max(16, plane), PIECES), F32),
            pltpu.VMEM((plane * cap, sums), BF16),
            pltpu.VMEM((sums, plane * cap), BF16),
            pltpu.VMEM((PAIRS, SLOTS, WIDE), F32),
            pltpu.VMEM((PAIRS, sums, WIDE), F32),
            pltpu.VMEM((PAIRS, sums, WIDE), BF16),
            pltpu.VMEM((3, PAIRS, SLOTS, WIDE), BF16),
            pltpu.VMEM((SLOTS, PIECES), BF16),
            pltpu.VMEM((PIECES, WIDE), F32),
            pltpu.VMEM((sums, sums), BF16),
            pltpu.VMEM((sums, sums), BF16),
            pltpu.VMEM((PAIRS, listed, WIDE), BF16),
            pltpu.VMEM((PAIRS, listed, WIDE), BF16),
            pltpu.VMEM((PER, SLOTS, WIDE), F32),
            pltpu.VMEM((SLOTS, LANES), F32),
            pltpu.VMEM((SLOTS, count_x * SLOTS), BF16),
            pltpu.VMEM((SLOTS, LANES), BF16),
            pltpu.VMEM((count_x, SLOTS, LANES), BF16),
            pltpu.VMEM((4, EDGE, length // 4), F32),
            pltpu.VMEM((2, EDGE, length // 4), F32),
            pltpu.SemaphoreType.DMA((2,)),
            pltpu.SemaphoreType.DMA((2,)),
            pltpu.SemaphoreType.DMA((1,)),
            pltpu.SemaphoreType.DMA((PAIRS,)),
            pltpu.SemaphoreType.DMA((2,)),
            pltpu.SemaphoreType.DMA((PAIRS, 4)),
            pltpu.SemaphoreType.DMA((count_x,)),
            pltpu.SemaphoreType.DMA((count_x,)),
        ],
        name="exchange",
        compiler_params=pltpu.CompilerParams(
            collective_id=collective_id, has_side_effects=True, vmem_limit_bytes=44 * 2**20
        ),
        cost_estimate=pl.CostEstimate(flops=3 * 10**9, bytes_accessed=2**23, transcendentals=0),
    )(shifts, along, *rest, *tables)


def finish_kernel(*refs):
    count = len(refs) // 2
    sems = refs[-1]
    copies = [pltpu.make_async_copy(refs[i], refs[count + i], sems.at[i]) for i in range(count)]
    for copy in copies:
        copy.start()
    for copy in copies:
        copy.wait()


def finish(*results):
    hbm = pl.BlockSpec(memory_space=pltpu.HBM)
    return pl.pallas_call(
        finish_kernel,
        out_shape=[jax.ShapeDtypeStruct(r.shape, r.dtype) for r in results],
        in_specs=[pl.BlockSpec(memory_space=pltpu.VMEM)] * len(results),
        out_specs=[hbm] * len(results),
        scratch_shapes=[pltpu.SemaphoreType.DMA((len(results),))],
        name="finish",
    )(*results)


def per_device(tiles, shifts, piece_target, coarse_target):
    tile = tiles[0, 0]
    count_y = lax.axis_size("ty")
    count_x = lax.axis_size("tx")
    cap = NZ * 2 * PIECES // (count_y * count_x)
    listed = (NZ - 1) * SLOTS
    fewer, shorter = cap * 3 // 4, listed * 5 // 6
    *operands, fits = front(shifts[0, 0], tile, piece_target[0], coarse_target[0], count_y, count_x, fewer, shorter)
    run = functools.partial(exchange, shifts[0, 0], *operands, count_y=count_y, count_x=count_x)
    if fewer % 16:
        return tuple(finish(*run(cap=cap, listed=listed, collective_id=1)))
    results = lax.cond(
        fits[0, 0] == 1,
        lambda: tuple(run(cap=fewer, listed=shorter, collective_id=1)),
        lambda: tuple(run(cap=cap, listed=listed, collective_id=2)),
    )
    return tuple(finish(*results))


def solution(mesh):
    placed = (
        P("ty", "tx", None, None, None),
        P("ty", "tx", None),
        P("ty", "tx", None),
        P("ty", "tx", None),
    )
    return jax.shard_map(
        per_device,
        mesh=mesh,
        in_specs=placed,
        out_specs=(P(("ty", "tx"), None), P(("ty", "tx"), None), P("ty", "tx"), P("ty", "tx")),
        check_vma=False,
    )
```

```python
import functools
import math

import jax
import jax.numpy as jnp
import numpy as np
from jax import lax
from jax.experimental import pallas as pl
from jax.experimental.pallas import tpu as pltpu
from jax.sharding import PartitionSpec as P

SIDE = 32
OV = 48
H = 8
SLOTS = 64
LANES = 128
GROUPS = LANES // SIDE
EDGE = 2 * H
NZ = 4
PIECES = 256
PAIRS = SIDE // 2
WIDE = 2 * LANES
CHUNKS = 8
AHEAD = 3
LEAD = AHEAD // 2 + 1
LAG = 3
PER = PAIRS // CHUNKS
F32 = jnp.float32
BF16 = jnp.bfloat16
MESH = pl.DeviceIdType.MESH
DIRECTIONS = ((1, 0), (-1, 0), (0, 1), (0, -1), (1, 1), (1, -1), (-1, 1), (-1, -1))


def highest(left, right):
    return jnp.dot(left, right, precision=lax.Precision.HIGHEST, preferred_element_type=F32)


def iota(shape, dim):
    return lax.broadcasted_iota(jnp.int32, shape, dim)


def mm(a, b):
    return jnp.dot(a, b, preferred_element_type=F32)


def mm_t(a, b):
    return lax.dot_general(a, b, (((1,), (1,)), ((), ())), preferred_element_type=F32)


def mark(condition):
    return condition.astype(F32).astype(BF16)


def swap_groups(parts):
    group = iota(parts[0].shape, 1) // SIDE

    def pick(choices):
        value = choices[3]
        for g in range(3):
            value = jnp.where(group == g, choices[g], value)
        return value

    turned = []
    for d in range(GROUPS):
        mixed = pick([parts[(g + d) % GROUPS] for g in range(GROUPS)])
        turned.append(pltpu.roll(mixed, d * SIDE, 1) if d else mixed)
    return [pick([turned[(j - g) % GROUPS] for j in range(GROUPS)]) for g in range(GROUPS)]


def taps(offset, out, column):
    whole, frac = offset
    at = out + whole + H
    return (
        jnp.where(column == at, 1.0 - frac, 0.0) + jnp.where(column == at + 1, frac, 0.0)
    ).astype(BF16)


def split_shift(shift):
    whole = lax.shift_right_arithmetic(shift, 2)
    return whole, (shift - 4 * whole).astype(F32) * 0.25


def ramp_at(index, length):
    nearest = jnp.minimum(jnp.minimum(index + 1, length - index), OV).astype(F32)
    return 1.0 + nearest * (3.0 / OV)


def turned_row(at, grid):
    return (at % grid) * SIDE + at // grid


def edge_index(c, length):
    return c % H + jnp.where(c < EDGE, 0, length + H)


def column_of(targets, count_x):
    owner = targets // SLOTS
    return (owner // count_x) * (count_x // NZ) + owner % (count_x // NZ)


def front_kernel(
    count_y, count_x, fewer, shorter, tile_hbm, piece_ids_hbm, coarse_ids_hbm,
    tile_ref, tb_ref, side_ref, ct_ref, cb_ref, sums_ref, all_ids_ref, fits_ref,
    piece_ids_ref, coarse_ids_ref, ids_ref, ids_rows_ref, strips_ref, ends_ref,
    tile_sem, halo_send, halo_recv, id_send, id_recv,
):
    depth, length, _ = tile_ref.shape
    devices = count_y * count_x
    ty, tx = lax.axis_index("ty"), lax.axis_index("tx")
    me = ty * count_x + tx
    barrier = pltpu.get_barrier_semaphore()
    load = pltpu.make_async_copy(tile_hbm, tile_ref, tile_sem.at[0])
    load.start()
    loads = (
        pltpu.make_async_copy(piece_ids_hbm, piece_ids_ref, tile_sem.at[1]),
        pltpu.make_async_copy(coarse_ids_hbm, coarse_ids_ref, tile_sem.at[2]),
    )
    for copy in loads:
        copy.start()

    def at(peer):
        return (peer // count_x, peer % count_x)

    def greet(d, carry):
        pl.semaphore_signal(barrier, inc=1, device_id=at((me + d) % devices), device_id_type=MESH)
        return carry

    lax.fori_loop(1, devices, greet, 0)

    def there(dy, dx):
        y, x = ty + dy, tx + dx
        return (y >= 0) & (y < count_y) & (x >= 0) & (x < count_x)

    low, high = pl.ds(0, EDGE), pl.ds(EDGE, EDGE)

    def landing(dy, dx):
        if dx == 0:
            return tb_ref.at[:, low if dy == 1 else high, :]
        half = low if dx == 1 else high
        if dy == 0:
            return side_ref.at[:, half, :]
        return (ct_ref if dy == 1 else cb_ref).at[:, half, :]

    def halo(i):
        dy, dx = DIRECTIONS[i]
        if dx == 0:
            source = ends_ref.at[:, high if dy == 1 else low, :]
        else:
            half = high if dx == 1 else low
            if dy == 0:
                source = strips_ref.at[:, half, :]
            else:
                source = strips_ref.at[:, half, pl.ds(length - LANES if dy == 1 else 0, LANES)]
        return pltpu.make_async_remote_copy(
            src_ref=source,
            dst_ref=landing(dy, dx),
            send_sem=halo_send.at[i],
            recv_sem=halo_recv.at[i],
            device_id=(ty + dy, tx + dx),
            device_id_type=MESH,
        )

    for dy, dx in DIRECTIONS:

        @pl.when(jnp.logical_not(there(-dy, -dx)))
        def _():
            ref = landing(dy, dx)
            ref[...] = jnp.zeros(ref.shape, ref.dtype)

    for copy in loads:
        copy.wait()
    ids_ref[...] = jnp.full(ids_ref.shape, -1, jnp.int32)
    ids_ref[0:1, :] = piece_ids_ref[...]
    ids_ref[1:2, :SLOTS] = coarse_ids_ref[...]

    pl.semaphore_wait(barrier, devices - 1)

    def ids(peer):
        return pltpu.make_async_remote_copy(
            src_ref=ids_ref,
            dst_ref=all_ids_ref.at[me],
            send_sem=id_send.at[peer],
            recv_sem=id_recv.at[0],
            device_id=at(peer),
            device_id_type=MESH,
        )

    def start(d, carry):
        ids((me + d) % devices).start()
        return carry

    lax.fori_loop(1, devices, start, 0)
    all_ids_ref[me] = ids_ref[...]

    row, lane = iota((2 * EDGE, LANES), 0), iota((2 * EDGE, LANES), 1)
    back = lane - (LANES - OV)
    first_bins = (row >= EDGE) & (lane < OV) & (lane // 4 == row - EDGE)
    last_bins = (row >= EDGE) & (back >= 0) & (back // 4 == row - EDGE)

    def picks(z):
        own = (row < EDGE) & (row // H == z % 2)
        first = mark((own & (lane == row % H)) | first_bins)
        return first, mark((own & (lane - (LANES - H) == row % H)) | last_bins)

    load.wait()
    left = right = jnp.zeros((EDGE, length), F32)
    for k in range(depth // 2):
        lows = highs = jnp.zeros((2 * EDGE, length), F32)
        for z in (2 * k, 2 * k + 1):
            first, last = picks(z)
            lows += mm_t(first, tile_ref[z, :, :LANES])
            highs += mm_t(last, tile_ref[z, :, length - LANES :])
        left += lows[EDGE:]
        right += highs[EDGE:]
        strips_ref[k, :EDGE, :] = lows[:EDGE].astype(BF16)
        strips_ref[k, EDGE:, :] = highs[:EDGE].astype(BF16)
        pair = (2 * k, 2 * k + 1)
        ends = [tile_ref[z, :EDGE, :].astype(F32)[:H] for z in pair]
        ends += [tile_ref[z, length - EDGE :, :].astype(F32)[H:] for z in pair]
        ends_ref[k] = jnp.concatenate(ends).astype(BF16)
    first, last = picks(0)

    for i, (dy, dx) in enumerate(DIRECTIONS):

        @pl.when(there(dy, dx))
        def _():
            halo(i).start()

    top = bottom = jnp.zeros((EDGE, length), F32)
    for z in range(depth):
        top += mm(first[EDGE:], tile_ref[z, :LANES, :])
        bottom += mm(last[EDGE:], tile_ref[z, length - LANES :, :])
    sums_ref[...] = jnp.concatenate([left, top, right, bottom])

    others = pl.ds(0, devices - 1)
    pltpu.make_async_remote_copy(
        src_ref=all_ids_ref.at[others],
        dst_ref=all_ids_ref.at[others],
        send_sem=id_send.at[me],
        recv_sem=id_recv.at[0],
        device_id=at(me),
        device_id_type=MESH,
    ).wait_recv()

    def gather(d, carry):
        ids_rows_ref[pl.ds(d, 1), :] = all_ids_ref[d][0:1, :]
        return carry

    lax.fori_loop(0, devices, gather, 0)
    columns = column_of(ids_rows_ref[...], count_x)
    ones = jnp.ones((PIECES, LANES), BF16)
    most = jnp.zeros((devices, LANES), F32)
    for p in range(count_y * (count_x // NZ)):
        most = jnp.maximum(most, mm(mark(columns == p), ones))
    fits = jnp.max(most) <= float(fewer)

    ny = count_x // NZ
    owner = iota((count_y * ny, devices), 1)
    in_column = (owner // count_x) * ny + owner % ny == iota((count_y * ny, devices), 0)
    filled = jnp.zeros((1, 1), F32)
    for end in (0, NZ - 1):
        counts = jnp.zeros((devices, SLOTS), F32)
        for p in range(count_y * ny):
            d = (p // ny) * count_x + end * ny + p % ny
            targets = ids_rows_ref[d : d + 1, :]
            owners = mark(iota((devices, PIECES), 0) == targets // SLOTS)
            counts += mm_t(owners, mark(iota((SLOTS, PIECES), 0) == targets % SLOTS))
        elsewhere = mark(in_column & (owner % count_x // ny != end))
        slots = mm(elsewhere, mark(counts > 0.0))
        filled = jnp.maximum(filled, jnp.max(jnp.sum(slots, axis=1, keepdims=True)))
    fits_ref[0, 0] = jnp.where(fits & (jnp.max(filled) <= float(shorter)), 1, 0)

    for i, (dy, dx) in enumerate(DIRECTIONS):

        @pl.when(there(-dy, -dx))
        def _():
            halo(i).wait_recv()

    for i, (dy, dx) in enumerate(DIRECTIONS):

        @pl.when(there(dy, dx))
        def _():
            halo(i).wait_send()

    def finish(d, carry):
        ids((me + d) % devices).wait_send()
        return carry

    lax.fori_loop(1, devices, finish, 0)


def front(tile, piece_ids, coarse_ids, count_y, count_x, fewer, shorter):
    depth, length, _ = tile.shape
    devices = count_y * count_x
    vmem = pl.BlockSpec(memory_space=pltpu.VMEM)
    smem = pl.BlockSpec(memory_space=pltpu.SMEM)
    strip = jax.ShapeDtypeStruct((depth // 2, 2 * EDGE, length), BF16)
    corner = jax.ShapeDtypeStruct((depth // 2, 2 * EDGE, LANES), BF16)
    return pl.pallas_call(
        functools.partial(front_kernel, count_y, count_x, fewer, shorter),
        out_shape=[
            jax.ShapeDtypeStruct(tile.shape, BF16),
            strip, strip, corner, corner,
            jax.ShapeDtypeStruct((4 * EDGE, length), F32),
            jax.ShapeDtypeStruct((devices, 2, PIECES), jnp.int32),
            jax.ShapeDtypeStruct((1, 1), jnp.int32),
        ],
        in_specs=[pl.BlockSpec(memory_space=pltpu.HBM)] * 3,
        out_specs=[vmem] * 7 + [smem],
        scratch_shapes=[
            pltpu.VMEM((1, PIECES), jnp.int32),
            pltpu.VMEM((1, SLOTS), jnp.int32),
            pltpu.VMEM((2, PIECES), jnp.int32),
            pltpu.VMEM((devices, PIECES), jnp.int32),
            pltpu.VMEM((depth // 2, 2 * EDGE, length), BF16),
            pltpu.VMEM((depth // 2, 2 * EDGE, length), BF16),
            pltpu.SemaphoreType.DMA((3,)),
            pltpu.SemaphoreType.DMA((8,)),
            pltpu.SemaphoreType.DMA((8,)),
            pltpu.SemaphoreType.DMA((devices,)),
            pltpu.SemaphoreType.DMA((1,)),
        ],
        name="front",
        compiler_params=pltpu.CompilerParams(
            collective_id=0, has_side_effects=True, vmem_limit_bytes=57 * 2**20
        ),
        cost_estimate=pl.CostEstimate(flops=10**9, bytes_accessed=2**21, transcendentals=0),
    )(tile, piece_ids, coarse_ids)


def phase(cos_a, sin_a, cos_b, sin_b, own, other):
    def spectrum(values):
        left_cos = highest(cos_a, values)
        left_sin = highest(sin_a, values)
        re = highest(left_cos, cos_b) - highest(left_sin, sin_b)
        im = -(highest(left_cos, sin_b) + highest(left_sin, cos_b))
        return (re, im)

    own_re, own_im = spectrum(own)
    other_re, other_im = spectrum(other)
    cross_re = own_re * other_re + own_im * other_im
    cross_im = own_im * other_re - own_re * other_im
    scale = 1.0 / jnp.sqrt(cross_re * cross_re + cross_im * cross_im + 1.0)
    normed_re = cross_re * scale
    normed_im = cross_im * scale
    out = highest(highest(cos_a, normed_re) - highest(sin_a, normed_im), cos_b)
    return out - highest(highest(sin_a, normed_re) + highest(cos_a, normed_im), sin_b)


def exchange_kernel(
    count_y, count_x, length, cap, listed, shift_ref, tile_ref, tb_ref, side_ref, above_ref, below_ref, sums_ref, ids_ref,
    ca_ref, sa_ref, cb_ref, sb_ref,
    joined_ref, coarse_ref, corr_right_ref, corr_below_ref,
    rx_ref, rx_edge_ref, pack_ref, piece_ref, send_ref, recv_ref, targets_ref, rank_ref, turn_ref, reduce_ref, inv_ref, dense_ref, zsend_ref, zrecv_ref,
    counts_ref, ramp_ref, expand_ref, list_ref, lists_ref, got_lists_ref, total_ref,
    sum_ref, regroup_ref, quads_ref, all_quads_ref,
    bins_ref, next_ref, bin_send, bin_recv, plane_send, plane_recv, line_send, line_recv, row_send, row_recv,
):
    ny = count_x // NZ
    plane = count_y * ny
    devices = count_y * count_x
    sums = NZ * SLOTS
    grid = length // SIDE
    ty, tx = lax.axis_index("ty"), lax.axis_index("tx")
    me = ty * count_x + tx
    y, z = tx % ny, tx // ny
    mine = ty * ny + y
    near = z + 1 - 2 * (z % 2)
    cross, diag = NZ - 1 - z, NZ - 1 - near
    mid = ((z + 1) // 2) % 2
    barrier = pltpu.get_barrier_semaphore()

    def in_plane(p):
        return (p // ny, z * ny + p % ny)

    def in_line(other):
        return (ty, other * ny + y)

    def greet_plane(d, carry):
        pl.semaphore_signal(barrier, inc=1, device_id=in_plane((mine + d) % plane), device_id_type=MESH)
        return carry

    def greet_row(d, carry):
        pl.semaphore_signal(barrier, inc=1, device_id=(ty, (z * ny + d) % count_x), device_id_type=MESH)
        return carry

    lax.fori_loop(1, plane, greet_plane, 0)
    lax.fori_loop(ny, count_x, greet_row, 0)

    def targets_of(device):
        return ids_ref[device][0:1, :]

    def sum_row_of(targets):
        return ((targets // SLOTS) % count_x) // ny * SLOTS + targets % SLOTS

    square = (PIECES, PIECES)
    earlier = mark(iota(square, 0) < iota(square, 1))
    column = column_of(targets_of(me), count_x)
    onehot = (iota((targets_ref.shape[0], PIECES), 0) == column).astype(F32)
    rank = jnp.sum(onehot * mm(onehot.astype(BF16), earlier), axis=0, keepdims=True)
    position = (column * cap).astype(F32) + rank
    chosen = mark(iota((plane * cap, PIECES), 0).astype(F32) == position)
    stacked = iota(square, 1)
    stacked = mark(iota(square, 0) == (stacked % grid) * grid + stacked // grid)
    pack_ref[...] = mm(chosen, stacked).astype(BF16)

    sx = split_shift(shift_ref[1])
    depth = tile_ref.shape[0]
    part = length // CHUNKS
    rows = depth * part
    edges = depth // 2 * 2 * EDGE
    full, wide = (length, length), (edges, length)
    rx_ref[...] = taps(sx, iota(full, 1), iota(full, 0) + H)
    rx_edge_ref[...] = taps(sx, iota(wide, 1), edge_index(iota(wide, 0) % (2 * EDGE), length))
    sy = split_shift(shift_ref[0])
    side = side_ref[...].reshape(edges, length)
    tb = tb_ref[...].reshape(edges, length)
    above = above_ref[...].reshape(edges, LANES)
    below = below_ref[...].reshape(edges, LANES)

    def slice_of(c):
        return c // (2 * EDGE) * 2 + c // H % 2

    ramp_x = ramp_at(iota((1, length), 1), length)

    pl.semaphore_wait(barrier, plane - 1 + count_x - ny)

    def rows_of(p):
        return pl.ds(pl.multiple_of(p * cap, cap), cap)

    def plane_copy(i, peer):
        return pltpu.make_async_remote_copy(
            src_ref=send_ref.at[i, rows_of(peer), :],
            dst_ref=recv_ref.at[i, rows_of(mine), :],
            send_sem=plane_send.at[0],
            recv_sem=plane_recv.at[i],
            device_id=in_plane(peer),
            device_id_type=MESH,
        )

    def pack(c):
        def of(shape, column):
            return taps(sy, turned_row(iota(shape, 0) % part + c * part, grid), column)

        lane = iota((rows, edges), 1)
        mine_only = slice_of(lane) == iota((rows, edges), 0) // part
        ends = of((rows, edges), jnp.where(mine_only, edge_index(lane % (2 * EDGE), length), -1))
        ry = of((part, length), iota((part, length), 1) + H)
        along = jnp.concatenate([mm(ry, tile_ref[d]) for d in range(depth)])
        along = (along + mm(ends, tb)).astype(BF16)
        aside = (
            mm_t(ry, side)
            + mm_t(of((part, LANES), iota((part, LANES), 1) + (H - LANES)), above)
            + mm_t(of((part, LANES), iota((part, LANES), 1) + (length + H)), below)
        )
        aside = jnp.where(mine_only, jnp.concatenate([aside] * depth), 0.0).astype(BF16)
        work = mm(along, rx_ref[...]) + mm(aside, rx_edge_ref[...])
        at = iota((rows, 1), 0) % part + c * part
        work = work * (ramp_at(turned_row(at, grid), length) * ramp_x)
        for q in range(length // LANES):
            parts = [work[d * part : (d + 1) * part, q * LANES : (q + 1) * LANES] for d in range(depth)]
            for g, piece in enumerate(swap_groups(parts)):
                into = slice((q * GROUPS + g) * grid, (q * GROUPS + g + 1) * grid)
                for r in range(2 * PER):
                    value = piece[r * grid : (r + 1) * grid].astype(BF16)
                    piece_ref[r // 2, into, (r % 2) * LANES : (r % 2 + 1) * LANES] = value
        for j in range(PER):
            i = c * PER + j
            send_ref[i] = mm(pack_ref[...], piece_ref[j]).astype(BF16)
            recv_ref[i, rows_of(mine), :] = send_ref[i, rows_of(mine), :]

    def send(i):
        def start(d, inner):
            plane_copy(i, (mine + d) % plane).start()
            return inner

        lax.fori_loop(1, plane, start, 0)

    for c in range(LEAD):
        pack(c)
        for i in range(c * PER, min((c + 1) * PER, AHEAD)):
            send(i)

    def bins_copy(i):
        return pltpu.make_async_remote_copy(
            src_ref=bins_ref.at[i],
            dst_ref=next_ref.at[i],
            send_sem=bin_send.at[i],
            recv_sem=bin_recv.at[i],
            device_id=((ty, tx - 1), (ty - 1, tx))[i],
            device_id_type=MESH,
        )

    to_there = (tx > 0, ty > 0)
    from_there = (tx < count_x - 1, ty < count_y - 1)

    def bins():
        pool = (iota((length, length // 4), 0) // 4 == iota((length, length // 4), 1)).astype(F32)
        value = highest(sums_ref[...], pool) * (1.0 / math.sqrt(16.0 * depth))
        for i in range(4):
            bins_ref[i] = value[i * EDGE : (i + 1) * EDGE]
        for i in range(2):

            @pl.when(to_there[i])
            def _():
                bins_copy(i).start()

            @pl.when(jnp.logical_not(from_there[i]))
            def _():
                next_ref[i] = jnp.zeros(next_ref.shape[1:], F32)

    end = mid * near + (1 - mid) * z

    def fill(p, filled):
        targets = targets_of((p // ny) * count_x + end * ny + p % ny)
        into = jnp.where(column_of(targets, count_x) == mine, sum_row_of(targets), -1)
        return filled + (iota((sums, PIECES), 0) == into).astype(F32)

    filled = lax.fori_loop(0, plane, fill, jnp.zeros((sums, PIECES), F32))
    filled = jnp.broadcast_to(jnp.sum(filled, axis=1, keepdims=True), (sums, sums))
    filled = (filled > 0.0) & (iota((sums, sums), 0) // SLOTS != end)
    before = mm(mark(iota((sums, sums), 1) < iota((sums, sums), 0)), mark(filled))
    expand = mark(filled & (before == iota((sums, sums), 1).astype(F32)))
    eye = mark(iota((sums, sums), 0) == iota((sums, sums), 1))
    expand_ref[...] = expand
    list_ref[...] = mm_t(eye, expand).astype(BF16)

    targets_ref[...] = jnp.full(targets_ref.shape, -1, jnp.int32)

    def fetch(p, carry):
        targets_ref[pl.ds(p, 1), :] = targets_of((p // ny) * count_x + z * ny + p % ny)
        return carry

    lax.fori_loop(0, plane, fetch, 0)
    rank_ref[...] = mm(mark(column_of(targets_ref[...], count_x) == mine), earlier)

    def turn(p, carry):
        targets = targets_ref[pl.ds(p, 1), :]
        into = jnp.where(column_of(targets, count_x) == mine, sum_row_of(targets), -1)
        into = mark(iota((sums, PIECES), 0) == into)
        chosen = mark(iota((cap, PIECES), 0).astype(F32) == rank_ref[pl.ds(p, 1), :])
        turn_ref[rows_of(p), :] = mm_t(chosen, into).astype(BF16)
        return carry

    lax.fori_loop(0, plane, turn, 0)
    reduce_ref[...] = mm_t(eye, turn_ref[...]).astype(BF16)

    def unit_rows(unit):
        return pl.ds(pl.multiple_of(unit * SLOTS, SLOTS), SLOTS)

    def line_copy(i, unit, slot, peer):
        return pltpu.make_async_remote_copy(
            src_ref=zsend_ref.at[i, unit_rows(unit), :],
            dst_ref=zrecv_ref.at[slot, i],
            send_sem=line_send.at[0],
            recv_sem=line_recv.at[i, slot],
            device_id=in_line(peer),
            device_id_type=MESH,
        )

    def list_copy(i):
        return pltpu.make_async_remote_copy(
            src_ref=lists_ref.at[i],
            dst_ref=got_lists_ref.at[i],
            send_sem=line_send.at[1],
            recv_sem=line_recv.at[i, 3],
            device_id=in_line(near),
            device_id_type=MESH,
        )

    def plane_done(i):
        others = pl.ds(0, (plane - 1) * cap)
        return pltpu.make_async_remote_copy(
            src_ref=send_ref.at[i, others, :],
            dst_ref=recv_ref.at[i, others, :],
            send_sem=plane_send.at[0],
            recv_sem=plane_recv.at[i],
            device_id=in_line(near),
            device_id_type=MESH,
        )

    def reduce(i):
        plane_done(i).wait_recv()
        value = mm(reduce_ref[...], recv_ref[i])
        dense_ref[i] = value
        zsend_ref[i] = value.astype(BF16)

        @pl.when(mid == 1)
        def _():
            line_copy(i, near, 0, near).start()

        @pl.when(mid == 0)
        def _():
            lists_ref[i] = mm(list_ref[:listed, :], zsend_ref[i]).astype(BF16)
            list_copy(i).start()

    def merge(i):
        @pl.when(mid == 1)
        def _():
            list_copy(i).wait_recv()
            dense_ref[i] = dense_ref[i] + mm(expand_ref[:, :listed], got_lists_ref[i])
            for unit, slot in ((diag, 1), (cross, 2)):
                zsend_ref[i, unit_rows(unit), :] = dense_ref[i, unit_rows(unit), :].astype(BF16)
                line_copy(i, unit, slot, unit).start()

    slot = iota((SLOTS, PIECES), 0) + me * SLOTS

    def count(device, counts):
        return counts + (targets_of(device) == slot).astype(F32)

    place = iota((PIECES, 1), 0)
    lane = iota((1, WIDE), 1)

    def tally():
        counts = lax.fori_loop(0, devices, count, jnp.zeros((SLOTS, PIECES), F32))
        counts_ref[...] = counts.astype(BF16)
        ramp_ref[...] = ramp_at(place % grid * SIDE + lane % SIDE, length)

    def weigh(i):
        patch = (ramp_at(place // grid * SIDE + lane // LANES + 2 * i, length) * ramp_ref[...]).astype(BF16)
        inv_ref[i] = 1.0 / jnp.maximum(mm(counts_ref[...], patch), 1.0)

    def surface(i, ref):
        @pl.when(from_there[i])
        def _():
            bins_copy(i).wait_recv()

        @pl.when(to_there[i])
        def _():
            bins_copy(i).wait_send()

        tables = (ca_ref[...], sa_ref[...], cb_ref[...], sb_ref[...])
        ref[...] = phase(*tables, bins_ref[2 + i], next_ref[i])[: ref.shape[0]]

    inner = iota((WIDE, LANES), 0)
    outer = iota((WIDE, LANES), 1)
    pooled = inner % LANES // (2 * SIDE) * (SIDE // 2) + inner % SIDE // 2

    def final(c):
        for j in range(PER):
            i = c * PER + j

            @pl.when(mid == 1)
            def _():
                line_copy(i, cross, 2, cross).wait_recv()
                total_ref[j] = dense_ref[i, unit_rows(z), :] + zrecv_ref[2, i].astype(F32)

            @pl.when(mid == 0)
            def _():
                line_copy(i, near, 0, near).wait_recv()
                line_copy(i, near, 1, near).wait_recv()
                value = dense_ref[i, unit_rows(z), :] + zrecv_ref[0, i].astype(F32)
                total_ref[j] = value + zrecv_ref[1, i].astype(F32)

        level = jnp.zeros((SLOTS, LANES), F32)
        rows = []
        for j in range(PER):
            i = c * PER + j
            value = (total_ref[j] * inv_ref[i]).astype(BF16)
            level += mm(value, mark(outer == pooled + j * SIDE))
            value = value.astype(F32)
            rows += [value[:, :LANES], value[:, LANES:]]
        for s, part in enumerate(swap_groups(rows)):
            joined_ref[:, pl.ds(pl.multiple_of(s * SIDE * SIDE + c * LANES, LANES), LANES)] = part.astype(BF16)
        a, b = iota((LANES, LANES), 0), iota((LANES, LANES), 1)
        into = c * (SIDE // 4) + a % (SIDE // 2) // 2
        sum_ref[...] += mm((level * 0.125).astype(BF16), mark((a < PER * SIDE) & (b == into)))

    def regroup():
        u = iota((SLOTS, LANES), 0)
        wanted = tx * SLOTS + 4 * (u % (SLOTS // 4)) + u // (SLOTS // 4)
        for q in range(count_x // 2):
            pair = [ids_ref[ty * count_x + 2 * q + j][1:2, :LANES] for j in range(2)]
            named = jnp.where(iota((1, LANES), 1) < SLOTS, pair[0], pltpu.roll(pair[1], SLOTS, 1))
            regroup_ref[:, q * LANES : (q + 1) * LANES] = mark(named == wanted)

    sum_ref[...] = jnp.zeros_like(sum_ref)

    def step(i, carry):
        @pl.when(i < PAIRS)
        def _():
            reduce(i)

        @pl.when(i + AHEAD < PAIRS)
        def _():
            send(i + AHEAD)

        @pl.when((i % PER == 0) & (i // PER + LEAD < CHUNKS))
        def _():
            pack(i // PER + LEAD)

        @pl.when((i >= 3) & (i < PAIRS + 3))
        def _():
            weigh(i - 3)

        pl.when(i == 1)(bins)
        pl.when(i == 2)(tally)
        pl.when(i == 5)(lambda: surface(0, corr_right_ref))
        pl.when(i == 7)(lambda: surface(1, corr_below_ref))
        pl.when(i == 9)(regroup)

        @pl.when((i >= LAG) & (i < PAIRS + LAG))
        def _():
            merge(i - LAG)

        last = i - LAG - LAG

        @pl.when((last >= 0) & (last % PER == PER - 1))
        def _():
            final(last // PER)

        return carry

    lax.fori_loop(0, PAIRS + LAG + LAG, step, 0)
    quads_ref[...] = (sum_ref[...] * 0.125).astype(BF16)

    def row_copy(peer):
        return pltpu.make_async_remote_copy(
            src_ref=quads_ref,
            dst_ref=all_quads_ref.at[tx],
            send_sem=row_send.at[0],
            recv_sem=row_recv.at[0],
            device_id=(ty, peer),
            device_id_type=MESH,
        )

    def start_row(d, carry):
        row_copy((tx + d) % count_x).start()
        return carry

    lax.fori_loop(1, count_x, start_row, 0)
    all_quads_ref[tx] = quads_ref[...]

    pltpu.make_async_remote_copy(
        src_ref=send_ref.at[:, pl.ds(0, (plane - 1) * cap), :],
        dst_ref=send_ref.at[:, pl.ds(0, (plane - 1) * cap), :],
        send_sem=plane_send.at[0],
        recv_sem=plane_recv.at[0],
        device_id=in_line(near),
        device_id_type=MESH,
    ).wait_send()

    def sent(ref, which):
        return pltpu.make_async_remote_copy(
            src_ref=ref,
            dst_ref=ref,
            send_sem=line_send.at[which],
            recv_sem=line_recv.at[0, 0],
            device_id=in_line(near),
            device_id_type=MESH,
        )

    @pl.when(mid == 1)
    def _():
        sent(zsend_ref.at[:, pl.ds(0, 3 * SLOTS), :], 0).wait_send()

    @pl.when(mid == 0)
    def _():
        sent(lists_ref, 1).wait_send()

    others = all_quads_ref.at[pl.ds(0, count_x - 1)]
    row = pltpu.make_async_remote_copy(
        src_ref=others,
        dst_ref=others,
        send_sem=row_send.at[0],
        recv_sem=row_recv.at[0],
        device_id=in_line(near),
        device_id_type=MESH,
    )
    row.wait_send()
    row.wait_recv()
    placed = mm(regroup_ref[...], all_quads_ref[...].reshape(count_x * SLOTS, LANES)).astype(BF16)
    side = SIDE // 4
    a, b = iota((LANES, WIDE), 0), iota((LANES, WIDE), 1)
    out = jnp.zeros((SLOTS // 4, WIDE), F32)
    for q in range(4):
        into = (q // 2) * 2 * side * side + a // side * 2 * side + (q % 2) * side + a % side
        out += mm(placed[q * (SLOTS // 4) : (q + 1) * (SLOTS // 4)], mark((a < side * side) & (b == into)))
    coarse_ref[...] = out.astype(BF16)


def dft_tables(length, padded):
    index = np.arange(length)
    angle = (index[:, None] * index[None, :] % length) * (2.0 * math.pi / length)
    pad = ((0, padded - length),) * 2
    return tuple(
        jnp.asarray(np.pad(table / math.sqrt(length), pad).astype(np.float32)) for table in (np.cos(angle), np.sin(angle))
    )


def exchange(shifts, tile, *rest, cap, listed, count_y, count_x, collective_id):
    length = tile.shape[2]
    edges = rest[0].shape[0] * 2 * EDGE
    plane = count_y * (count_x // NZ)
    sums = NZ * SLOTS
    vmem = pl.BlockSpec(memory_space=pltpu.VMEM)
    tables = dft_tables(OV // 4, EDGE) + dft_tables(length // 4, length // 4)
    corr = jax.ShapeDtypeStruct((OV // 4, length // 4), F32)
    return pl.pallas_call(
        functools.partial(exchange_kernel, count_y, count_x, length, cap, listed),
        out_shape=[
            jax.ShapeDtypeStruct((SLOTS, SIDE * LANES), BF16),
            jax.ShapeDtypeStruct((SLOTS // 4, WIDE), BF16),
            corr,
            corr,
        ],
        in_specs=[pl.BlockSpec(memory_space=pltpu.SMEM)] + [vmem] * 11,
        out_specs=[vmem] * 4,
        scratch_shapes=[
            pltpu.VMEM((length, length), BF16),
            pltpu.VMEM((edges, length), BF16),
            pltpu.VMEM((plane * cap, PIECES), BF16),
            pltpu.VMEM((PER, PIECES, WIDE), BF16),
            pltpu.VMEM((PAIRS, plane * cap, WIDE), BF16),
            pltpu.VMEM((PAIRS, plane * cap, WIDE), BF16),
            pltpu.VMEM((max(16, plane), PIECES), jnp.int32),
            pltpu.VMEM((max(16, plane), PIECES), F32),
            pltpu.VMEM((plane * cap, sums), BF16),
            pltpu.VMEM((sums, plane * cap), BF16),
            pltpu.VMEM((PAIRS, SLOTS, WIDE), F32),
            pltpu.VMEM((PAIRS, sums, WIDE), F32),
            pltpu.VMEM((PAIRS, sums, WIDE), BF16),
            pltpu.VMEM((3, PAIRS, SLOTS, WIDE), BF16),
            pltpu.VMEM((SLOTS, PIECES), BF16),
            pltpu.VMEM((PIECES, WIDE), F32),
            pltpu.VMEM((sums, sums), BF16),
            pltpu.VMEM((sums, sums), BF16),
            pltpu.VMEM((PAIRS, listed, WIDE), BF16),
            pltpu.VMEM((PAIRS, listed, WIDE), BF16),
            pltpu.VMEM((PER, SLOTS, WIDE), F32),
            pltpu.VMEM((SLOTS, LANES), F32),
            pltpu.VMEM((SLOTS, count_x * SLOTS), BF16),
            pltpu.VMEM((SLOTS, LANES), BF16),
            pltpu.VMEM((count_x, SLOTS, LANES), BF16),
            pltpu.VMEM((4, EDGE, length // 4), F32),
            pltpu.VMEM((2, EDGE, length // 4), F32),
            pltpu.SemaphoreType.DMA((2,)),
            pltpu.SemaphoreType.DMA((2,)),
            pltpu.SemaphoreType.DMA((1,)),
            pltpu.SemaphoreType.DMA((PAIRS,)),
            pltpu.SemaphoreType.DMA((2,)),
            pltpu.SemaphoreType.DMA((PAIRS, 4)),
            pltpu.SemaphoreType.DMA((1,)),
            pltpu.SemaphoreType.DMA((1,)),
        ],
        name="exchange",
        compiler_params=pltpu.CompilerParams(
            collective_id=collective_id, has_side_effects=True, vmem_limit_bytes=44 * 2**20
        ),
        cost_estimate=pl.CostEstimate(flops=3 * 10**9, bytes_accessed=2**23, transcendentals=0),
    )(shifts, tile, *rest, *tables)


def finish_kernel(*refs):
    count = len(refs) // 2
    sems = refs[-1]
    copies = [pltpu.make_async_copy(refs[i], refs[count + i], sems.at[i]) for i in range(count)]
    for copy in copies:
        copy.start()
    for copy in copies:
        copy.wait()


def finish(*results):
    hbm = pl.BlockSpec(memory_space=pltpu.HBM)
    return pl.pallas_call(
        finish_kernel,
        out_shape=[jax.ShapeDtypeStruct(r.shape, r.dtype) for r in results],
        in_specs=[pl.BlockSpec(memory_space=pltpu.VMEM)] * len(results),
        out_specs=[hbm] * len(results),
        scratch_shapes=[pltpu.SemaphoreType.DMA((len(results),))],
        name="finish",
    )(*results)


def per_device(tiles, shifts, piece_target, coarse_target):
    tile = tiles[0, 0]
    count_y = lax.axis_size("ty")
    count_x = lax.axis_size("tx")
    cap = NZ * 2 * PIECES // (count_y * count_x)
    listed = (NZ - 1) * SLOTS
    fewer, shorter = cap * 3 // 4, listed * 5 // 6
    *operands, fits = front(tile, piece_target[0], coarse_target[0], count_y, count_x, fewer, shorter)
    run = functools.partial(exchange, shifts[0, 0], *operands, count_y=count_y, count_x=count_x)
    if fewer % 16:
        return tuple(finish(*run(cap=cap, listed=listed, collective_id=1)))
    results = lax.cond(
        fits[0, 0] == 1,
        lambda: tuple(run(cap=fewer, listed=shorter, collective_id=1)),
        lambda: tuple(run(cap=cap, listed=listed, collective_id=2)),
    )
    return tuple(finish(*results))


def solution(mesh):
    placed = (
        P("ty", "tx", None, None, None),
        P("ty", "tx", None),
        P("ty", "tx", None),
        P("ty", "tx", None),
    )
    return jax.shard_map(
        per_device,
        mesh=mesh,
        in_specs=placed,
        out_specs=(P(("ty", "tx"), None), P(("ty", "tx"), None), P("ty", "tx"), P("ty", "tx")),
        check_vma=False,
    )
```

```python
import functools
import math

import jax
import jax.numpy as jnp
import numpy as np
from jax import lax
from jax.experimental import pallas as pl
from jax.experimental.pallas import tpu as pltpu
from jax.sharding import PartitionSpec as P

SIDE = 32
OV = 48
H = 8
SLOTS = 64
LANES = 128
GROUPS = LANES // SIDE
EDGE = 2 * H
NZ = 4
PIECES = 256
PAIRS = SIDE // 2
WIDE = 2 * LANES
CHUNKS = 8
AHEAD = 3
LEAD = AHEAD // 2 + 1
LAG = 3
PER = PAIRS // CHUNKS
F32 = jnp.float32
BF16 = jnp.bfloat16
MESH = pl.DeviceIdType.MESH
DIRECTIONS = ((1, 0), (-1, 0), (0, 1), (0, -1), (1, 1), (1, -1), (-1, 1), (-1, -1))


def highest(left, right):
    return jnp.dot(left, right, precision=lax.Precision.HIGHEST, preferred_element_type=F32)


def iota(shape, dim):
    return lax.broadcasted_iota(jnp.int32, shape, dim)


def mm(a, b):
    return jnp.dot(a, b, preferred_element_type=F32)


def mm_t(a, b):
    return lax.dot_general(a, b, (((1,), (1,)), ((), ())), preferred_element_type=F32)


def mark(condition):
    return condition.astype(F32).astype(BF16)


def swap_groups(parts):
    group = iota(parts[0].shape, 1) // SIDE

    def pick(choices):
        value = choices[3]
        for g in range(3):
            value = jnp.where(group == g, choices[g], value)
        return value

    turned = []
    for d in range(GROUPS):
        mixed = pick([parts[(g + d) % GROUPS] for g in range(GROUPS)])
        turned.append(pltpu.roll(mixed, d * SIDE, 1) if d else mixed)
    return [pick([turned[(j - g) % GROUPS] for j in range(GROUPS)]) for g in range(GROUPS)]


def taps(offset, out, column):
    whole, frac = offset
    at = out + whole + H
    return (
        jnp.where(column == at, 1.0 - frac, 0.0) + jnp.where(column == at + 1, frac, 0.0)
    ).astype(BF16)


def split_shift(shift):
    whole = lax.shift_right_arithmetic(shift, 2)
    return whole, (shift - 4 * whole).astype(F32) * 0.25


def ramp_at(index, length):
    nearest = jnp.minimum(jnp.minimum(index + 1, length - index), OV).astype(F32)
    return 1.0 + nearest * (3.0 / OV)


def turned_row(at, grid):
    return (at % grid) * SIDE + at // grid


def edge_index(c, length):
    return c % H + jnp.where(c < EDGE, 0, length + H)


def column_of(targets, count_x):
    owner = targets // SLOTS
    return (owner // count_x) * (count_x // NZ) + owner % (count_x // NZ)


def front_kernel(
    count_y, count_x, fewer, shorter, tile_hbm, piece_ids_hbm, coarse_ids_hbm,
    tile_ref, tb_ref, side_ref, ct_ref, cb_ref, sums_ref, all_ids_ref, fits_ref,
    piece_ids_ref, coarse_ids_ref, ids_ref, ids_rows_ref, strips_ref, ends_ref,
    tile_sem, halo_send, halo_recv, id_send, id_recv,
):
    depth, length, _ = tile_ref.shape
    devices = count_y * count_x
    ty, tx = lax.axis_index("ty"), lax.axis_index("tx")
    me = ty * count_x + tx
    barrier = pltpu.get_barrier_semaphore()
    load = pltpu.make_async_copy(tile_hbm, tile_ref, tile_sem.at[0])
    load.start()
    loads = (
        pltpu.make_async_copy(piece_ids_hbm, piece_ids_ref, tile_sem.at[1]),
        pltpu.make_async_copy(coarse_ids_hbm, coarse_ids_ref, tile_sem.at[2]),
    )
    for copy in loads:
        copy.start()

    def at(peer):
        return (peer // count_x, peer % count_x)

    def greet(d, carry):
        pl.semaphore_signal(barrier, inc=1, device_id=at((me + d) % devices), device_id_type=MESH)
        return carry

    lax.fori_loop(1, devices, greet, 0)

    def there(dy, dx):
        y, x = ty + dy, tx + dx
        return (y >= 0) & (y < count_y) & (x >= 0) & (x < count_x)

    low, high = pl.ds(0, EDGE), pl.ds(EDGE, EDGE)

    def landing(dy, dx):
        if dx == 0:
            return tb_ref.at[:, low if dy == 1 else high, :]
        half = low if dx == 1 else high
        if dy == 0:
            return side_ref.at[:, half, :]
        return (ct_ref if dy == 1 else cb_ref).at[:, half, :]

    def halo(i):
        dy, dx = DIRECTIONS[i]
        if dx == 0:
            source = ends_ref.at[:, high if dy == 1 else low, :]
        else:
            half = high if dx == 1 else low
            if dy == 0:
                source = strips_ref.at[:, half, :]
            else:
                source = strips_ref.at[:, half, pl.ds(length - LANES if dy == 1 else 0, LANES)]
        return pltpu.make_async_remote_copy(
            src_ref=source,
            dst_ref=landing(dy, dx),
            send_sem=halo_send.at[i],
            recv_sem=halo_recv.at[i],
            device_id=(ty + dy, tx + dx),
            device_id_type=MESH,
        )

    for dy, dx in DIRECTIONS:

        @pl.when(jnp.logical_not(there(-dy, -dx)))
        def _():
            ref = landing(dy, dx)
            ref[...] = jnp.zeros(ref.shape, ref.dtype)

    for copy in loads:
        copy.wait()
    ids_ref[...] = jnp.full(ids_ref.shape, -1, jnp.int32)
    ids_ref[0:1, :] = piece_ids_ref[...]
    ids_ref[1:2, :SLOTS] = coarse_ids_ref[...]

    pl.semaphore_wait(barrier, devices - 1)

    def ids(peer):
        return pltpu.make_async_remote_copy(
            src_ref=ids_ref,
            dst_ref=all_ids_ref.at[me],
            send_sem=id_send.at[peer],
            recv_sem=id_recv.at[0],
            device_id=at(peer),
            device_id_type=MESH,
        )

    def start(d, carry):
        ids((me + d) % devices).start()
        return carry

    lax.fori_loop(1, devices, start, 0)
    all_ids_ref[me] = ids_ref[...]

    row, lane = iota((2 * EDGE, LANES), 0), iota((2 * EDGE, LANES), 1)
    back = lane - (LANES - OV)
    first_bins = (row >= EDGE) & (lane < OV) & (lane // 4 == row - EDGE)
    last_bins = (row >= EDGE) & (back >= 0) & (back // 4 == row - EDGE)

    def picks(z):
        own = (row < EDGE) & (row // H == z % 2)
        first = mark((own & (lane == row % H)) | first_bins)
        return first, mark((own & (lane - (LANES - H) == row % H)) | last_bins)

    load.wait()
    left = right = jnp.zeros((EDGE, length), F32)
    for k in range(depth // 2):
        lows = highs = jnp.zeros((2 * EDGE, length), F32)
        for z in (2 * k, 2 * k + 1):
            first, last = picks(z)
            lows += mm_t(first, tile_ref[z, :, :LANES])
            highs += mm_t(last, tile_ref[z, :, length - LANES :])
        left += lows[EDGE:]
        right += highs[EDGE:]
        strips_ref[k, :EDGE, :] = lows[:EDGE].astype(BF16)
        strips_ref[k, EDGE:, :] = highs[:EDGE].astype(BF16)
        pair = (2 * k, 2 * k + 1)
        ends = [tile_ref[z, :EDGE, :].astype(F32)[:H] for z in pair]
        ends += [tile_ref[z, length - EDGE :, :].astype(F32)[H:] for z in pair]
        ends_ref[k] = jnp.concatenate(ends).astype(BF16)
    first, last = picks(0)

    for i, (dy, dx) in enumerate(DIRECTIONS):

        @pl.when(there(dy, dx))
        def _():
            halo(i).start()

    top = bottom = jnp.zeros((EDGE, length), F32)
    for z in range(depth):
        top += mm(first[EDGE:], tile_ref[z, :LANES, :])
        bottom += mm(last[EDGE:], tile_ref[z, length - LANES :, :])
    sums_ref[...] = jnp.concatenate([left, top, right, bottom])

    others = pl.ds(0, devices - 1)
    pltpu.make_async_remote_copy(
        src_ref=all_ids_ref.at[others],
        dst_ref=all_ids_ref.at[others],
        send_sem=id_send.at[me],
        recv_sem=id_recv.at[0],
        device_id=at(me),
        device_id_type=MESH,
    ).wait_recv()

    def gather(d, carry):
        ids_rows_ref[pl.ds(d, 1), :] = all_ids_ref[d][0:1, :]
        return carry

    lax.fori_loop(0, devices, gather, 0)
    columns = column_of(ids_rows_ref[...], count_x)
    ones = jnp.ones((PIECES, LANES), BF16)
    most = jnp.zeros((devices, LANES), F32)
    for p in range(count_y * (count_x // NZ)):
        most = jnp.maximum(most, mm(mark(columns == p), ones))
    fits = jnp.max(most) <= float(fewer)

    ny = count_x // NZ
    owner = iota((count_y * ny, devices), 1)
    in_column = (owner // count_x) * ny + owner % ny == iota((count_y * ny, devices), 0)
    filled = jnp.zeros((1, 1), F32)
    for end in (0, NZ - 1):
        counts = jnp.zeros((devices, SLOTS), F32)
        for p in range(count_y * ny):
            d = (p // ny) * count_x + end * ny + p % ny
            targets = ids_rows_ref[d : d + 1, :]
            owners = mark(iota((devices, PIECES), 0) == targets // SLOTS)
            counts += mm_t(owners, mark(iota((SLOTS, PIECES), 0) == targets % SLOTS))
        elsewhere = mark(in_column & (owner % count_x // ny != end))
        slots = mm(elsewhere, mark(counts > 0.0))
        filled = jnp.maximum(filled, jnp.max(jnp.sum(slots, axis=1, keepdims=True)))
    fits_ref[0, 0] = jnp.where(fits & (jnp.max(filled) <= float(shorter)), 1, 0)

    for i, (dy, dx) in enumerate(DIRECTIONS):

        @pl.when(there(-dy, -dx))
        def _():
            halo(i).wait_recv()

    for i, (dy, dx) in enumerate(DIRECTIONS):

        @pl.when(there(dy, dx))
        def _():
            halo(i).wait_send()

    def finish(d, carry):
        ids((me + d) % devices).wait_send()
        return carry

    lax.fori_loop(1, devices, finish, 0)


def front(tile, piece_ids, coarse_ids, count_y, count_x, fewer, shorter):
    depth, length, _ = tile.shape
    devices = count_y * count_x
    vmem = pl.BlockSpec(memory_space=pltpu.VMEM)
    smem = pl.BlockSpec(memory_space=pltpu.SMEM)
    strip = jax.ShapeDtypeStruct((depth // 2, 2 * EDGE, length), BF16)
    corner = jax.ShapeDtypeStruct((depth // 2, 2 * EDGE, LANES), BF16)
    return pl.pallas_call(
        functools.partial(front_kernel, count_y, count_x, fewer, shorter),
        out_shape=[
            jax.ShapeDtypeStruct(tile.shape, BF16),
            strip, strip, corner, corner,
            jax.ShapeDtypeStruct((4 * EDGE, length), F32),
            jax.ShapeDtypeStruct((devices, 2, PIECES), jnp.int32),
            jax.ShapeDtypeStruct((1, 1), jnp.int32),
        ],
        in_specs=[pl.BlockSpec(memory_space=pltpu.HBM)] * 3,
        out_specs=[vmem] * 7 + [smem],
        scratch_shapes=[
            pltpu.VMEM((1, PIECES), jnp.int32),
            pltpu.VMEM((1, SLOTS), jnp.int32),
            pltpu.VMEM((2, PIECES), jnp.int32),
            pltpu.VMEM((devices, PIECES), jnp.int32),
            pltpu.VMEM((depth // 2, 2 * EDGE, length), BF16),
            pltpu.VMEM((depth // 2, 2 * EDGE, length), BF16),
            pltpu.SemaphoreType.DMA((3,)),
            pltpu.SemaphoreType.DMA((8,)),
            pltpu.SemaphoreType.DMA((8,)),
            pltpu.SemaphoreType.DMA((devices,)),
            pltpu.SemaphoreType.DMA((1,)),
        ],
        name="front",
        compiler_params=pltpu.CompilerParams(
            collective_id=0, has_side_effects=True, vmem_limit_bytes=57 * 2**20
        ),
        cost_estimate=pl.CostEstimate(flops=10**9, bytes_accessed=2**21, transcendentals=0),
    )(tile, piece_ids, coarse_ids)


def phase(cos_a, sin_a, cos_b, sin_b, own, other):
    def spectrum(values):
        left_cos = highest(cos_a, values)
        left_sin = highest(sin_a, values)
        re = highest(left_cos, cos_b) - highest(left_sin, sin_b)
        im = -(highest(left_cos, sin_b) + highest(left_sin, cos_b))
        return (re, im)

    own_re, own_im = spectrum(own)
    other_re, other_im = spectrum(other)
    cross_re = own_re * other_re + own_im * other_im
    cross_im = own_im * other_re - own_re * other_im
    scale = 1.0 / jnp.sqrt(cross_re * cross_re + cross_im * cross_im + 1.0)
    normed_re = cross_re * scale
    normed_im = cross_im * scale
    out = highest(highest(cos_a, normed_re) - highest(sin_a, normed_im), cos_b)
    return out - highest(highest(sin_a, normed_re) + highest(cos_a, normed_im), sin_b)


def exchange_kernel(
    count_y, count_x, length, cap, listed, shift_ref, tile_ref, tb_ref, side_ref, above_ref, below_ref, sums_ref, ids_ref,
    ca_ref, sa_ref, cb_ref, sb_ref,
    joined_ref, coarse_ref, corr_right_ref, corr_below_ref,
    rx_ref, rx_edge_ref, pack_ref, piece_ref, send_ref, recv_ref, targets_ref, rank_ref, turn_ref, reduce_ref, inv_ref, dense_ref, zsend_ref, zrecv_ref,
    counts_ref, ramp_ref, expand_ref, list_ref, lists_ref, got_lists_ref, total_ref,
    sum_ref, regroup_ref, quads_ref, all_quads_ref,
    bins_ref, next_ref, bin_send, bin_recv, plane_send, plane_recv, line_send, line_recv, row_send, row_recv,
):
    ny = count_x // NZ
    plane = count_y * ny
    devices = count_y * count_x
    sums = NZ * SLOTS
    grid = length // SIDE
    ty, tx = lax.axis_index("ty"), lax.axis_index("tx")
    me = ty * count_x + tx
    y, z = tx % ny, tx // ny
    mine = ty * ny + y
    near = z + 1 - 2 * (z % 2)
    cross, diag = NZ - 1 - z, NZ - 1 - near
    mid = ((z + 1) // 2) % 2
    barrier = pltpu.get_barrier_semaphore()

    def in_plane(p):
        return (p // ny, z * ny + p % ny)

    def in_line(other):
        return (ty, other * ny + y)

    def greet_plane(d, carry):
        pl.semaphore_signal(barrier, inc=1, device_id=in_plane((mine + d) % plane), device_id_type=MESH)
        return carry

    def greet_row(d, carry):
        pl.semaphore_signal(barrier, inc=1, device_id=(ty, (z * ny + d) % count_x), device_id_type=MESH)
        return carry

    lax.fori_loop(1, plane, greet_plane, 0)
    lax.fori_loop(ny, count_x, greet_row, 0)

    def targets_of(device):
        return ids_ref[device][0:1, :]

    def sum_row_of(targets):
        return ((targets // SLOTS) % count_x) // ny * SLOTS + targets % SLOTS

    square = (PIECES, PIECES)
    earlier = mark(iota(square, 0) < iota(square, 1))
    column = column_of(targets_of(me), count_x)
    onehot = (iota((targets_ref.shape[0], PIECES), 0) == column).astype(F32)
    rank = jnp.sum(onehot * mm(onehot.astype(BF16), earlier), axis=0, keepdims=True)
    position = (column * cap).astype(F32) + rank
    chosen = mark(iota((plane * cap, PIECES), 0).astype(F32) == position)
    stacked = iota(square, 1)
    stacked = mark(iota(square, 0) == (stacked % grid) * grid + stacked // grid)
    pack_ref[...] = mm(chosen, stacked).astype(BF16)

    sx = split_shift(shift_ref[1])
    depth = tile_ref.shape[0]
    part = length // CHUNKS
    rows = depth * part
    edges = depth // 2 * 2 * EDGE
    full, wide = (length, length), (edges, length)
    rx_ref[...] = taps(sx, iota(full, 1), iota(full, 0) + H)
    rx_edge_ref[...] = taps(sx, iota(wide, 1), edge_index(iota(wide, 0) % (2 * EDGE), length))
    sy = split_shift(shift_ref[0])
    side = side_ref[...].reshape(edges, length)
    tb = tb_ref[...].reshape(edges, length)
    above = above_ref[...].reshape(edges, LANES)
    below = below_ref[...].reshape(edges, LANES)

    def slice_of(c):
        return c // (2 * EDGE) * 2 + c // H % 2

    ramp_x = ramp_at(iota((1, length), 1), length)

    pl.semaphore_wait(barrier, plane - 1 + count_x - ny)

    def rows_of(p):
        return pl.ds(pl.multiple_of(p * cap, cap), cap)

    def plane_copy(i, peer):
        return pltpu.make_async_remote_copy(
            src_ref=send_ref.at[i, rows_of(peer), :],
            dst_ref=recv_ref.at[i, rows_of(mine), :],
            send_sem=plane_send.at[0],
            recv_sem=plane_recv.at[i],
            device_id=in_plane(peer),
            device_id_type=MESH,
        )

    def pack(c):
        def of(shape, column):
            return taps(sy, turned_row(iota(shape, 0) % part + c * part, grid), column)

        lane = iota((rows, edges), 1)
        mine_only = slice_of(lane) == iota((rows, edges), 0) // part
        ends = of((rows, edges), jnp.where(mine_only, edge_index(lane % (2 * EDGE), length), -1))
        ry = of((part, length), iota((part, length), 1) + H)
        along = jnp.concatenate([mm(ry, tile_ref[d]) for d in range(depth)])
        along = (along + mm(ends, tb)).astype(BF16)
        aside = (
            mm_t(ry, side)
            + mm_t(of((part, LANES), iota((part, LANES), 1) + (H - LANES)), above)
            + mm_t(of((part, LANES), iota((part, LANES), 1) + (length + H)), below)
        )
        aside = jnp.where(mine_only, jnp.concatenate([aside] * depth), 0.0).astype(BF16)
        work = mm(along, rx_ref[...]) + mm(aside, rx_edge_ref[...])
        at = iota((rows, 1), 0) % part + c * part
        work = work * (ramp_at(turned_row(at, grid), length) * ramp_x)
        for q in range(length // LANES):
            parts = [work[d * part : (d + 1) * part, q * LANES : (q + 1) * LANES] for d in range(depth)]
            for g, piece in enumerate(swap_groups(parts)):
                into = slice((q * GROUPS + g) * grid, (q * GROUPS + g + 1) * grid)
                for r in range(2 * PER):
                    value = piece[r * grid : (r + 1) * grid].astype(BF16)
                    piece_ref[r // 2, into, (r % 2) * LANES : (r % 2 + 1) * LANES] = value
        for j in range(PER):
            i = c * PER + j
            send_ref[i] = mm(pack_ref[...], piece_ref[j]).astype(BF16)
            recv_ref[i, rows_of(mine), :] = send_ref[i, rows_of(mine), :]

    def send(i):
        def start(d, inner):
            plane_copy(i, (mine + d) % plane).start()
            return inner

        lax.fori_loop(1, plane, start, 0)

    for c in range(LEAD):
        pack(c)
        for i in range(c * PER, min((c + 1) * PER, AHEAD)):
            send(i)

    def bins_copy(i):
        return pltpu.make_async_remote_copy(
            src_ref=bins_ref.at[i],
            dst_ref=next_ref.at[i],
            send_sem=bin_send.at[i],
            recv_sem=bin_recv.at[i],
            device_id=((ty, tx - 1), (ty - 1, tx))[i],
            device_id_type=MESH,
        )

    to_there = (tx > 0, ty > 0)
    from_there = (tx < count_x - 1, ty < count_y - 1)

    def bins():
        pool = (iota((length, length // 4), 0) // 4 == iota((length, length // 4), 1)).astype(F32)
        value = highest(sums_ref[...], pool) * (1.0 / math.sqrt(16.0 * depth))
        for i in range(4):
            bins_ref[i] = value[i * EDGE : (i + 1) * EDGE]
        for i in range(2):

            @pl.when(to_there[i])
            def _():
                bins_copy(i).start()

            @pl.when(jnp.logical_not(from_there[i]))
            def _():
                next_ref[i] = jnp.zeros(next_ref.shape[1:], F32)

    end = mid * near + (1 - mid) * z

    def fill(p, filled):
        targets = targets_of((p // ny) * count_x + end * ny + p % ny)
        into = jnp.where(column_of(targets, count_x) == mine, sum_row_of(targets), -1)
        return filled + (iota((sums, PIECES), 0) == into).astype(F32)

    filled = lax.fori_loop(0, plane, fill, jnp.zeros((sums, PIECES), F32))
    filled = jnp.broadcast_to(jnp.sum(filled, axis=1, keepdims=True), (sums, sums))
    filled = (filled > 0.0) & (iota((sums, sums), 0) // SLOTS != end)
    before = mm(mark(iota((sums, sums), 1) < iota((sums, sums), 0)), mark(filled))
    expand = mark(filled & (before == iota((sums, sums), 1).astype(F32)))
    eye = mark(iota((sums, sums), 0) == iota((sums, sums), 1))
    expand_ref[...] = expand
    list_ref[...] = mm_t(eye, expand).astype(BF16)

    targets_ref[...] = jnp.full(targets_ref.shape, -1, jnp.int32)

    def fetch(p, carry):
        targets_ref[pl.ds(p, 1), :] = targets_of((p // ny) * count_x + z * ny + p % ny)
        return carry

    lax.fori_loop(0, plane, fetch, 0)
    rank_ref[...] = mm(mark(column_of(targets_ref[...], count_x) == mine), earlier)

    def turn(p, carry):
        targets = targets_ref[pl.ds(p, 1), :]
        into = jnp.where(column_of(targets, count_x) == mine, sum_row_of(targets), -1)
        into = mark(iota((sums, PIECES), 0) == into)
        chosen = mark(iota((cap, PIECES), 0).astype(F32) == rank_ref[pl.ds(p, 1), :])
        turn_ref[rows_of(p), :] = mm_t(chosen, into).astype(BF16)
        return carry

    lax.fori_loop(0, plane, turn, 0)
    reduce_ref[...] = mm_t(eye, turn_ref[...]).astype(BF16)

    def unit_rows(unit):
        return pl.ds(pl.multiple_of(unit * SLOTS, SLOTS), SLOTS)

    def line_copy(i, unit, slot, peer):
        return pltpu.make_async_remote_copy(
            src_ref=zsend_ref.at[i, unit_rows(unit), :],
            dst_ref=zrecv_ref.at[slot, i],
            send_sem=line_send.at[0],
            recv_sem=line_recv.at[i, slot],
            device_id=in_line(peer),
            device_id_type=MESH,
        )

    def list_copy(i):
        return pltpu.make_async_remote_copy(
            src_ref=lists_ref.at[i],
            dst_ref=got_lists_ref.at[i],
            send_sem=line_send.at[1],
            recv_sem=line_recv.at[i, 3],
            device_id=in_line(near),
            device_id_type=MESH,
        )

    def plane_done(i):
        others = pl.ds(0, (plane - 1) * cap)
        return pltpu.make_async_remote_copy(
            src_ref=send_ref.at[i, others, :],
            dst_ref=recv_ref.at[i, others, :],
            send_sem=plane_send.at[0],
            recv_sem=plane_recv.at[i],
            device_id=in_line(near),
            device_id_type=MESH,
        )

    def reduce(i):
        plane_done(i).wait_recv()
        value = mm(reduce_ref[...], recv_ref[i])
        dense_ref[i] = value
        zsend_ref[i] = value.astype(BF16)

        @pl.when(mid == 1)
        def _():
            line_copy(i, near, 0, near).start()

        @pl.when(mid == 0)
        def _():
            lists_ref[i] = mm(list_ref[:listed, :], zsend_ref[i]).astype(BF16)
            list_copy(i).start()

    def merge(i):
        @pl.when(mid == 1)
        def _():
            list_copy(i).wait_recv()
            dense_ref[i] = dense_ref[i] + mm(expand_ref[:, :listed], got_lists_ref[i])
            for unit, slot in ((diag, 1), (cross, 2)):
                zsend_ref[i, unit_rows(unit), :] = dense_ref[i, unit_rows(unit), :].astype(BF16)
                line_copy(i, unit, slot, unit).start()

    slot = iota((SLOTS, PIECES), 0) + me * SLOTS

    def count(device, counts):
        return counts + (targets_of(device) == slot).astype(F32)

    place = iota((PIECES, 1), 0)
    lane = iota((1, WIDE), 1)

    def tally():
        counts = lax.fori_loop(0, devices, count, jnp.zeros((SLOTS, PIECES), F32))
        counts_ref[...] = counts.astype(BF16)
        ramp_ref[...] = ramp_at(place % grid * SIDE + lane % SIDE, length)

    def weigh(i):
        patch = (ramp_at(place // grid * SIDE + lane // LANES + 2 * i, length) * ramp_ref[...]).astype(BF16)
        inv_ref[i] = 1.0 / jnp.maximum(mm(counts_ref[...], patch), 1.0)

    def surface(i, ref):
        @pl.when(from_there[i])
        def _():
            bins_copy(i).wait_recv()

        @pl.when(to_there[i])
        def _():
            bins_copy(i).wait_send()

        tables = (ca_ref[...], sa_ref[...], cb_ref[...], sb_ref[...])
        ref[...] = phase(*tables, bins_ref[2 + i], next_ref[i])[: ref.shape[0]]

    inner = iota((WIDE, LANES), 0)
    outer = iota((WIDE, LANES), 1)
    pooled = inner % LANES // (2 * SIDE) * (SIDE // 2) + inner % SIDE // 2

    def final(c):
        for j in range(PER):
            i = c * PER + j

            @pl.when(mid == 1)
            def _():
                line_copy(i, cross, 2, cross).wait_recv()
                total_ref[j] = dense_ref[i, unit_rows(z), :] + zrecv_ref[2, i].astype(F32)

            @pl.when(mid == 0)
            def _():
                line_copy(i, near, 0, near).wait_recv()
                line_copy(i, near, 1, near).wait_recv()
                value = dense_ref[i, unit_rows(z), :] + zrecv_ref[0, i].astype(F32)
                total_ref[j] = value + zrecv_ref[1, i].astype(F32)

        level = jnp.zeros((SLOTS, LANES), F32)
        rows = []
        for j in range(PER):
            i = c * PER + j
            value = (total_ref[j] * inv_ref[i]).astype(BF16)
            level += mm(value, mark(outer == pooled + j * SIDE))
            value = value.astype(F32)
            rows += [value[:, :LANES], value[:, LANES:]]
        for s, part in enumerate(swap_groups(rows)):
            joined_ref[:, pl.ds(pl.multiple_of(s * SIDE * SIDE + c * LANES, LANES), LANES)] = part.astype(BF16)
        a, b = iota((LANES, LANES), 0), iota((LANES, LANES), 1)
        into = c * (SIDE // 4) + a % (SIDE // 2) // 2
        sum_ref[...] += mm((level * 0.125).astype(BF16), mark((a < PER * SIDE) & (b == into)))

    def regroup():
        u = iota((SLOTS, LANES), 0)
        wanted = tx * SLOTS + 4 * (u % (SLOTS // 4)) + u // (SLOTS // 4)
        for q in range(count_x // 2):
            pair = [ids_ref[ty * count_x + 2 * q + j][1:2, :LANES] for j in range(2)]
            named = jnp.where(iota((1, LANES), 1) < SLOTS, pair[0], pltpu.roll(pair[1], SLOTS, 1))
            regroup_ref[:, q * LANES : (q + 1) * LANES] = mark(named == wanted)

    sum_ref[...] = jnp.zeros_like(sum_ref)

    def step(i, carry):
        @pl.when(i < PAIRS)
        def _():
            reduce(i)

        @pl.when(i + AHEAD < PAIRS)
        def _():
            send(i + AHEAD)

        @pl.when((i % PER == 0) & (i // PER + LEAD < CHUNKS))
        def _():
            pack(i // PER + LEAD)

        @pl.when((i >= 3) & (i < PAIRS + 3))
        def _():
            weigh(i - 3)

        pl.when(i == 1)(bins)
        pl.when(i == 2)(tally)

        @pl.when((i >= LAG) & (i < PAIRS + LAG))
        def _():
            merge(i - LAG)

        pl.when(i == PAIRS)(lambda: surface(0, corr_right_ref))
        pl.when(i == PAIRS + 1)(regroup)
        pl.when(i == PAIRS + LAG - 1)(lambda: surface(1, corr_below_ref))

        last = i - LAG - LAG

        @pl.when((last >= 0) & (last % PER == PER - 1))
        def _():
            final(last // PER)

        return carry

    lax.fori_loop(0, PAIRS + LAG + LAG, step, 0)
    quads_ref[...] = (sum_ref[...] * 0.125).astype(BF16)

    def row_copy(peer):
        return pltpu.make_async_remote_copy(
            src_ref=quads_ref,
            dst_ref=all_quads_ref.at[tx],
            send_sem=row_send.at[0],
            recv_sem=row_recv.at[0],
            device_id=(ty, peer),
            device_id_type=MESH,
        )

    def start_row(d, carry):
        row_copy((tx + d) % count_x).start()
        return carry

    lax.fori_loop(1, count_x, start_row, 0)
    all_quads_ref[tx] = quads_ref[...]

    pltpu.make_async_remote_copy(
        src_ref=send_ref.at[:, pl.ds(0, (plane - 1) * cap), :],
        dst_ref=send_ref.at[:, pl.ds(0, (plane - 1) * cap), :],
        send_sem=plane_send.at[0],
        recv_sem=plane_recv.at[0],
        device_id=in_line(near),
        device_id_type=MESH,
    ).wait_send()

    def sent(ref, which):
        return pltpu.make_async_remote_copy(
            src_ref=ref,
            dst_ref=ref,
            send_sem=line_send.at[which],
            recv_sem=line_recv.at[0, 0],
            device_id=in_line(near),
            device_id_type=MESH,
        )

    @pl.when(mid == 1)
    def _():
        sent(zsend_ref.at[:, pl.ds(0, 3 * SLOTS), :], 0).wait_send()

    @pl.when(mid == 0)
    def _():
        sent(lists_ref, 1).wait_send()

    others = all_quads_ref.at[pl.ds(0, count_x - 1)]
    row = pltpu.make_async_remote_copy(
        src_ref=others,
        dst_ref=others,
        send_sem=row_send.at[0],
        recv_sem=row_recv.at[0],
        device_id=in_line(near),
        device_id_type=MESH,
    )
    row.wait_send()
    row.wait_recv()
    placed = mm(regroup_ref[...], all_quads_ref[...].reshape(count_x * SLOTS, LANES)).astype(BF16)
    side = SIDE // 4
    a, b = iota((LANES, WIDE), 0), iota((LANES, WIDE), 1)
    out = jnp.zeros((SLOTS // 4, WIDE), F32)
    for q in range(4):
        into = (q // 2) * 2 * side * side + a // side * 2 * side + (q % 2) * side + a % side
        out += mm(placed[q * (SLOTS // 4) : (q + 1) * (SLOTS // 4)], mark((a < side * side) & (b == into)))
    coarse_ref[...] = out.astype(BF16)


def dft_tables(length, padded):
    index = np.arange(length)
    angle = (index[:, None] * index[None, :] % length) * (2.0 * math.pi / length)
    pad = ((0, padded - length),) * 2
    return tuple(
        jnp.asarray(np.pad(table / math.sqrt(length), pad).astype(np.float32)) for table in (np.cos(angle), np.sin(angle))
    )


def exchange(shifts, tile, *rest, cap, listed, count_y, count_x, collective_id):
    length = tile.shape[2]
    edges = rest[0].shape[0] * 2 * EDGE
    plane = count_y * (count_x // NZ)
    sums = NZ * SLOTS
    vmem = pl.BlockSpec(memory_space=pltpu.VMEM)
    tables = dft_tables(OV // 4, EDGE) + dft_tables(length // 4, length // 4)
    corr = jax.ShapeDtypeStruct((OV // 4, length // 4), F32)
    return pl.pallas_call(
        functools.partial(exchange_kernel, count_y, count_x, length, cap, listed),
        out_shape=[
            jax.ShapeDtypeStruct((SLOTS, SIDE * LANES), BF16),
            jax.ShapeDtypeStruct((SLOTS // 4, WIDE), BF16),
            corr,
            corr,
        ],
        in_specs=[pl.BlockSpec(memory_space=pltpu.SMEM)] + [vmem] * 11,
        out_specs=[vmem] * 4,
        scratch_shapes=[
            pltpu.VMEM((length, length), BF16),
            pltpu.VMEM((edges, length), BF16),
            pltpu.VMEM((plane * cap, PIECES), BF16),
            pltpu.VMEM((PER, PIECES, WIDE), BF16),
            pltpu.VMEM((PAIRS, plane * cap, WIDE), BF16),
            pltpu.VMEM((PAIRS, plane * cap, WIDE), BF16),
            pltpu.VMEM((max(16, plane), PIECES), jnp.int32),
            pltpu.VMEM((max(16, plane), PIECES), F32),
            pltpu.VMEM((plane * cap, sums), BF16),
            pltpu.VMEM((sums, plane * cap), BF16),
            pltpu.VMEM((PAIRS, SLOTS, WIDE), F32),
            pltpu.VMEM((PAIRS, sums, WIDE), F32),
            pltpu.VMEM((PAIRS, sums, WIDE), BF16),
            pltpu.VMEM((3, PAIRS, SLOTS, WIDE), BF16),
            pltpu.VMEM((SLOTS, PIECES), BF16),
            pltpu.VMEM((PIECES, WIDE), F32),
            pltpu.VMEM((sums, sums), BF16),
            pltpu.VMEM((sums, sums), BF16),
            pltpu.VMEM((PAIRS, listed, WIDE), BF16),
            pltpu.VMEM((PAIRS, listed, WIDE), BF16),
            pltpu.VMEM((PER, SLOTS, WIDE), F32),
            pltpu.VMEM((SLOTS, LANES), F32),
            pltpu.VMEM((SLOTS, count_x * SLOTS), BF16),
            pltpu.VMEM((SLOTS, LANES), BF16),
            pltpu.VMEM((count_x, SLOTS, LANES), BF16),
            pltpu.VMEM((4, EDGE, length // 4), F32),
            pltpu.VMEM((2, EDGE, length // 4), F32),
            pltpu.SemaphoreType.DMA((2,)),
            pltpu.SemaphoreType.DMA((2,)),
            pltpu.SemaphoreType.DMA((1,)),
            pltpu.SemaphoreType.DMA((PAIRS,)),
            pltpu.SemaphoreType.DMA((2,)),
            pltpu.SemaphoreType.DMA((PAIRS, 4)),
            pltpu.SemaphoreType.DMA((1,)),
            pltpu.SemaphoreType.DMA((1,)),
        ],
        name="exchange",
        compiler_params=pltpu.CompilerParams(
            collective_id=collective_id, has_side_effects=True, vmem_limit_bytes=44 * 2**20
        ),
        cost_estimate=pl.CostEstimate(flops=3 * 10**9, bytes_accessed=2**23, transcendentals=0),
    )(shifts, tile, *rest, *tables)


def finish_kernel(*refs):
    count = len(refs) // 2
    sems = refs[-1]
    copies = [pltpu.make_async_copy(refs[i], refs[count + i], sems.at[i]) for i in range(count)]
    for copy in copies:
        copy.start()
    for copy in copies:
        copy.wait()


def finish(*results):
    hbm = pl.BlockSpec(memory_space=pltpu.HBM)
    return pl.pallas_call(
        finish_kernel,
        out_shape=[jax.ShapeDtypeStruct(r.shape, r.dtype) for r in results],
        in_specs=[pl.BlockSpec(memory_space=pltpu.VMEM)] * len(results),
        out_specs=[hbm] * len(results),
        scratch_shapes=[pltpu.SemaphoreType.DMA((len(results),))],
        name="finish",
    )(*results)


def per_device(tiles, shifts, piece_target, coarse_target):
    tile = tiles[0, 0]
    count_y = lax.axis_size("ty")
    count_x = lax.axis_size("tx")
    cap = NZ * 2 * PIECES // (count_y * count_x)
    listed = (NZ - 1) * SLOTS
    fewer, shorter = cap * 3 // 4, listed * 5 // 6
    *operands, fits = front(tile, piece_target[0], coarse_target[0], count_y, count_x, fewer, shorter)
    run = functools.partial(exchange, shifts[0, 0], *operands, count_y=count_y, count_x=count_x)
    if fewer % 16:
        return tuple(finish(*run(cap=cap, listed=listed, collective_id=1)))
    results = lax.cond(
        fits[0, 0] == 1,
        lambda: tuple(run(cap=fewer, listed=shorter, collective_id=1)),
        lambda: tuple(run(cap=cap, listed=listed, collective_id=2)),
    )
    return tuple(finish(*results))


def solution(mesh):
    placed = (
        P("ty", "tx", None, None, None),
        P("ty", "tx", None),
        P("ty", "tx", None),
        P("ty", "tx", None),
    )
    return jax.shard_map(
        per_device,
        mesh=mesh,
        in_specs=placed,
        out_specs=(P(("ty", "tx"), None), P(("ty", "tx"), None), P("ty", "tx"), P("ty", "tx")),
        check_vma=False,
    )
```
